128 devices in a mesh: gene: 8 (over y, x_lo), bin: 16 (over z, x_hi, core).
Axes of the slice: x: 4 (x_hi: 2, x_lo: 2; x = x_hi * 2 + x_lo), y: 4, z: 4, core: 2. Of those that a mesh axis runs over, the one named last changes fastest.
Arguments:
- counts: bfloat16 [49152, 18432], P('bin', 'gene'), may hold values from 2 to 80
- factors: float32 [49152, 256], P('bin'), may hold values from 0.01 to 1
- loadings: float32 [256, 18432], P(None, 'gene'), may hold values from 0.01 to 1
- position: int32 [49152], P('bin'), may hold values from 0 to 49151, as said below
- edge_codes: int32 [192, 256], P('bin'), may hold values from 1 to 15
Outputs:
- factors_new: float32 [49152, 256], P('bin')
- loadings_new: float32 [256, 18432], P(None, 'gene')
The draws below stay inside these ranges and needn't reach their ends.
Inputs may be any that keep to these rules, and one draw needn't show every extreme that they name: Each grid position is named by exactly one barcode. The barcodes of one index s of bin (rows s * 3072 on) fall in 16 aligned groups of 192; group t holds positions in grid rows t * 12 to (t + 1) * 12 - 1, 192 from every such index.
All inputs are finite; a program needn't handle non-finite values.
Results may differ from the reference program's by a relative error of at most 0.0003.
Values sent between devices are 32-bit elements; how exact they have to be, the bound alone decides.
A program may use at most 128 MiB of HBM per device.

```python
import math
import jax
import jax.numpy as jnp
from jax import lax

K = 256
G = 18432
GCOL = 256
NROWS = 192
BINS_DEV = 3072
BINS = 49152
GROUP = 192
N_BIN = 16


def draw_position(key, part):
    orders = jax.vmap(lambda band: jax.random.permutation(jax.random.fold_in(key, band), BINS_DEV))(jnp.arange(N_BIN))
    blocks = orders.astype(jnp.int32).reshape(N_BIN, N_BIN, GROUP)
    blocks = blocks + (jnp.arange(N_BIN, dtype=jnp.int32) * BINS_DEV)[:, None, None]
    return jnp.transpose(blocks, (1, 0, 2)).reshape(BINS).astype(jnp.int32)


def set_ends(values, stream_key, least, largest):
    index_at = [jax.random.randint(jax.random.fold_in(stream_key, axis), (), 0, length) for axis, length in enumerate(values.shape)]
    longest = values.shape.index(max(values.shape))
    beside = index_at[:longest] + [(index_at[longest] + 1) % values.shape[longest]] + index_at[longest + 1:]
    return values.at[tuple(index_at)].set(least).at[tuple(beside)].set(largest)


def shard_levels(key, extent, pieces, smallest, high):
    level, own = 1.0, jax.random.fold_in(key, 6)
    for axis_at, parts in pieces:
        steps = jnp.exp(jax.random.uniform(jax.random.fold_in(own, axis_at), (parts,), jnp.float32, smallest / len(pieces), high / len(pieces)))
        level = level * jnp.repeat(steps, extent[axis_at] // parts).reshape([-1 if axis == axis_at else 1 for axis in range(len(extent))])
    return level


def setup_inputs(seed: int = 0) -> dict:
    streams_of = jax.random.split(jax.random.key(seed), 6)
    counts = jnp.clip(jnp.exp(math.log(80.0) - 3.6888795 * jax.random.uniform(streams_of[0], (BINS, G), jnp.float32) ** shard_levels(streams_of[0], (BINS, G), ((0, 16), (1, 8)), -0.2, 0.2)), 2.0, 80.0).astype(jnp.bfloat16)
    factors = jnp.clip(jnp.exp(math.log(1.0) - 4.6051702 * jax.random.uniform(streams_of[1], (BINS, K), jnp.float32) ** shard_levels(streams_of[1], (BINS, K), ((0, 16),), -0.2, 0.2)), 0.01, 1.0)
    loadings = jnp.clip(jnp.exp(math.log(1.0) - 4.6051702 * jax.random.uniform(streams_of[2], (K, G), jnp.float32) ** shard_levels(streams_of[2], (K, G), ((1, 8),), -0.2, 0.2)), 0.01, 1.0)
    position = draw_position(jax.random.fold_in(streams_of[5], 71), 0)
    edge_codes = set_ends(jax.random.randint(streams_of[4], (NROWS, GCOL), 1, 16), jax.random.fold_in(streams_of[4], 1), 1, 15).astype(jnp.int32)
    return {"counts": counts, "factors": factors, "loadings": loadings, "position": position, "edge_codes": edge_codes}


def neighbours(values):
    beside = jnp.pad(values[:, 1:], ((0, 0), (0, 1), (0, 0))) + jnp.pad(values[:, :-1], ((0, 0), (1, 0), (0, 0)))
    vertical = jnp.pad(values[1:], ((0, 1), (0, 0), (0, 0))) + jnp.pad(values[:-1], ((1, 0), (0, 0), (0, 0)))
    return beside + 0.5 * vertical


def reference(counts, factors, loadings, position, edge_codes):
    load_bf = loadings.astype(jnp.bfloat16)
    numer = jnp.dot(counts, load_bf.T, preferred_element_type=jnp.float32)
    load_gram = jnp.dot(load_bf, load_bf.T, preferred_element_type=jnp.float32)
    grid_w = jnp.zeros((BINS, K), jnp.float32).at[position].set(factors).reshape(NROWS, GCOL, K)
    cell_scale = edge_codes.astype(jnp.float32) / 8.0
    weighted = cell_scale[:, :, None] * grid_w
    smooth_grid = cell_scale[:, :, None] * neighbours(weighted)
    degree_grid = cell_scale * neighbours(cell_scale[:, :, None])[:, :, 0]
    smooth = smooth_grid.reshape(BINS, K)[position]
    degree = degree_grid.reshape(BINS)[position]
    penalty = float(G * K) / 64.0
    denom = jnp.dot(factors, load_gram, precision=lax.Precision.HIGHEST) + penalty * degree[:, None] * factors
    factors_new = factors * (numer + penalty * smooth) / denom
    fac_bf = factors_new.astype(jnp.bfloat16)
    cross = jnp.dot(fac_bf.T, counts, preferred_element_type=jnp.float32)
    fac_gram = jnp.dot(fac_bf.T, fac_bf, preferred_element_type=jnp.float32)
    loadings_new = loadings * cross / jnp.dot(fac_gram, loadings, precision=lax.Precision.HIGHEST)
    return factors_new, loadings_new
```

```python
import jax
import jax.numpy as jnp
from jax import lax
from jax.sharding import PartitionSpec as P

K = 256
G = 18432


def passed_along(block, axis, distance):
    devices = range(lax.axis_size(axis))
    route = [(i - distance, i) for i in devices if i - distance in devices]
    return lax.ppermute(block, axis, route)


def neighbour_sum(values, from_above, from_below):
    upper = jnp.concatenate([from_above[None], values[:-1]], 0)
    lower = jnp.concatenate([values[1:], from_below[None]], 0)
    beside = jnp.pad(values[:, 1:], ((0, 0), (0, 1), (0, 0))) + jnp.pad(
        values[:, :-1], ((0, 0), (1, 0), (0, 0))
    )
    return beside + 0.5 * (lower + upper)


def neighbour_first(values, from_above, from_below):
    upper = jnp.concatenate([from_above[:, None], values[:, :-1]], 1)
    lower = jnp.concatenate([values[:, 1:], from_below[:, None]], 1)
    beside = jnp.pad(values[:, :, 1:], ((0, 0), (0, 0), (0, 1))) + jnp.pad(
        values[:, :, :-1], ((0, 0), (0, 0), (1, 0))
    )
    return beside + 0.5 * (lower + upper)


def stencil_term(payload, col_width, position, edge_codes):
    bin_count = lax.axis_size("bin")
    row_count = position.shape[0]
    group_size = row_count // bin_count
    grid_rows, grid_cols = edge_codes.shape
    pos_float = position.astype(jnp.float32).reshape(bin_count, group_size)
    got_rows, got_pos = (
        lax.all_to_all(payload, "bin", split_axis=0, concat_axis=0, tiled=True),
        lax.all_to_all(pos_float, "bin", split_axis=0, concat_axis=0, tiled=True),
    )
    tile_slot = got_pos.reshape(row_count).astype(jnp.int32) - lax.axis_index("bin") * row_count
    cell_scale = edge_codes.astype(jnp.float32) / 8.0
    tile_rows = (
        jnp.zeros((row_count, col_width), jnp.float32)
        .at[tile_slot]
        .set(got_rows.reshape(row_count, col_width))
    )
    weighted = cell_scale[:, :, None] * tile_rows.reshape(grid_rows, grid_cols, col_width)
    rim_last, rim_first = (weighted[-1], weighted[0])
    upper_rows, upper_scale = passed_along((rim_last, cell_scale[-1]), "bin", 1)
    lower_rows, lower_scale = passed_along((rim_first, cell_scale[0]), "bin", -1)
    degree_grid = (
        cell_scale * neighbour_first(cell_scale[None], upper_scale[None], lower_scale[None])[0]
    )
    back_degree = degree_grid.reshape(row_count)[tile_slot]
    smooth_grid = cell_scale[:, :, None] * neighbour_sum(weighted, upper_rows, lower_rows)
    back_send = smooth_grid.reshape(row_count, col_width)[tile_slot].reshape(
        bin_count, group_size * col_width
    )
    smooth, degree = (
        lax.all_to_all(back_send, "bin", split_axis=0, concat_axis=0, tiled=True),
        lax.all_to_all(
            back_degree.reshape(bin_count, group_size),
            "bin",
            split_axis=0,
            concat_axis=0,
            tiled=True,
        ),
    )
    smooth = smooth.reshape(row_count, col_width)
    return (smooth, degree.reshape(row_count))


def on_device(counts, factors, loadings, position, edge_codes):
    bin_count = lax.axis_size("bin")
    gene_count = lax.axis_size("gene")
    row_count, width_all = factors.shape
    group_size = row_count // bin_count
    width = width_all // gene_count
    k_rows = width_all // bin_count
    gene_at = lax.axis_index("gene")
    bin_at = lax.axis_index("bin")
    load_bf = loadings.astype(jnp.bfloat16)
    right_dims = (((1,), (1,)), ((), ()))
    numer_part = lax.dot_general(counts, load_bf, right_dims, preferred_element_type=jnp.float32)
    gram_part = lax.dot_general(load_bf, load_bf, right_dims, preferred_element_type=jnp.float32)
    numer, load_gram = lax.psum_scatter(
        (numer_part, gram_part), "gene", scatter_dimension=1, tiled=True
    )
    own = lax.dynamic_slice_in_dim(factors, gene_at * width, width, 1)
    payload = own.reshape(bin_count, group_size * width)
    smooth, degree = stencil_term(payload, width, position, edge_codes)
    penalty = float(G * K) / 64.0
    denom = (
        jnp.dot(factors, load_gram, precision=lax.Precision.HIGHEST)
        + penalty * degree[:, None] * own
    )
    new_own = own * (numer + penalty * smooth) / denom
    factors_new = lax.all_gather(new_own, "gene", axis=1, tiled=True)
    fac_bf = factors_new.astype(jnp.bfloat16)
    left_dims = (((0,), (0,)), ((), ()))
    cross_part = lax.dot_general(fac_bf, counts, left_dims, preferred_element_type=jnp.float32)
    fgram_part = lax.dot_general(fac_bf, fac_bf, left_dims, preferred_element_type=jnp.float32)
    cross, fac_gram = lax.psum_scatter(
        (cross_part, fgram_part), "bin", scatter_dimension=0, tiled=True
    )
    own_load = lax.dynamic_slice_in_dim(loadings, bin_at * k_rows, k_rows, 0)
    new_load = own_load * cross / jnp.dot(fac_gram, loadings, precision=lax.Precision.HIGHEST)
    loadings_new = lax.all_gather(new_load, "bin", axis=0, tiled=True)
    return (factors_new, loadings_new)


def solution(mesh):
    placed = (P("bin", "gene"), P("bin", None), P(None, "gene"), P("bin"), P("bin", None))
    return jax.shard_map(
        on_device,
        mesh=mesh,
        in_specs=placed,
        out_specs=(P("bin", None), P(None, "gene")),
        check_vma=False,
    )
```

```python
import jax
import jax.numpy as jnp
from jax import lax
from jax.sharding import PartitionSpec as P

K = 256
G = 18432


def passed_along(block, axis, distance):
    devices = range(lax.axis_size(axis))
    route = [(i - distance, i) for i in devices if i - distance in devices]
    return lax.ppermute(block, axis, route)


def neighbour_sum(values, from_above, from_below):
    upper = jnp.concatenate([from_above[None], values[:-1]], 0)
    lower = jnp.concatenate([values[1:], from_below[None]], 0)
    beside = jnp.pad(values[:, 1:], ((0, 0), (0, 1), (0, 0))) + jnp.pad(
        values[:, :-1], ((0, 0), (1, 0), (0, 0))
    )
    return beside + 0.5 * (lower + upper)


def neighbour_first(values, from_above, from_below):
    upper = jnp.concatenate([from_above[:, None], values[:, :-1]], 1)
    lower = jnp.concatenate([values[:, 1:], from_below[:, None]], 1)
    beside = jnp.pad(values[:, :, 1:], ((0, 0), (0, 0), (0, 1))) + jnp.pad(
        values[:, :, :-1], ((0, 0), (0, 0), (1, 0))
    )
    return beside + 0.5 * (lower + upper)


def split_three(values):
    high = lax.reduce_precision(values, exponent_bits=8, mantissa_bits=7)
    rest = values - high
    mid = lax.reduce_precision(rest, exponent_bits=8, mantissa_bits=7)
    low = rest - mid
    return jnp.concatenate([high, mid, low], 1).astype(jnp.bfloat16)


def join_three(parts, width):
    return (parts[:, :width] + parts[:, width : 2 * width]) + parts[:, 2 * width :]


def stencil_term(own, position, edge_codes):
    bin_count = lax.axis_size("bin")
    row_count, width = own.shape
    group_size = row_count // bin_count
    grid_rows, grid_cols = edge_codes.shape
    payload = jnp.concatenate([own, position.astype(jnp.float32)[:, None]], 1)
    got = lax.all_to_all(
        payload.reshape(bin_count, group_size * (width + 1)), "bin", 0, 0, tiled=True
    ).reshape(row_count, width + 1)
    tile_slot = got[:, width].astype(jnp.int32) - lax.axis_index("bin") * row_count
    cells = lax.broadcasted_iota(jnp.int32, (row_count, row_count), 1)
    onehot = (tile_slot[:, None] == cells).astype(jnp.bfloat16)
    placed = lax.dot_general(
        onehot, split_three(got[:, :width]), (((0,), (0,)), ((), ())),
        preferred_element_type=jnp.float32,
    )
    tile_rows = join_three(placed, width)
    cell_scale = edge_codes.astype(jnp.float32) / 8.0
    weighted = cell_scale[:, :, None] * tile_rows.reshape(grid_rows, grid_cols, width)
    rim_last, rim_first = (weighted[-1], weighted[0])
    upper_rows, upper_scale = passed_along((rim_last, cell_scale[-1]), "bin", 1)
    lower_rows, lower_scale = passed_along((rim_first, cell_scale[0]), "bin", -1)
    degree_grid = (
        cell_scale * neighbour_first(cell_scale[None], upper_scale[None], lower_scale[None])[0]
    )
    smooth_grid = cell_scale[:, :, None] * neighbour_sum(weighted, upper_rows, lower_rows)
    back = jnp.concatenate(
        [smooth_grid.reshape(row_count, width), degree_grid.reshape(row_count, 1)], 1
    )
    back_rows = join_three(
        jnp.dot(onehot, split_three(back), preferred_element_type=jnp.float32), width + 1
    )
    ret = lax.all_to_all(
        back_rows.reshape(bin_count, group_size * (width + 1)), "bin", 0, 0, tiled=True
    ).reshape(row_count, width + 1)
    return (ret[:, :width], ret[:, width])


def on_device(counts, factors, loadings, position, edge_codes):
    bin_count = lax.axis_size("bin")
    gene_count = lax.axis_size("gene")
    row_count, width_all = factors.shape
    group_size = row_count // bin_count
    width = width_all // gene_count
    k_rows = width_all // bin_count
    gene_at = lax.axis_index("gene")
    bin_at = lax.axis_index("bin")
    load_bf = loadings.astype(jnp.bfloat16)
    right_dims = (((1,), (1,)), ((), ()))
    numer_part = lax.dot_general(counts, load_bf, right_dims, preferred_element_type=jnp.float32)
    gram_part = lax.dot_general(load_bf, load_bf, right_dims, preferred_element_type=jnp.float32)
    both = lax.psum_scatter(
        jnp.concatenate([numer_part, gram_part], 0), "gene", scatter_dimension=1, tiled=True
    )
    numer, load_gram = both[:row_count], both[row_count:]
    own = lax.dynamic_slice_in_dim(factors, gene_at * width, width, 1)
    smooth, degree = stencil_term(own, position, edge_codes)
    penalty = float(G * K) / 64.0
    denom = (
        jnp.dot(factors, load_gram, precision=lax.Precision.HIGHEST)
        + penalty * degree[:, None] * own
    )
    new_own = own * (numer + penalty * smooth) / denom
    factors_new = lax.all_gather(new_own, "gene", axis=1, tiled=True)
    fac_bf = factors_new.astype(jnp.bfloat16)
    left_dims = (((0,), (0,)), ((), ()))
    cross_part = lax.dot_general(fac_bf, counts, left_dims, preferred_element_type=jnp.float32)
    fgram_part = lax.dot_general(fac_bf, fac_bf, left_dims, preferred_element_type=jnp.float32)
    both_bin = lax.psum_scatter(
        jnp.concatenate([cross_part, fgram_part], 1), "bin", scatter_dimension=0, tiled=True
    )
    cross, fac_gram = both_bin[:, : cross_part.shape[1]], both_bin[:, cross_part.shape[1] :]
    own_load = lax.dynamic_slice_in_dim(loadings, bin_at * k_rows, k_rows, 0)
    new_load = own_load * cross / jnp.dot(fac_gram, loadings, precision=lax.Precision.HIGHEST)
    loadings_new = lax.all_gather(new_load, "bin", axis=0, tiled=True)
    return (factors_new, loadings_new)


def solution(mesh):
    placed = (P("bin", "gene"), P("bin", None), P(None, "gene"), P("bin"), P("bin", None))
    return jax.shard_map(
        on_device,
        mesh=mesh,
        in_specs=placed,
        out_specs=(P("bin", None), P(None, "gene")),
        check_vma=False,
    )
```

```python
import functools

import jax
import jax.numpy as jnp
from jax import lax
from jax.experimental import pallas as pl
from jax.experimental.pallas import tpu as pltpu
from jax.sharding import PartitionSpec as P

K = 256
G = 18432


def passed_along(block, axis, distance):
    devices = range(lax.axis_size(axis))
    route = [(i - distance, i) for i in devices if i - distance in devices]
    return lax.ppermute(block, axis, route)


def neighbour_sum(values, from_above, from_below):
    upper = jnp.concatenate([from_above[None], values[:-1]], 0)
    lower = jnp.concatenate([values[1:], from_below[None]], 0)
    beside = jnp.pad(values[:, 1:], ((0, 0), (0, 1), (0, 0))) + jnp.pad(
        values[:, :-1], ((0, 0), (1, 0), (0, 0))
    )
    return beside + 0.5 * (lower + upper)


def neighbour_first(values, from_above, from_below):
    upper = jnp.concatenate([from_above[:, None], values[:, :-1]], 1)
    lower = jnp.concatenate([values[:, 1:], from_below[:, None]], 1)
    beside = jnp.pad(values[:, :, 1:], ((0, 0), (0, 0), (0, 1))) + jnp.pad(
        values[:, :, :-1], ((0, 0), (0, 0), (1, 0))
    )
    return beside + 0.5 * (lower + upper)


def snake_gene(place, count):
    wide = 1 - ((place + count - 1) % count) // (count // 2)
    row = wide * (place - 1) + (1 - wide) * ((count - place) % count)
    return 2 * row + wide


def snake_place(index, count):
    row, wide = index // 2, index % 2
    return wide * (1 + row) + (1 - wide) * ((count - row) % count)


def gather_kernel(count, x_ref, out_ref, send_sem, recv_sem):
    me = lax.axis_index("gene")
    place = snake_place(me, count)
    ahead = snake_gene((place + 1) % count, count)
    behind = snake_gene((place + count - 1) % count, count)
    half = x_ref.shape[0] // 2
    barrier = pltpu.get_barrier_semaphore()
    for peer in (ahead, behind):
        pl.semaphore_signal(barrier, inc=1, device_id={"gene": peer},
                            device_id_type=pl.DeviceIdType.MESH)
    pl.semaphore_wait(barrier, 2)
    out_ref[me] = x_ref[...]

    def copy(step, way):
        rows = pl.ds(way * half, half)
        if way == 0:
            origin = snake_gene((place - step + count) % count, count)
            target = ahead
        else:
            origin = snake_gene((place + step) % count, count)
            target = behind
        src = x_ref.at[rows] if step == 0 else out_ref.at[origin, rows]
        return pltpu.make_async_remote_copy(
            src_ref=src,
            dst_ref=out_ref.at[origin, rows],
            send_sem=send_sem.at[way, step],
            recv_sem=recv_sem.at[way, step],
            device_id={"gene": target},
            device_id_type=pl.DeviceIdType.MESH,
        )

    for step in range(count - 1):
        for way in (0, 1):
            if step >= 1:
                copy(step - 1, way).wait_recv()
            copy(step, way).start()
    for way in (0, 1):
        copy(count - 2, way).wait_recv()
    for step in range(count - 1):
        for way in (0, 1):
            copy(step, way).wait_send()


def gene_gather(x):
    count = lax.axis_size("gene")
    return pl.pallas_call(
        functools.partial(gather_kernel, count),
        out_shape=jax.ShapeDtypeStruct((count,) + x.shape, x.dtype),
        in_specs=[pl.BlockSpec(memory_space=pltpu.VMEM)],
        out_specs=pl.BlockSpec(memory_space=pltpu.VMEM),
        scratch_shapes=[
            pltpu.SemaphoreType.DMA((2, count - 1)),
            pltpu.SemaphoreType.DMA((2, count - 1)),
        ],
        compiler_params=pltpu.CompilerParams(collective_id=0, has_side_effects=True),
    )(x)


def split_three(values):
    high = lax.reduce_precision(values, exponent_bits=8, mantissa_bits=7)
    rest = values - high
    mid = lax.reduce_precision(rest, exponent_bits=8, mantissa_bits=7)
    low = rest - mid
    return jnp.concatenate([high, mid, low], 1).astype(jnp.bfloat16)


def join_three(parts, width):
    return (parts[:, :width] + parts[:, width : 2 * width]) + parts[:, 2 * width :]


def stencil_term(own, position, edge_codes):
    bin_count = lax.axis_size("bin")
    row_count, width = own.shape
    group_size = row_count // bin_count
    grid_rows, grid_cols = edge_codes.shape
    payload = jnp.concatenate([own, position.astype(jnp.float32)[:, None]], 1)
    got = lax.all_to_all(
        payload.reshape(bin_count, group_size * (width + 1)), "bin", 0, 0, tiled=True
    ).reshape(row_count, width + 1)
    tile_slot = got[:, width].astype(jnp.int32) - lax.axis_index("bin") * row_count
    cells = lax.broadcasted_iota(jnp.int32, (row_count, row_count), 1)
    onehot = (tile_slot[:, None] == cells).astype(jnp.bfloat16)
    placed = lax.dot_general(
        onehot, split_three(got[:, :width]), (((0,), (0,)), ((), ())),
        preferred_element_type=jnp.float32,
    )
    tile_rows = join_three(placed, width)
    cell_scale = edge_codes.astype(jnp.float32) / 8.0
    weighted = cell_scale[:, :, None] * tile_rows.reshape(grid_rows, grid_cols, width)
    rim_last, rim_first = (weighted[-1], weighted[0])
    upper_rows, upper_scale = passed_along((rim_last, cell_scale[-1]), "bin", 1)
    lower_rows, lower_scale = passed_along((rim_first, cell_scale[0]), "bin", -1)
    degree_grid = (
        cell_scale * neighbour_first(cell_scale[None], upper_scale[None], lower_scale[None])[0]
    )
    smooth_grid = cell_scale[:, :, None] * neighbour_sum(weighted, upper_rows, lower_rows)
    back = jnp.concatenate(
        [smooth_grid.reshape(row_count, width), degree_grid.reshape(row_count, 1)], 1
    )
    back_rows = join_three(
        jnp.dot(onehot, split_three(back), preferred_element_type=jnp.float32), width + 1
    )
    ret = lax.all_to_all(
        back_rows.reshape(bin_count, group_size * (width + 1)), "bin", 0, 0, tiled=True
    ).reshape(row_count, width + 1)
    return (ret[:, :width], ret[:, width])


def on_device(counts, factors, loadings, position, edge_codes):
    bin_count = lax.axis_size("bin")
    gene_count = lax.axis_size("gene")
    row_count, width_all = factors.shape
    group_size = row_count // bin_count
    width = width_all // gene_count
    k_rows = width_all // bin_count
    gene_at = lax.axis_index("gene")
    bin_at = lax.axis_index("bin")
    load_bf = loadings.astype(jnp.bfloat16)
    right_dims = (((1,), (1,)), ((), ()))
    numer_part = lax.dot_general(counts, load_bf, right_dims, preferred_element_type=jnp.float32)
    gram_part = lax.dot_general(load_bf, load_bf, right_dims, preferred_element_type=jnp.float32)
    both = lax.psum_scatter(
        jnp.concatenate([numer_part, gram_part], 0), "gene", scatter_dimension=1, tiled=True
    )
    numer, load_gram = both[:row_count], both[row_count:]
    own = lax.dynamic_slice_in_dim(factors, gene_at * width, width, 1)
    smooth, degree = stencil_term(own, position, edge_codes)
    penalty = float(G * K) / 64.0
    denom = (
        jnp.dot(factors, load_gram, precision=lax.Precision.HIGHEST)
        + penalty * degree[:, None] * own
    )
    new_own = own * (numer + penalty * smooth) / denom
    factors_t = gene_gather(new_own.T).reshape(width_all, row_count)
    factors_new = factors_t.T
    fac_bf_t = factors_t.astype(jnp.bfloat16)
    cross_part = jnp.dot(fac_bf_t, counts, preferred_element_type=jnp.float32)
    fgram_part = lax.dot_general(fac_bf_t, fac_bf_t, right_dims, preferred_element_type=jnp.float32)
    both_bin = lax.psum_scatter(
        jnp.concatenate([cross_part, fgram_part], 1), "bin", scatter_dimension=0, tiled=True
    )
    cross, fac_gram = both_bin[:, : cross_part.shape[1]], both_bin[:, cross_part.shape[1] :]
    own_load = lax.dynamic_slice_in_dim(loadings, bin_at * k_rows, k_rows, 0)
    new_load = own_load * cross / jnp.dot(fac_gram, loadings, precision=lax.Precision.HIGHEST)
    loadings_new = lax.all_gather(new_load, "bin", axis=0, tiled=True)
    return (factors_new, loadings_new)


def solution(mesh):
    placed = (P("bin", "gene"), P("bin", None), P(None, "gene"), P("bin"), P("bin", None))
    return jax.shard_map(
        on_device,
        mesh=mesh,
        in_specs=placed,
        out_specs=(P("bin", None), P(None, "gene")),
        check_vma=False,
    )
```

```python
import functools

import jax
import jax.numpy as jnp
from jax import lax
from jax.experimental import pallas as pl
from jax.experimental.pallas import tpu as pltpu
from jax.sharding import PartitionSpec as P

K = 256
G = 18432


def passed_along(block, axis, distance):
    devices = range(lax.axis_size(axis))
    route = [(i - distance, i) for i in devices if i - distance in devices]
    return lax.ppermute(block, axis, route)


def neighbour_sum(values, from_above, from_below):
    upper = jnp.concatenate([from_above[None], values[:-1]], 0)
    lower = jnp.concatenate([values[1:], from_below[None]], 0)
    beside = jnp.pad(values[:, 1:], ((0, 0), (0, 1), (0, 0))) + jnp.pad(
        values[:, :-1], ((0, 0), (1, 0), (0, 0))
    )
    return beside + 0.5 * (lower + upper)


def neighbour_first(values, from_above, from_below):
    upper = jnp.concatenate([from_above[:, None], values[:, :-1]], 1)
    lower = jnp.concatenate([values[:, 1:], from_below[:, None]], 1)
    beside = jnp.pad(values[:, :, 1:], ((0, 0), (0, 0), (0, 1))) + jnp.pad(
        values[:, :, :-1], ((0, 0), (0, 0), (1, 0))
    )
    return beside + 0.5 * (lower + upper)


def gray(value):
    return value + (value // 2) * (1 - 2 * (value % 2))


def gene_at_place(place, count):
    wide = 1 - ((place + count - 1) % count) // (count // 2)
    row = wide * (place - 1) + (1 - wide) * ((count - place) % count)
    return 2 * row + wide


def gene_place(index, count):
    row, wide = index // 2, index % 2
    return wide * (1 + row) + (1 - wide) * ((count - row) % count)


def bin_at_place(place, count):
    plane, step = place // 4, place % 4
    turned = step + (plane % 2) * (3 - 2 * step)
    return plane * 4 + gray(turned)


def bin_place(index, count):
    plane = index // 4
    turned = gray(index % 4)
    return plane * 4 + turned + (plane % 2) * (3 - 2 * turned)


RINGS = {"gene": (gene_at_place, gene_place), "bin": (bin_at_place, bin_place)}


def ring_peers(axis, count):
    at_place, place_of = RINGS[axis]
    place = place_of(lax.axis_index(axis), count)
    return place, (lambda shift: at_place((place + shift + count) % count, count))


def enter(axis, peers):
    barrier = pltpu.get_barrier_semaphore()
    for peer in peers:
        pl.semaphore_signal(barrier, inc=1, device_id={axis: peer},
                            device_id_type=pl.DeviceIdType.MESH)
    pl.semaphore_wait(barrier, len(peers))


def gather_kernel(axis, count, x_ref, out_ref, send_sem, recv_sem):
    place, member = ring_peers(axis, count)
    ahead, behind = member(1), member(-1)
    half = x_ref.shape[0] // 2
    enter(axis, (ahead, behind))
    out_ref[member(0)] = x_ref[...]

    def copy(step, way):
        rows = pl.ds(way * half, half)
        origin = member(-step) if way == 0 else member(step)
        src = x_ref.at[rows] if step == 0 else out_ref.at[origin, rows]
        return pltpu.make_async_remote_copy(
            src_ref=src,
            dst_ref=out_ref.at[origin, rows],
            send_sem=send_sem.at[way, step],
            recv_sem=recv_sem.at[way, step],
            device_id={axis: ahead if way == 0 else behind},
            device_id_type=pl.DeviceIdType.MESH,
        )

    for step in range(count - 1):
        for way in (0, 1):
            if step >= 1:
                copy(step - 1, way).wait_recv()
            copy(step, way).start()
    for way in (0, 1):
        copy(count - 2, way).wait_recv()
    for step in range(count - 1):
        for way in (0, 1):
            copy(step, way).wait_send()


def ring_gather(x, axis, collective_id):
    count = lax.axis_size(axis)
    return pl.pallas_call(
        functools.partial(gather_kernel, axis, count),
        out_shape=jax.ShapeDtypeStruct((count,) + x.shape, x.dtype),
        in_specs=[pl.BlockSpec(memory_space=pltpu.VMEM)],
        out_specs=pl.BlockSpec(memory_space=pltpu.VMEM),
        scratch_shapes=[
            pltpu.SemaphoreType.DMA((2, count - 1)),
            pltpu.SemaphoreType.DMA((2, count - 1)),
        ],
        compiler_params=pltpu.CompilerParams(
            collective_id=collective_id, has_side_effects=True
        ),
    )(x)


def scatter_kernel(axis, count, x_ref, out_ref, got, sent, send_sem, recv_sem):
    place, member = ring_peers(axis, count)
    ahead, behind = member(1), member(-1)
    half = x_ref.shape[2] // 2
    enter(axis, (ahead, behind))

    def copy(step, way):
        lanes = pl.ds(way * half, half)
        if step == 0:
            source = x_ref.at[member(-1) if way == 0 else member(1), :, lanes]
        else:
            source = sent.at[way, step]
        return pltpu.make_async_remote_copy(
            src_ref=source,
            dst_ref=got.at[way, step],
            send_sem=send_sem.at[way, step],
            recv_sem=recv_sem.at[way, step],
            device_id={axis: ahead if way == 0 else behind},
            device_id_type=pl.DeviceIdType.MESH,
        )

    for step in range(count - 1):
        for way in (0, 1):
            if step >= 1:
                lanes = pl.ds(way * half, half)
                owner = member(-step - 1) if way == 0 else member(step + 1)
                copy(step - 1, way).wait_recv()
                sent[way, step] = got[way, step - 1] + x_ref[owner, :, lanes]
            copy(step, way).start()
    for way in (0, 1):
        lanes = pl.ds(way * half, half)
        copy(count - 2, way).wait_recv()
        out_ref[:, lanes] = got[way, count - 2] + x_ref[member(0), :, lanes]
    for step in range(count - 1):
        for way in (0, 1):
            copy(step, way).wait_send()


def ring_scatter(x, axis, collective_id):
    count, rows, lanes = x.shape
    return pl.pallas_call(
        functools.partial(scatter_kernel, axis, count),
        out_shape=jax.ShapeDtypeStruct((rows, lanes), x.dtype),
        in_specs=[pl.BlockSpec(memory_space=pltpu.VMEM)],
        out_specs=pl.BlockSpec(memory_space=pltpu.VMEM),
        scratch_shapes=[
            pltpu.VMEM((2, count - 1, rows, lanes // 2), x.dtype),
            pltpu.VMEM((2, count - 1, rows, lanes // 2), x.dtype),
            pltpu.SemaphoreType.DMA((2, count - 1)),
            pltpu.SemaphoreType.DMA((2, count - 1)),
        ],
        compiler_params=pltpu.CompilerParams(
            collective_id=collective_id, has_side_effects=True
        ),
    )(x)


def split_three(values):
    high = lax.reduce_precision(values, exponent_bits=8, mantissa_bits=7)
    rest = values - high
    mid = lax.reduce_precision(rest, exponent_bits=8, mantissa_bits=7)
    low = rest - mid
    return jnp.concatenate([high, mid, low], 1).astype(jnp.bfloat16)


def join_three(parts, width):
    return (parts[:, :width] + parts[:, width : 2 * width]) + parts[:, 2 * width :]


def stencil_term(own, position, edge_codes):
    bin_count = lax.axis_size("bin")
    row_count, width = own.shape
    group_size = row_count // bin_count
    grid_rows, grid_cols = edge_codes.shape
    payload = jnp.concatenate([own, position.astype(jnp.float32)[:, None]], 1)
    got = lax.all_to_all(
        payload.reshape(bin_count, group_size * (width + 1)), "bin", 0, 0, tiled=True
    ).reshape(row_count, width + 1)
    tile_slot = got[:, width].astype(jnp.int32) - lax.axis_index("bin") * row_count
    cells = lax.broadcasted_iota(jnp.int32, (row_count, row_count), 1)
    onehot = (tile_slot[:, None] == cells).astype(jnp.bfloat16)
    placed = lax.dot_general(
        onehot, split_three(got[:, :width]), (((0,), (0,)), ((), ())),
        preferred_element_type=jnp.float32,
    )
    tile_rows = join_three(placed, width)
    cell_scale = edge_codes.astype(jnp.float32) / 8.0
    weighted = cell_scale[:, :, None] * tile_rows.reshape(grid_rows, grid_cols, width)
    rim_last, rim_first = (weighted[-1], weighted[0])
    upper_rows, upper_scale = passed_along((rim_last, cell_scale[-1]), "bin", 1)
    lower_rows, lower_scale = passed_along((rim_first, cell_scale[0]), "bin", -1)
    degree_grid = (
        cell_scale * neighbour_first(cell_scale[None], upper_scale[None], lower_scale[None])[0]
    )
    smooth_grid = cell_scale[:, :, None] * neighbour_sum(weighted, upper_rows, lower_rows)
    back = jnp.concatenate(
        [smooth_grid.reshape(row_count, width), degree_grid.reshape(row_count, 1)], 1
    )
    back_rows = join_three(
        jnp.dot(onehot, split_three(back), preferred_element_type=jnp.float32), width + 1
    )
    ret = lax.all_to_all(
        back_rows.reshape(bin_count, group_size * (width + 1)), "bin", 0, 0, tiled=True
    ).reshape(row_count, width + 1)
    return (ret[:, :width], ret[:, width])


def on_device(counts, factors, loadings, position, edge_codes):
    bin_count = lax.axis_size("bin")
    gene_count = lax.axis_size("gene")
    row_count, width_all = factors.shape
    width = width_all // gene_count
    k_rows = width_all // bin_count
    gene_at = lax.axis_index("gene")
    bin_at = lax.axis_index("bin")
    load_bf = loadings.astype(jnp.bfloat16)
    right_dims = (((1,), (1,)), ((), ()))
    numer_part = lax.dot_general(load_bf, counts, right_dims, preferred_element_type=jnp.float32)
    gram_part = lax.dot_general(load_bf, load_bf, right_dims, preferred_element_type=jnp.float32)
    both = jnp.concatenate([numer_part, gram_part], 1)
    both = ring_scatter(both.reshape(gene_count, width, -1), "gene", 1)
    numer_t, gram_rows = both[:, :row_count], both[:, row_count:]
    own = lax.dynamic_slice_in_dim(factors, gene_at * width, width, 1)
    smooth, degree = stencil_term(own, position, edge_codes)
    penalty = float(G * K) / 64.0
    own_t = own.T
    denom_t = (
        lax.dot_general(gram_rows, factors, right_dims, precision=lax.Precision.HIGHEST)
        + penalty * degree[None, :] * own_t
    )
    new_t = own_t * (numer_t + penalty * smooth.T) / denom_t
    factors_t = ring_gather(new_t, "gene", 0).reshape(width_all, row_count)
    factors_new = factors_t.T
    fac_bf_t = factors_t.astype(jnp.bfloat16)
    cross_part = jnp.dot(fac_bf_t, counts, preferred_element_type=jnp.float32)
    fgram_part = lax.dot_general(fac_bf_t, fac_bf_t, right_dims, preferred_element_type=jnp.float32)
    both_bin = jnp.concatenate([cross_part, fgram_part], 1)
    both_bin = ring_scatter(both_bin.reshape(bin_count, k_rows, -1), "bin", 2)
    cross, fac_gram = both_bin[:, : cross_part.shape[1]], both_bin[:, cross_part.shape[1] :]
    own_load = lax.dynamic_slice_in_dim(loadings, bin_at * k_rows, k_rows, 0)
    new_load = own_load * cross / jnp.dot(fac_gram, loadings, precision=lax.Precision.HIGHEST)
    loadings_new = ring_gather(new_load, "bin", 3).reshape(width_all, -1)
    return (factors_new, loadings_new)


def solution(mesh):
    placed = (P("bin", "gene"), P("bin", None), P(None, "gene"), P("bin"), P("bin", None))
    return jax.shard_map(
        on_device,
        mesh=mesh,
        in_specs=placed,
        out_specs=(P("bin", None), P(None, "gene")),
        check_vma=False,
    )
```

```python
import functools

import jax
import jax.numpy as jnp
from jax import lax
from jax.experimental import pallas as pl
from jax.experimental.pallas import tpu as pltpu
from jax.sharding import PartitionSpec as P

K = 256
G = 18432


def passed_along(block, axis, distance):
    devices = range(lax.axis_size(axis))
    route = [(i - distance, i) for i in devices if i - distance in devices]
    return lax.ppermute(block, axis, route)


def neighbour_sum(values, from_above, from_below):
    upper = jnp.concatenate([from_above[None], values[:-1]], 0)
    lower = jnp.concatenate([values[1:], from_below[None]], 0)
    beside = jnp.pad(values[:, 1:], ((0, 0), (0, 1), (0, 0))) + jnp.pad(
        values[:, :-1], ((0, 0), (1, 0), (0, 0))
    )
    return beside + 0.5 * (lower + upper)


def neighbour_first(values, from_above, from_below):
    upper = jnp.concatenate([from_above[:, None], values[:, :-1]], 1)
    lower = jnp.concatenate([values[:, 1:], from_below[:, None]], 1)
    beside = jnp.pad(values[:, :, 1:], ((0, 0), (0, 0), (0, 1))) + jnp.pad(
        values[:, :, :-1], ((0, 0), (0, 0), (1, 0))
    )
    return beside + 0.5 * (lower + upper)


def gray(value):
    return value + (value // 2) * (1 - 2 * (value % 2))


def gene_at_place(place, count):
    wide = 1 - ((place + count - 1) % count) // (count // 2)
    row = wide * (place - 1) + (1 - wide) * ((count - place) % count)
    return 2 * row + wide


def gene_place(index, count):
    row, wide = index // 2, index % 2
    return wide * (1 + row) + (1 - wide) * ((count - row) % count)


def bin_at_place(place, count):
    plane, step = place // 4, place % 4
    turned = step + (plane % 2) * (3 - 2 * step)
    return plane * 4 + gray(turned)


def bin_place(index, count):
    plane = index // 4
    turned = gray(index % 4)
    return plane * 4 + turned + (plane % 2) * (3 - 2 * turned)


RINGS = {"gene": (gene_at_place, gene_place), "bin": (bin_at_place, bin_place)}


def ring_peers(axis, count):
    at_place, place_of = RINGS[axis]
    place = place_of(lax.axis_index(axis), count)
    return place, (lambda shift: at_place((place + shift + count) % count, count))


def enter(axis, peers):
    barrier = pltpu.get_barrier_semaphore()
    for peer in peers:
        pl.semaphore_signal(barrier, inc=1, device_id={axis: peer},
                            device_id_type=pl.DeviceIdType.MESH)
    pl.semaphore_wait(barrier, len(peers))


def gather_kernel(axis, count, x_ref, out_ref, send_sem, recv_sem):
    place, member = ring_peers(axis, count)
    ahead, behind = member(1), member(-1)
    half = x_ref.shape[0] // 2
    enter(axis, (ahead, behind))
    out_ref[member(0)] = x_ref[...]

    def copy(step, way):
        rows = pl.ds(way * half, half)
        origin = member(-step) if way == 0 else member(step)
        src = x_ref.at[rows] if step == 0 else out_ref.at[origin, rows]
        return pltpu.make_async_remote_copy(
            src_ref=src,
            dst_ref=out_ref.at[origin, rows],
            send_sem=send_sem.at[way, step],
            recv_sem=recv_sem.at[way, step],
            device_id={axis: ahead if way == 0 else behind},
            device_id_type=pl.DeviceIdType.MESH,
        )

    for step in range(count - 1):
        for way in (0, 1):
            if step >= 1:
                copy(step - 1, way).wait_recv()
            copy(step, way).start()
    for way in (0, 1):
        copy(count - 2, way).wait_recv()
    for step in range(count - 1):
        for way in (0, 1):
            copy(step, way).wait_send()


def ring_gather(x, axis, collective_id):
    count = lax.axis_size(axis)
    return pl.pallas_call(
        functools.partial(gather_kernel, axis, count),
        out_shape=jax.ShapeDtypeStruct((count,) + x.shape, x.dtype),
        in_specs=[pl.BlockSpec(memory_space=pltpu.VMEM)],
        out_specs=pl.BlockSpec(memory_space=pltpu.VMEM),
        scratch_shapes=[
            pltpu.SemaphoreType.DMA((2, count - 1)),
            pltpu.SemaphoreType.DMA((2, count - 1)),
        ],
        compiler_params=pltpu.CompilerParams(
            collective_id=collective_id, has_side_effects=True
        ),
    )(x)


def scatter_kernel(axis, count, x_ref, out_ref, got, sent, send_sem, recv_sem):
    place, member = ring_peers(axis, count)
    ahead, behind = member(1), member(-1)
    half = x_ref.shape[2] // 2
    enter(axis, (ahead, behind))

    def copy(step, way):
        lanes = pl.ds(way * half, half)
        if step == 0:
            source = x_ref.at[member(-1) if way == 0 else member(1), :, lanes]
        else:
            source = sent.at[way, step]
        return pltpu.make_async_remote_copy(
            src_ref=source,
            dst_ref=got.at[way, step],
            send_sem=send_sem.at[way, step],
            recv_sem=recv_sem.at[way, step],
            device_id={axis: ahead if way == 0 else behind},
            device_id_type=pl.DeviceIdType.MESH,
        )

    for step in range(count - 1):
        for way in (0, 1):
            if step >= 1:
                lanes = pl.ds(way * half, half)
                owner = member(-step - 1) if way == 0 else member(step + 1)
                copy(step - 1, way).wait_recv()
                sent[way, step] = got[way, step - 1] + x_ref[owner, :, lanes]
            copy(step, way).start()
    for way in (0, 1):
        lanes = pl.ds(way * half, half)
        copy(count - 2, way).wait_recv()
        out_ref[:, lanes] = got[way, count - 2] + x_ref[member(0), :, lanes]
    for step in range(count - 1):
        for way in (0, 1):
            copy(step, way).wait_send()


def ring_scatter(x, axis, collective_id):
    count, rows, lanes = x.shape
    return pl.pallas_call(
        functools.partial(scatter_kernel, axis, count),
        out_shape=jax.ShapeDtypeStruct((rows, lanes), x.dtype),
        in_specs=[pl.BlockSpec(memory_space=pltpu.VMEM)],
        out_specs=pl.BlockSpec(memory_space=pltpu.VMEM),
        scratch_shapes=[
            pltpu.VMEM((2, count - 1, rows, lanes // 2), x.dtype),
            pltpu.VMEM((2, count - 1, rows, lanes // 2), x.dtype),
            pltpu.SemaphoreType.DMA((2, count - 1)),
            pltpu.SemaphoreType.DMA((2, count - 1)),
        ],
        compiler_params=pltpu.CompilerParams(
            collective_id=collective_id, has_side_effects=True
        ),
    )(x)


def split_three(values):
    high = lax.reduce_precision(values, exponent_bits=8, mantissa_bits=7)
    rest = values - high
    mid = lax.reduce_precision(rest, exponent_bits=8, mantissa_bits=7)
    low = rest - mid
    return jnp.concatenate([high, mid, low], 1).astype(jnp.bfloat16)


def join_three(parts, width):
    return (parts[:, :width] + parts[:, width : 2 * width]) + parts[:, 2 * width :]


def stencil_term(own, position, edge_codes):
    bin_count = lax.axis_size("bin")
    row_count, width = own.shape
    group_size = row_count // bin_count
    grid_rows, grid_cols = edge_codes.shape
    payload = jnp.concatenate([own, position.astype(jnp.float32)[:, None]], 1)
    got = lax.all_to_all(
        payload.reshape(bin_count, group_size * (width + 1)), "bin", 0, 0, tiled=True
    ).reshape(row_count, width + 1)
    tile_slot = got[:, width].astype(jnp.int32) - lax.axis_index("bin") * row_count
    cells = lax.broadcasted_iota(jnp.int32, (row_count, row_count), 1)
    onehot = (tile_slot[:, None] == cells).astype(jnp.bfloat16)
    placed = lax.dot_general(
        onehot, split_three(got[:, :width]), (((0,), (0,)), ((), ())),
        preferred_element_type=jnp.float32,
    )
    tile_rows = join_three(placed, width)
    cell_scale = edge_codes.astype(jnp.float32) / 8.0
    weighted = cell_scale[:, :, None] * tile_rows.reshape(grid_rows, grid_cols, width)
    rim_last, rim_first = (weighted[-1], weighted[0])
    upper_rows, upper_scale = passed_along((rim_last, cell_scale[-1]), "bin", 1)
    lower_rows, lower_scale = passed_along((rim_first, cell_scale[0]), "bin", -1)
    degree_grid = (
        cell_scale * neighbour_first(cell_scale[None], upper_scale[None], lower_scale[None])[0]
    )
    smooth_grid = cell_scale[:, :, None] * neighbour_sum(weighted, upper_rows, lower_rows)
    back = jnp.concatenate(
        [smooth_grid.reshape(row_count, width), degree_grid.reshape(row_count, 1)], 1
    )
    back_rows = join_three(
        jnp.dot(onehot, split_three(back), preferred_element_type=jnp.float32), width + 1
    )
    ret = lax.all_to_all(
        back_rows.reshape(bin_count, group_size * (width + 1)), "bin", 0, 0, tiled=True
    ).reshape(row_count, width + 1)
    return (ret[:, :width], ret[:, width])


def on_device(counts, factors, loadings, position, edge_codes):
    bin_count = lax.axis_size("bin")
    gene_count = lax.axis_size("gene")
    row_count, width_all = factors.shape
    width = width_all // gene_count
    k_rows = width_all // bin_count
    gene_at = lax.axis_index("gene")
    bin_at = lax.axis_index("bin")
    load_bf = loadings.astype(jnp.bfloat16)
    right_dims = (((1,), (1,)), ((), ()))
    numer_part = lax.dot_general(load_bf, counts, right_dims, preferred_element_type=jnp.float32)
    gram_part = lax.dot_general(load_bf, load_bf, right_dims, preferred_element_type=jnp.float32)
    both = jnp.concatenate([numer_part, gram_part], 1)
    both = lax.psum_scatter(
        both.reshape(gene_count, width, -1), "gene", scatter_dimension=0, tiled=True
    ).reshape(width, -1)
    numer_t, gram_rows = both[:, :row_count], both[:, row_count:]
    own = lax.dynamic_slice_in_dim(factors, gene_at * width, width, 1)
    smooth, degree = stencil_term(own, position, edge_codes)
    penalty = float(G * K) / 64.0
    own_t = own.T
    denom_t = (
        lax.dot_general(gram_rows, factors, right_dims, precision=lax.Precision.HIGHEST)
        + penalty * degree[None, :] * own_t
    )
    new_t = own_t * (numer_t + penalty * smooth.T) / denom_t
    factors_t = ring_gather(new_t, "gene", 0).reshape(width_all, row_count)
    factors_new = factors_t.T
    fac_bf_t = factors_t.astype(jnp.bfloat16)
    cross_part = jnp.dot(fac_bf_t, counts, preferred_element_type=jnp.float32)
    fgram_part = lax.dot_general(fac_bf_t, fac_bf_t, right_dims, preferred_element_type=jnp.float32)
    both_bin = jnp.concatenate([cross_part, fgram_part], 1)
    both_bin = ring_scatter(both_bin.reshape(bin_count, k_rows, -1), "bin", 2)
    cross, fac_gram = both_bin[:, : cross_part.shape[1]], both_bin[:, cross_part.shape[1] :]
    own_load = lax.dynamic_slice_in_dim(loadings, bin_at * k_rows, k_rows, 0)
    new_load = own_load * cross / jnp.dot(fac_gram, loadings, precision=lax.Precision.HIGHEST)
    loadings_new = lax.all_gather(new_load, "bin", axis=0, tiled=True)
    return (factors_new, loadings_new)


def solution(mesh):
    placed = (P("bin", "gene"), P("bin", None), P(None, "gene"), P("bin"), P("bin", None))
    return jax.shard_map(
        on_device,
        mesh=mesh,
        in_specs=placed,
        out_specs=(P("bin", None), P(None, "gene")),
        check_vma=False,
    )
```

```python
import functools

import jax
import jax.numpy as jnp
from jax import lax
from jax.experimental import pallas as pl
from jax.experimental.pallas import tpu as pltpu
from jax.sharding import PartitionSpec as P

K = 256
G = 18432


def passed_along(block, axis, distance):
    devices = range(lax.axis_size(axis))
    route = [(i - distance, i) for i in devices if i - distance in devices]
    return lax.ppermute(block, axis, route)


def neighbour_sum(values, from_above, from_below):
    upper = jnp.concatenate([from_above[None], values[:-1]], 0)
    lower = jnp.concatenate([values[1:], from_below[None]], 0)
    beside = jnp.pad(values[:, 1:], ((0, 0), (0, 1), (0, 0))) + jnp.pad(
        values[:, :-1], ((0, 0), (1, 0), (0, 0))
    )
    return beside + 0.5 * (lower + upper)


def neighbour_first(values, from_above, from_below):
    upper = jnp.concatenate([from_above[:, None], values[:, :-1]], 1)
    lower = jnp.concatenate([values[:, 1:], from_below[:, None]], 1)
    beside = jnp.pad(values[:, :, 1:], ((0, 0), (0, 0), (0, 1))) + jnp.pad(
        values[:, :, :-1], ((0, 0), (0, 0), (1, 0))
    )
    return beside + 0.5 * (lower + upper)


def gray(value):
    return value + (value // 2) * (1 - 2 * (value % 2))


def gene_at_place(place, count):
    wide = 1 - ((place + count - 1) % count) // (count // 2)
    row = wide * (place - 1) + (1 - wide) * ((count - place) % count)
    return 2 * row + wide


def gene_place(index, count):
    row, wide = index // 2, index % 2
    return wide * (1 + row) + (1 - wide) * ((count - row) % count)


def bin_at_place(place, count):
    plane, step = place // 4, place % 4
    turned = step + (plane % 2) * (3 - 2 * step)
    return plane * 4 + gray(turned)


def bin_place(index, count):
    plane = index // 4
    turned = gray(index % 4)
    return plane * 4 + turned + (plane % 2) * (3 - 2 * turned)


RINGS = {"gene": (gene_at_place, gene_place), "bin": (bin_at_place, bin_place)}


def ring_peers(axis, count):
    at_place, place_of = RINGS[axis]
    place = place_of(lax.axis_index(axis), count)
    return place, (lambda shift: at_place((place + shift + count) % count, count))


def enter(axis, peers):
    barrier = pltpu.get_barrier_semaphore()
    for peer in peers:
        pl.semaphore_signal(barrier, inc=1, device_id={axis: peer},
                            device_id_type=pl.DeviceIdType.MESH)
    pl.semaphore_wait(barrier, len(peers))


def gather_kernel(axis, count, x_ref, out_ref, send_sem, recv_sem):
    place, member = ring_peers(axis, count)
    ahead, behind = member(1), member(-1)
    half = x_ref.shape[0] // 2
    enter(axis, (ahead, behind))
    out_ref[member(0)] = x_ref[...]

    def copy(step, way):
        rows = pl.ds(way * half, half)
        origin = member(-step) if way == 0 else member(step)
        src = x_ref.at[rows] if step == 0 else out_ref.at[origin, rows]
        return pltpu.make_async_remote_copy(
            src_ref=src,
            dst_ref=out_ref.at[origin, rows],
            send_sem=send_sem.at[way, step],
            recv_sem=recv_sem.at[way, step],
            device_id={axis: ahead if way == 0 else behind},
            device_id_type=pl.DeviceIdType.MESH,
        )

    for step in range(count - 1):
        for way in (0, 1):
            if step >= 1:
                copy(step - 1, way).wait_recv()
            copy(step, way).start()
    for way in (0, 1):
        copy(count - 2, way).wait_recv()
    for step in range(count - 1):
        for way in (0, 1):
            copy(step, way).wait_send()


def ring_gather(x, axis, collective_id):
    count = lax.axis_size(axis)
    return pl.pallas_call(
        functools.partial(gather_kernel, axis, count),
        out_shape=jax.ShapeDtypeStruct((count,) + x.shape, x.dtype),
        in_specs=[pl.BlockSpec(memory_space=pltpu.VMEM)],
        out_specs=pl.BlockSpec(memory_space=pltpu.VMEM),
        scratch_shapes=[
            pltpu.SemaphoreType.DMA((2, count - 1)),
            pltpu.SemaphoreType.DMA((2, count - 1)),
        ],
        compiler_params=pltpu.CompilerParams(
            collective_id=collective_id, has_side_effects=True
        ),
    )(x)


def scatter_kernel(axis, count, x_ref, out_ref, got, sent, send_sem, recv_sem):
    place, member = ring_peers(axis, count)
    ahead, behind = member(1), member(-1)
    half = x_ref.shape[2] // 2
    enter(axis, (ahead, behind))

    def copy(step, way):
        lanes = pl.ds(way * half, half)
        if step == 0:
            source = x_ref.at[member(-1) if way == 0 else member(1), :, lanes]
        else:
            source = sent.at[way, step]
        return pltpu.make_async_remote_copy(
            src_ref=source,
            dst_ref=got.at[way, step],
            send_sem=send_sem.at[way, step],
            recv_sem=recv_sem.at[way, step],
            device_id={axis: ahead if way == 0 else behind},
            device_id_type=pl.DeviceIdType.MESH,
        )

    for step in range(count - 1):
        for way in (0, 1):
            if step >= 1:
                lanes = pl.ds(way * half, half)
                owner = member(-step - 1) if way == 0 else member(step + 1)
                copy(step - 1, way).wait_recv()
                sent[way, step] = got[way, step - 1] + x_ref[owner, :, lanes]
            copy(step, way).start()
    for way in (0, 1):
        lanes = pl.ds(way * half, half)
        copy(count - 2, way).wait_recv()
        out_ref[:, lanes] = got[way, count - 2] + x_ref[member(0), :, lanes]
    for step in range(count - 1):
        for way in (0, 1):
            copy(step, way).wait_send()


def ring_scatter(x, axis, collective_id):
    count, rows, lanes = x.shape
    return pl.pallas_call(
        functools.partial(scatter_kernel, axis, count),
        out_shape=jax.ShapeDtypeStruct((rows, lanes), x.dtype),
        in_specs=[pl.BlockSpec(memory_space=pltpu.VMEM)],
        out_specs=pl.BlockSpec(memory_space=pltpu.VMEM),
        scratch_shapes=[
            pltpu.VMEM((2, count - 1, rows, lanes // 2), x.dtype),
            pltpu.VMEM((2, count - 1, rows, lanes // 2), x.dtype),
            pltpu.SemaphoreType.DMA((2, count - 1)),
            pltpu.SemaphoreType.DMA((2, count - 1)),
        ],
        compiler_params=pltpu.CompilerParams(
            collective_id=collective_id, has_side_effects=True
        ),
    )(x)


def greet_all(axis, me, count):
    barrier = pltpu.get_barrier_semaphore()
    for shift in range(1, count):
        pl.semaphore_signal(barrier, inc=1, device_id={axis: (me + shift) % count},
                            device_id_type=pl.DeviceIdType.MESH)
    pl.semaphore_wait(barrier, count - 1)


def exchange_kernel(axis, count, summed, x_ref, out_ref, *rest):
    if summed:
        got, send_sem, recv_sem = rest
    else:
        got, (send_sem, recv_sem) = out_ref, rest
    me = lax.axis_index(axis)
    greet_all(axis, me, count)

    def copy(shift):
        target = (me + shift) % count
        return pltpu.make_async_remote_copy(
            src_ref=x_ref.at[target] if summed else x_ref,
            dst_ref=got.at[me],
            send_sem=send_sem.at[shift],
            recv_sem=recv_sem.at[me],
            device_id={axis: target},
            device_id_type=pl.DeviceIdType.MESH,
        )

    def arrival(shift):
        origin = (me + count - shift) % count
        return pltpu.make_async_remote_copy(
            src_ref=x_ref.at[origin] if summed else x_ref,
            dst_ref=got.at[origin],
            send_sem=send_sem.at[shift],
            recv_sem=recv_sem.at[origin],
            device_id={axis: origin},
            device_id_type=pl.DeviceIdType.MESH,
        )

    for shift in range(1, count):
        copy(shift).start()
    if summed:
        total = x_ref[me]
        for shift in range(1, count):
            arrival(shift).wait_recv()
            total = total + got[(me + count - shift) % count]
        out_ref[...] = total
    else:
        out_ref[me] = x_ref[...]
        for shift in range(1, count):
            arrival(shift).wait_recv()
    for shift in range(1, count):
        copy(shift).wait_send()


def exchange(x, axis, collective_id, summed):
    count = lax.axis_size(axis)
    if summed:
        out_shape = x.shape[1:]
        scratch = [pltpu.VMEM(x.shape, x.dtype)]
    else:
        out_shape = (count,) + x.shape
        scratch = []
    return pl.pallas_call(
        functools.partial(exchange_kernel, axis, count, summed),
        out_shape=jax.ShapeDtypeStruct(out_shape, x.dtype),
        in_specs=[pl.BlockSpec(memory_space=pltpu.VMEM)],
        out_specs=pl.BlockSpec(memory_space=pltpu.VMEM),
        scratch_shapes=scratch + [
            pltpu.SemaphoreType.DMA((count,)),
            pltpu.SemaphoreType.DMA((count,)),
        ],
        compiler_params=pltpu.CompilerParams(
            collective_id=collective_id, has_side_effects=True
        ),
    )(x)


def split_three(values):
    high = lax.reduce_precision(values, exponent_bits=8, mantissa_bits=7)
    rest = values - high
    mid = lax.reduce_precision(rest, exponent_bits=8, mantissa_bits=7)
    low = rest - mid
    return jnp.concatenate([high, mid, low], 1).astype(jnp.bfloat16)


def join_three(parts, width):
    return (parts[:, :width] + parts[:, width : 2 * width]) + parts[:, 2 * width :]


def stencil_term(own, position, edge_codes):
    bin_count = lax.axis_size("bin")
    row_count, width = own.shape
    group_size = row_count // bin_count
    grid_rows, grid_cols = edge_codes.shape
    payload = jnp.concatenate([own, position.astype(jnp.float32)[:, None]], 1)
    got = lax.all_to_all(
        payload.reshape(bin_count, group_size * (width + 1)), "bin", 0, 0, tiled=True
    ).reshape(row_count, width + 1)
    tile_slot = got[:, width].astype(jnp.int32) - lax.axis_index("bin") * row_count
    cells = lax.broadcasted_iota(jnp.int32, (row_count, row_count), 1)
    onehot = (tile_slot[:, None] == cells).astype(jnp.bfloat16)
    placed = lax.dot_general(
        onehot, split_three(got[:, :width]), (((0,), (0,)), ((), ())),
        preferred_element_type=jnp.float32,
    )
    tile_rows = join_three(placed, width)
    cell_scale = edge_codes.astype(jnp.float32) / 8.0
    weighted = cell_scale[:, :, None] * tile_rows.reshape(grid_rows, grid_cols, width)
    rim_last, rim_first = (weighted[-1], weighted[0])
    upper_rows, upper_scale = passed_along((rim_last, cell_scale[-1]), "bin", 1)
    lower_rows, lower_scale = passed_along((rim_first, cell_scale[0]), "bin", -1)
    degree_grid = (
        cell_scale * neighbour_first(cell_scale[None], upper_scale[None], lower_scale[None])[0]
    )
    smooth_grid = cell_scale[:, :, None] * neighbour_sum(weighted, upper_rows, lower_rows)
    back = jnp.concatenate(
        [smooth_grid.reshape(row_count, width), degree_grid.reshape(row_count, 1)], 1
    )
    back_rows = join_three(
        jnp.dot(onehot, split_three(back), preferred_element_type=jnp.float32), width + 1
    )
    ret = lax.all_to_all(
        back_rows.reshape(bin_count, group_size * (width + 1)), "bin", 0, 0, tiled=True
    ).reshape(row_count, width + 1)
    return (ret[:, :width], ret[:, width])


def on_device(counts, factors, loadings, position, edge_codes):
    bin_count = lax.axis_size("bin")
    gene_count = lax.axis_size("gene")
    row_count, width_all = factors.shape
    width = width_all // gene_count
    k_rows = width_all // bin_count
    gene_at = lax.axis_index("gene")
    bin_at = lax.axis_index("bin")
    load_bf = loadings.astype(jnp.bfloat16)
    right_dims = (((1,), (1,)), ((), ()))
    numer_part = lax.dot_general(load_bf, counts, right_dims, preferred_element_type=jnp.float32)
    gram_part = lax.dot_general(load_bf, load_bf, right_dims, preferred_element_type=jnp.float32)
    both = jnp.concatenate([numer_part, gram_part], 1)
    both = lax.psum_scatter(
        both.reshape(gene_count, width, -1), "gene", scatter_dimension=0, tiled=True
    ).reshape(width, -1)
    numer_t, gram_rows = both[:, :row_count], both[:, row_count:]
    own = lax.dynamic_slice_in_dim(factors, gene_at * width, width, 1)
    smooth, degree = stencil_term(own, position, edge_codes)
    penalty = float(G * K) / 64.0
    own_t = own.T
    denom_t = (
        lax.dot_general(gram_rows, factors, right_dims, precision=lax.Precision.HIGHEST)
        + penalty * degree[None, :] * own_t
    )
    new_t = own_t * (numer_t + penalty * smooth.T) / denom_t
    factors_t = ring_gather(new_t, "gene", 0).reshape(width_all, row_count)
    factors_new = factors_t.T
    fac_bf_t = factors_t.astype(jnp.bfloat16)
    cross_part = jnp.dot(fac_bf_t, counts, preferred_element_type=jnp.float32)
    fgram_part = lax.dot_general(fac_bf_t, fac_bf_t, right_dims, preferred_element_type=jnp.float32)
    both_bin = jnp.concatenate([cross_part, fgram_part], 1)
    both_bin = exchange(both_bin.reshape(bin_count, k_rows, -1), "bin", 2, True)
    cross, fac_gram = both_bin[:, : cross_part.shape[1]], both_bin[:, cross_part.shape[1] :]
    own_load = lax.dynamic_slice_in_dim(loadings, bin_at * k_rows, k_rows, 0)
    new_load = own_load * cross / jnp.dot(fac_gram, loadings, precision=lax.Precision.HIGHEST)
    loadings_new = exchange(new_load, "bin", 3, False).reshape(width_all, -1)
    return (factors_new, loadings_new)


def solution(mesh):
    placed = (P("bin", "gene"), P("bin", None), P(None, "gene"), P("bin"), P("bin", None))
    return jax.shard_map(
        on_device,
        mesh=mesh,
        in_specs=placed,
        out_specs=(P("bin", None), P(None, "gene")),
        check_vma=False,
    )
```

```python
import functools

import jax
import jax.numpy as jnp
from jax import lax
from jax.experimental import pallas as pl
from jax.experimental.pallas import tpu as pltpu
from jax.sharding import PartitionSpec as P

K = 256
G = 18432


def passed_along(block, axis, distance):
    devices = range(lax.axis_size(axis))
    route = [(i - distance, i) for i in devices if i - distance in devices]
    return lax.ppermute(block, axis, route)


def neighbour_sum(values, from_above, from_below):
    upper = jnp.concatenate([from_above[None], values[:-1]], 0)
    lower = jnp.concatenate([values[1:], from_below[None]], 0)
    beside = jnp.pad(values[:, 1:], ((0, 0), (0, 1), (0, 0))) + jnp.pad(
        values[:, :-1], ((0, 0), (1, 0), (0, 0))
    )
    return beside + 0.5 * (lower + upper)


def neighbour_first(values, from_above, from_below):
    upper = jnp.concatenate([from_above[:, None], values[:, :-1]], 1)
    lower = jnp.concatenate([values[:, 1:], from_below[:, None]], 1)
    beside = jnp.pad(values[:, :, 1:], ((0, 0), (0, 0), (0, 1))) + jnp.pad(
        values[:, :, :-1], ((0, 0), (0, 0), (1, 0))
    )
    return beside + 0.5 * (lower + upper)


def gray(value):
    return value + (value // 2) * (1 - 2 * (value % 2))


def gene_at_place(place, count):
    wide = 1 - ((place + count - 1) % count) // (count // 2)
    row = wide * (place - 1) + (1 - wide) * ((count - place) % count)
    return 2 * row + wide


def gene_place(index, count):
    row, wide = index // 2, index % 2
    return wide * (1 + row) + (1 - wide) * ((count - row) % count)


def bin_at_place(place, count):
    plane, step = place // 4, place % 4
    turned = step + (plane % 2) * (3 - 2 * step)
    return plane * 4 + gray(turned)


def bin_place(index, count):
    plane = index // 4
    turned = gray(index % 4)
    return plane * 4 + turned + (plane % 2) * (3 - 2 * turned)


RINGS = {"gene": (gene_at_place, gene_place), "bin": (bin_at_place, bin_place)}


def ring_peers(axis, count):
    at_place, place_of = RINGS[axis]
    place = place_of(lax.axis_index(axis), count)
    return place, (lambda shift: at_place((place + shift + count) % count, count))


def enter(axis, peers):
    barrier = pltpu.get_barrier_semaphore()
    for peer in peers:
        pl.semaphore_signal(barrier, inc=1, device_id={axis: peer},
                            device_id_type=pl.DeviceIdType.MESH)
    pl.semaphore_wait(barrier, len(peers))


def gather_kernel(axis, count, x_ref, out_ref, send_sem, recv_sem):
    place, member = ring_peers(axis, count)
    ahead, behind = member(1), member(-1)
    half = x_ref.shape[0] // 2
    enter(axis, (ahead, behind))
    out_ref[member(0)] = x_ref[...]

    def copy(step, way):
        rows = pl.ds(way * half, half)
        origin = member(-step) if way == 0 else member(step)
        src = x_ref.at[rows] if step == 0 else out_ref.at[origin, rows]
        return pltpu.make_async_remote_copy(
            src_ref=src,
            dst_ref=out_ref.at[origin, rows],
            send_sem=send_sem.at[way, step],
            recv_sem=recv_sem.at[way, step],
            device_id={axis: ahead if way == 0 else behind},
            device_id_type=pl.DeviceIdType.MESH,
        )

    for step in range(count - 1):
        for way in (0, 1):
            if step >= 1:
                copy(step - 1, way).wait_recv()
            copy(step, way).start()
    for way in (0, 1):
        copy(count - 2, way).wait_recv()
    for step in range(count - 1):
        for way in (0, 1):
            copy(step, way).wait_send()


def ring_gather(x, axis, collective_id):
    count = lax.axis_size(axis)
    return pl.pallas_call(
        functools.partial(gather_kernel, axis, count),
        out_shape=jax.ShapeDtypeStruct((count,) + x.shape, x.dtype),
        in_specs=[pl.BlockSpec(memory_space=pltpu.VMEM)],
        out_specs=pl.BlockSpec(memory_space=pltpu.VMEM),
        scratch_shapes=[
            pltpu.SemaphoreType.DMA((2, count - 1)),
            pltpu.SemaphoreType.DMA((2, count - 1)),
        ],
        compiler_params=pltpu.CompilerParams(
            collective_id=collective_id, has_side_effects=True
        ),
    )(x)


def scatter_kernel(axis, count, x_ref, out_ref, got, sent, send_sem, recv_sem):
    place, member = ring_peers(axis, count)
    ahead, behind = member(1), member(-1)
    half = x_ref.shape[2] // 2
    enter(axis, (ahead, behind))

    def copy(step, way):
        lanes = pl.ds(way * half, half)
        if step == 0:
            source = x_ref.at[member(-1) if way == 0 else member(1), :, lanes]
        else:
            source = sent.at[way, step]
        return pltpu.make_async_remote_copy(
            src_ref=source,
            dst_ref=got.at[way, step],
            send_sem=send_sem.at[way, step],
            recv_sem=recv_sem.at[way, step],
            device_id={axis: ahead if way == 0 else behind},
            device_id_type=pl.DeviceIdType.MESH,
        )

    for step in range(count - 1):
        for way in (0, 1):
            if step >= 1:
                lanes = pl.ds(way * half, half)
                owner = member(-step - 1) if way == 0 else member(step + 1)
                copy(step - 1, way).wait_recv()
                sent[way, step] = got[way, step - 1] + x_ref[owner, :, lanes]
            copy(step, way).start()
    for way in (0, 1):
        lanes = pl.ds(way * half, half)
        copy(count - 2, way).wait_recv()
        out_ref[:, lanes] = got[way, count - 2] + x_ref[member(0), :, lanes]
    for step in range(count - 1):
        for way in (0, 1):
            copy(step, way).wait_send()


def ring_scatter(x, axis, collective_id):
    count, rows, lanes = x.shape
    return pl.pallas_call(
        functools.partial(scatter_kernel, axis, count),
        out_shape=jax.ShapeDtypeStruct((rows, lanes), x.dtype),
        in_specs=[pl.BlockSpec(memory_space=pltpu.VMEM)],
        out_specs=pl.BlockSpec(memory_space=pltpu.VMEM),
        scratch_shapes=[
            pltpu.VMEM((2, count - 1, rows, lanes // 2), x.dtype),
            pltpu.VMEM((2, count - 1, rows, lanes // 2), x.dtype),
            pltpu.SemaphoreType.DMA((2, count - 1)),
            pltpu.SemaphoreType.DMA((2, count - 1)),
        ],
        compiler_params=pltpu.CompilerParams(
            collective_id=collective_id, has_side_effects=True
        ),
    )(x)


def greet_all(axis, me, count):
    barrier = pltpu.get_barrier_semaphore()
    for shift in range(1, count):
        pl.semaphore_signal(barrier, inc=1, device_id={axis: (me + shift) % count},
                            device_id_type=pl.DeviceIdType.MESH)
    pl.semaphore_wait(barrier, count - 1)


def exchange_kernel(axis, count, summed, x_ref, out_ref, *rest):
    if summed:
        got, send_sem, recv_sem = rest
    else:
        got, (send_sem, recv_sem) = out_ref, rest
    me = lax.axis_index(axis)
    greet_all(axis, me, count)

    def copy(shift):
        target = (me + shift) % count
        return pltpu.make_async_remote_copy(
            src_ref=x_ref.at[target] if summed else x_ref,
            dst_ref=got.at[me],
            send_sem=send_sem.at[shift],
            recv_sem=recv_sem.at[me],
            device_id={axis: target},
            device_id_type=pl.DeviceIdType.MESH,
        )

    def arrival(shift):
        origin = (me + count - shift) % count
        return pltpu.make_async_remote_copy(
            src_ref=x_ref.at[origin] if summed else x_ref,
            dst_ref=got.at[origin],
            send_sem=send_sem.at[shift],
            recv_sem=recv_sem.at[origin],
            device_id={axis: origin},
            device_id_type=pl.DeviceIdType.MESH,
        )

    for shift in range(1, count):
        copy(shift).start()
    if summed:
        total = x_ref[me]
        for shift in range(1, count):
            arrival(shift).wait_recv()
            total = total + got[(me + count - shift) % count]
        out_ref[...] = total
    else:
        out_ref[me] = x_ref[...]
        for shift in range(1, count):
            arrival(shift).wait_recv()
    for shift in range(1, count):
        copy(shift).wait_send()


def exchange(x, axis, collective_id, summed):
    count = lax.axis_size(axis)
    if summed:
        out_shape = x.shape[1:]
        scratch = [pltpu.VMEM(x.shape, x.dtype)]
    else:
        out_shape = (count,) + x.shape
        scratch = []
    return pl.pallas_call(
        functools.partial(exchange_kernel, axis, count, summed),
        out_shape=jax.ShapeDtypeStruct(out_shape, x.dtype),
        in_specs=[pl.BlockSpec(memory_space=pltpu.VMEM)],
        out_specs=pl.BlockSpec(memory_space=pltpu.VMEM),
        scratch_shapes=scratch + [
            pltpu.SemaphoreType.DMA((count,)),
            pltpu.SemaphoreType.DMA((count,)),
        ],
        compiler_params=pltpu.CompilerParams(
            collective_id=collective_id, has_side_effects=True
        ),
    )(x)


def split_three(values):
    high = lax.reduce_precision(values, exponent_bits=8, mantissa_bits=7)
    rest = values - high
    mid = lax.reduce_precision(rest, exponent_bits=8, mantissa_bits=7)
    low = rest - mid
    return jnp.concatenate([high, mid, low], 1).astype(jnp.bfloat16)


def join_three(parts, width):
    return (parts[:, :width] + parts[:, width : 2 * width]) + parts[:, 2 * width :]


def stencil_term(own, position, edge_codes):
    bin_count = lax.axis_size("bin")
    row_count, width = own.shape
    group_size = row_count // bin_count
    grid_rows, grid_cols = edge_codes.shape
    payload = jnp.concatenate([own, position.astype(jnp.float32)[:, None]], 1)
    got = lax.all_to_all(
        payload.reshape(bin_count, group_size * (width + 1)), "bin", 0, 0, tiled=True
    ).reshape(row_count, width + 1)
    tile_slot = got[:, width].astype(jnp.int32) - lax.axis_index("bin") * row_count
    cells = lax.broadcasted_iota(jnp.int32, (row_count, row_count), 1)
    onehot = (tile_slot[:, None] == cells).astype(jnp.bfloat16)
    placed = lax.dot_general(
        onehot, split_three(got[:, :width]), (((0,), (0,)), ((), ())),
        preferred_element_type=jnp.float32,
    )
    tile_rows = join_three(placed, width)
    cell_scale = edge_codes.astype(jnp.float32) / 8.0
    weighted = cell_scale[:, :, None] * tile_rows.reshape(grid_rows, grid_cols, width)
    rim_last, rim_first = (weighted[-1], weighted[0])
    upper_rows, upper_scale = passed_along((rim_last, cell_scale[-1]), "bin", 1)
    lower_rows, lower_scale = passed_along((rim_first, cell_scale[0]), "bin", -1)
    degree_grid = (
        cell_scale * neighbour_first(cell_scale[None], upper_scale[None], lower_scale[None])[0]
    )
    smooth_grid = cell_scale[:, :, None] * neighbour_sum(weighted, upper_rows, lower_rows)
    back = jnp.concatenate(
        [smooth_grid.reshape(row_count, width), degree_grid.reshape(row_count, 1)], 1
    )
    back_rows = join_three(
        jnp.dot(onehot, split_three(back), preferred_element_type=jnp.float32), width + 1
    )
    ret = lax.all_to_all(
        back_rows.reshape(bin_count, group_size * (width + 1)), "bin", 0, 0, tiled=True
    ).reshape(row_count, width + 1)
    return (ret[:, :width], ret[:, width])


def on_device(counts, factors, loadings, position, edge_codes):
    bin_count = lax.axis_size("bin")
    gene_count = lax.axis_size("gene")
    row_count, width_all = factors.shape
    width = width_all // gene_count
    k_rows = width_all // bin_count
    gene_at = lax.axis_index("gene")
    bin_at = lax.axis_index("bin")
    load_bf = loadings.astype(jnp.bfloat16)
    right_dims = (((1,), (1,)), ((), ()))
    numer_part = lax.dot_general(load_bf, counts, right_dims, preferred_element_type=jnp.float32)
    gram_part = lax.dot_general(load_bf, load_bf, right_dims, preferred_element_type=jnp.float32)
    both = jnp.concatenate([numer_part, gram_part], 1)
    both = lax.psum_scatter(
        both.reshape(gene_count, width, -1), "gene", scatter_dimension=0, tiled=True
    ).reshape(width, -1)
    numer_t, gram_rows = both[:, :row_count], both[:, row_count:]
    own = lax.dynamic_slice_in_dim(factors, gene_at * width, width, 1)
    smooth, degree = stencil_term(own, position, edge_codes)
    penalty = float(G * K) / 64.0
    own_t = own.T
    denom_t = (
        lax.dot_general(gram_rows, factors, right_dims, precision=lax.Precision.HIGHEST)
        + penalty * degree[None, :] * own_t
    )
    new_t = own_t * (numer_t + penalty * smooth.T) / denom_t
    factors_t = exchange(new_t, "gene", 0, False).reshape(width_all, row_count)
    factors_new = factors_t.T
    fac_bf_t = factors_t.astype(jnp.bfloat16)
    cross_part = jnp.dot(fac_bf_t, counts, preferred_element_type=jnp.float32)
    fgram_part = lax.dot_general(fac_bf_t, fac_bf_t, right_dims, preferred_element_type=jnp.float32)
    both_bin = jnp.concatenate([cross_part, fgram_part], 1)
    both_bin = exchange(both_bin.reshape(bin_count, k_rows, -1), "bin", 2, True)
    cross, fac_gram = both_bin[:, : cross_part.shape[1]], both_bin[:, cross_part.shape[1] :]
    own_load = lax.dynamic_slice_in_dim(loadings, bin_at * k_rows, k_rows, 0)
    new_load = own_load * cross / jnp.dot(fac_gram, loadings, precision=lax.Precision.HIGHEST)
    loadings_new = exchange(new_load, "bin", 3, False).reshape(width_all, -1)
    return (factors_new, loadings_new)


def solution(mesh):
    placed = (P("bin", "gene"), P("bin", None), P(None, "gene"), P("bin"), P("bin", None))
    return jax.shard_map(
        on_device,
        mesh=mesh,
        in_specs=placed,
        out_specs=(P("bin", None), P(None, "gene")),
        check_vma=False,
    )
```

```python
import functools

import jax
import jax.numpy as jnp
from jax import lax
from jax.experimental import pallas as pl
from jax.experimental.pallas import tpu as pltpu
from jax.sharding import PartitionSpec as P

K = 256
G = 18432


def passed_along(block, axis, distance):
    devices = range(lax.axis_size(axis))
    route = [(i - distance, i) for i in devices if i - distance in devices]
    return lax.ppermute(block, axis, route)


def neighbour_sum(values, from_above, from_below):
    upper = jnp.concatenate([from_above[None], values[:-1]], 0)
    lower = jnp.concatenate([values[1:], from_below[None]], 0)
    beside = jnp.pad(values[:, 1:], ((0, 0), (0, 1), (0, 0))) + jnp.pad(
        values[:, :-1], ((0, 0), (1, 0), (0, 0))
    )
    return beside + 0.5 * (lower + upper)


def neighbour_first(values, from_above, from_below):
    upper = jnp.concatenate([from_above[:, None], values[:, :-1]], 1)
    lower = jnp.concatenate([values[:, 1:], from_below[:, None]], 1)
    beside = jnp.pad(values[:, :, 1:], ((0, 0), (0, 0), (0, 1))) + jnp.pad(
        values[:, :, :-1], ((0, 0), (0, 0), (1, 0))
    )
    return beside + 0.5 * (lower + upper)


def gray(value):
    return value + (value // 2) * (1 - 2 * (value % 2))


def gene_at_place(place, count):
    wide = 1 - ((place + count - 1) % count) // (count // 2)
    row = wide * (place - 1) + (1 - wide) * ((count - place) % count)
    return 2 * row + wide


def gene_place(index, count):
    row, wide = index // 2, index % 2
    return wide * (1 + row) + (1 - wide) * ((count - row) % count)


def bin_at_place(place, count):
    plane, step = place // 4, place % 4
    turned = step + (plane % 2) * (3 - 2 * step)
    return plane * 4 + gray(turned)


def bin_place(index, count):
    plane = index // 4
    turned = gray(index % 4)
    return plane * 4 + turned + (plane % 2) * (3 - 2 * turned)


RINGS = {"gene": (gene_at_place, gene_place), "bin": (bin_at_place, bin_place)}


def ring_peers(axis, count):
    at_place, place_of = RINGS[axis]
    place = place_of(lax.axis_index(axis), count)
    return place, (lambda shift: at_place((place + shift + count) % count, count))


def enter(axis, peers):
    barrier = pltpu.get_barrier_semaphore()
    for peer in peers:
        pl.semaphore_signal(barrier, inc=1, device_id={axis: peer},
                            device_id_type=pl.DeviceIdType.MESH)
    pl.semaphore_wait(barrier, len(peers))


def gather_kernel(axis, count, x_ref, out_ref, send_sem, recv_sem):
    place, member = ring_peers(axis, count)
    ahead, behind = member(1), member(-1)
    half = x_ref.shape[0] // 2
    enter(axis, (ahead, behind))
    out_ref[member(0)] = x_ref[...]

    def copy(step, way):
        rows = pl.ds(way * half, half)
        origin = member(-step) if way == 0 else member(step)
        src = x_ref.at[rows] if step == 0 else out_ref.at[origin, rows]
        return pltpu.make_async_remote_copy(
            src_ref=src,
            dst_ref=out_ref.at[origin, rows],
            send_sem=send_sem.at[way, step],
            recv_sem=recv_sem.at[way, step],
            device_id={axis: ahead if way == 0 else behind},
            device_id_type=pl.DeviceIdType.MESH,
        )

    for step in range(count - 1):
        for way in (0, 1):
            if step >= 1:
                copy(step - 1, way).wait_recv()
            copy(step, way).start()
    for way in (0, 1):
        copy(count - 2, way).wait_recv()
    for step in range(count - 1):
        for way in (0, 1):
            copy(step, way).wait_send()


def ring_gather(x, axis, collective_id):
    count = lax.axis_size(axis)
    return pl.pallas_call(
        functools.partial(gather_kernel, axis, count),
        out_shape=jax.ShapeDtypeStruct((count,) + x.shape, x.dtype),
        in_specs=[pl.BlockSpec(memory_space=pltpu.VMEM)],
        out_specs=pl.BlockSpec(memory_space=pltpu.VMEM),
        scratch_shapes=[
            pltpu.SemaphoreType.DMA((2, count - 1)),
            pltpu.SemaphoreType.DMA((2, count - 1)),
        ],
        compiler_params=pltpu.CompilerParams(
            collective_id=collective_id, has_side_effects=True
        ),
    )(x)


def scatter_kernel(axis, count, x_ref, out_ref, got, sent, send_sem, recv_sem):
    place, member = ring_peers(axis, count)
    ahead, behind = member(1), member(-1)
    half = x_ref.shape[2] // 2
    enter(axis, (ahead, behind))

    def copy(step, way):
        lanes = pl.ds(way * half, half)
        if step == 0:
            source = x_ref.at[member(-1) if way == 0 else member(1), :, lanes]
        else:
            source = sent.at[way, step]
        return pltpu.make_async_remote_copy(
            src_ref=source,
            dst_ref=got.at[way, step],
            send_sem=send_sem.at[way, step],
            recv_sem=recv_sem.at[way, step],
            device_id={axis: ahead if way == 0 else behind},
            device_id_type=pl.DeviceIdType.MESH,
        )

    for step in range(count - 1):
        for way in (0, 1):
            if step >= 1:
                lanes = pl.ds(way * half, half)
                owner = member(-step - 1) if way == 0 else member(step + 1)
                copy(step - 1, way).wait_recv()
                sent[way, step] = got[way, step - 1] + x_ref[owner, :, lanes]
            copy(step, way).start()
    for way in (0, 1):
        lanes = pl.ds(way * half, half)
        copy(count - 2, way).wait_recv()
        out_ref[:, lanes] = got[way, count - 2] + x_ref[member(0), :, lanes]
    for step in range(count - 1):
        for way in (0, 1):
            copy(step, way).wait_send()


def ring_scatter(x, axis, collective_id):
    count, rows, lanes = x.shape
    return pl.pallas_call(
        functools.partial(scatter_kernel, axis, count),
        out_shape=jax.ShapeDtypeStruct((rows, lanes), x.dtype),
        in_specs=[pl.BlockSpec(memory_space=pltpu.VMEM)],
        out_specs=pl.BlockSpec(memory_space=pltpu.VMEM),
        scratch_shapes=[
            pltpu.VMEM((2, count - 1, rows, lanes // 2), x.dtype),
            pltpu.VMEM((2, count - 1, rows, lanes // 2), x.dtype),
            pltpu.SemaphoreType.DMA((2, count - 1)),
            pltpu.SemaphoreType.DMA((2, count - 1)),
        ],
        compiler_params=pltpu.CompilerParams(
            collective_id=collective_id, has_side_effects=True
        ),
    )(x)


def greet_all(axis, me, count):
    barrier = pltpu.get_barrier_semaphore()
    for shift in range(1, count):
        pl.semaphore_signal(barrier, inc=1, device_id={axis: (me + shift) % count},
                            device_id_type=pl.DeviceIdType.MESH)
    pl.semaphore_wait(barrier, count - 1)


def exchange_kernel(axis, count, mode, x_ref, out_ref, *rest):
    if mode == "sum":
        got, send_sem, recv_sem = rest
    else:
        got, (send_sem, recv_sem) = out_ref, rest
    me = lax.axis_index(axis)
    greet_all(axis, me, count)
    split = mode != "gather"

    def copy(shift):
        target = (me + shift) % count
        return pltpu.make_async_remote_copy(
            src_ref=x_ref.at[target] if split else x_ref,
            dst_ref=got.at[me],
            send_sem=send_sem.at[shift],
            recv_sem=recv_sem.at[me],
            device_id={axis: target},
            device_id_type=pl.DeviceIdType.MESH,
        )

    def arrival(shift):
        origin = (me + count - shift) % count
        return pltpu.make_async_remote_copy(
            src_ref=x_ref.at[origin] if split else x_ref,
            dst_ref=got.at[origin],
            send_sem=send_sem.at[shift],
            recv_sem=recv_sem.at[origin],
            device_id={axis: origin},
            device_id_type=pl.DeviceIdType.MESH,
        )

    for shift in range(1, count):
        copy(shift).start()
    if mode == "sum":
        total = x_ref[me]
        for shift in range(1, count):
            arrival(shift).wait_recv()
            total = total + got[(me + count - shift) % count]
        out_ref[...] = total
    else:
        out_ref[me] = x_ref[me] if split else x_ref[...]
        for shift in range(1, count):
            arrival(shift).wait_recv()
    for shift in range(1, count):
        copy(shift).wait_send()


def exchange(x, axis, collective_id, mode):
    count = lax.axis_size(axis)
    scratch = []
    if mode == "sum":
        out_shape = x.shape[1:]
        scratch = [pltpu.VMEM(x.shape, x.dtype)]
    elif mode == "gather":
        out_shape = (count,) + x.shape
    else:
        out_shape = x.shape
    return pl.pallas_call(
        functools.partial(exchange_kernel, axis, count, mode),
        out_shape=jax.ShapeDtypeStruct(out_shape, x.dtype),
        in_specs=[pl.BlockSpec(memory_space=pltpu.VMEM)],
        out_specs=pl.BlockSpec(memory_space=pltpu.VMEM),
        scratch_shapes=scratch + [
            pltpu.SemaphoreType.DMA((count,)),
            pltpu.SemaphoreType.DMA((count,)),
        ],
        compiler_params=pltpu.CompilerParams(
            collective_id=collective_id, has_side_effects=True
        ),
    )(x)


def swap_rows(rows, collective_id):
    bin_count = lax.axis_size("bin")
    row_count, width = rows.shape
    wide = 48
    padded = jnp.pad(rows, ((0, 0), (0, wide - width)))
    moved = exchange(padded.reshape(bin_count, -1, 128), "bin", collective_id, "swap")
    return moved.reshape(row_count, wide)[:, :width]


def split_three(values):
    high = lax.reduce_precision(values, exponent_bits=8, mantissa_bits=7)
    rest = values - high
    mid = lax.reduce_precision(rest, exponent_bits=8, mantissa_bits=7)
    low = rest - mid
    return jnp.concatenate([high, mid, low], 1).astype(jnp.bfloat16)


def join_three(parts, width):
    return (parts[:, :width] + parts[:, width : 2 * width]) + parts[:, 2 * width :]


def stencil_term(own, position, edge_codes):
    bin_count = lax.axis_size("bin")
    row_count, width = own.shape
    group_size = row_count // bin_count
    grid_rows, grid_cols = edge_codes.shape
    payload = jnp.concatenate([own, position.astype(jnp.float32)[:, None]], 1)
    got = swap_rows(payload, 4)
    tile_slot = got[:, width].astype(jnp.int32) - lax.axis_index("bin") * row_count
    cells = lax.broadcasted_iota(jnp.int32, (row_count, row_count), 1)
    onehot = (tile_slot[:, None] == cells).astype(jnp.bfloat16)
    placed = lax.dot_general(
        onehot, split_three(got[:, :width]), (((0,), (0,)), ((), ())),
        preferred_element_type=jnp.float32,
    )
    tile_rows = join_three(placed, width)
    cell_scale = edge_codes.astype(jnp.float32) / 8.0
    weighted = cell_scale[:, :, None] * tile_rows.reshape(grid_rows, grid_cols, width)
    rim_last, rim_first = (weighted[-1], weighted[0])
    upper_rows, upper_scale = passed_along((rim_last, cell_scale[-1]), "bin", 1)
    lower_rows, lower_scale = passed_along((rim_first, cell_scale[0]), "bin", -1)
    degree_grid = (
        cell_scale * neighbour_first(cell_scale[None], upper_scale[None], lower_scale[None])[0]
    )
    smooth_grid = cell_scale[:, :, None] * neighbour_sum(weighted, upper_rows, lower_rows)
    back = jnp.concatenate(
        [smooth_grid.reshape(row_count, width), degree_grid.reshape(row_count, 1)], 1
    )
    back_rows = join_three(
        jnp.dot(onehot, split_three(back), preferred_element_type=jnp.float32), width + 1
    )
    ret = swap_rows(back_rows, 5)
    return (ret[:, :width], ret[:, width])


def on_device(counts, factors, loadings, position, edge_codes):
    bin_count = lax.axis_size("bin")
    gene_count = lax.axis_size("gene")
    row_count, width_all = factors.shape
    width = width_all // gene_count
    k_rows = width_all // bin_count
    gene_at = lax.axis_index("gene")
    bin_at = lax.axis_index("bin")
    load_bf = loadings.astype(jnp.bfloat16)
    right_dims = (((1,), (1,)), ((), ()))
    numer_part = lax.dot_general(load_bf, counts, right_dims, preferred_element_type=jnp.float32)
    gram_part = lax.dot_general(load_bf, load_bf, right_dims, preferred_element_type=jnp.float32)
    both = jnp.concatenate([numer_part, gram_part], 1)
    both = lax.psum_scatter(
        both.reshape(gene_count, width, -1), "gene", scatter_dimension=0, tiled=True
    ).reshape(width, -1)
    numer_t, gram_rows = both[:, :row_count], both[:, row_count:]
    own = lax.dynamic_slice_in_dim(factors, gene_at * width, width, 1)
    smooth, degree = stencil_term(own, position, edge_codes)
    penalty = float(G * K) / 64.0
    own_t = own.T
    denom_t = (
        lax.dot_general(gram_rows, factors, right_dims, precision=lax.Precision.HIGHEST)
        + penalty * degree[None, :] * own_t
    )
    new_t = own_t * (numer_t + penalty * smooth.T) / denom_t
    factors_t = exchange(new_t, "gene", 0, "gather").reshape(width_all, row_count)
    factors_new = factors_t.T
    fac_bf_t = factors_t.astype(jnp.bfloat16)
    cross_part = jnp.dot(fac_bf_t, counts, preferred_element_type=jnp.float32)
    fgram_part = lax.dot_general(fac_bf_t, fac_bf_t, right_dims, preferred_element_type=jnp.float32)
    both_bin = jnp.concatenate([cross_part, fgram_part], 1)
    both_bin = exchange(both_bin.reshape(bin_count, k_rows, -1), "bin", 2, "sum")
    cross, fac_gram = both_bin[:, : cross_part.shape[1]], both_bin[:, cross_part.shape[1] :]
    own_load = lax.dynamic_slice_in_dim(loadings, bin_at * k_rows, k_rows, 0)
    new_load = own_load * cross / jnp.dot(fac_gram, loadings, precision=lax.Precision.HIGHEST)
    loadings_new = exchange(new_load, "bin", 3, "gather").reshape(width_all, -1)
    return (factors_new, loadings_new)


def solution(mesh):
    placed = (P("bin", "gene"), P("bin", None), P(None, "gene"), P("bin"), P("bin", None))
    return jax.shard_map(
        on_device,
        mesh=mesh,
        in_specs=placed,
        out_specs=(P("bin", None), P(None, "gene")),
        check_vma=False,
    )
```

```python
import functools

import jax
import jax.numpy as jnp
from jax import lax
from jax.experimental import pallas as pl
from jax.experimental.pallas import tpu as pltpu
from jax.sharding import PartitionSpec as P

K = 256
G = 18432


def passed_along(block, axis, distance):
    devices = range(lax.axis_size(axis))
    route = [(i - distance, i) for i in devices if i - distance in devices]
    return lax.ppermute(block, axis, route)


def neighbour_sum(values, from_above, from_below):
    upper = jnp.concatenate([from_above[None], values[:-1]], 0)
    lower = jnp.concatenate([values[1:], from_below[None]], 0)
    beside = jnp.pad(values[:, 1:], ((0, 0), (0, 1), (0, 0))) + jnp.pad(
        values[:, :-1], ((0, 0), (1, 0), (0, 0))
    )
    return beside + 0.5 * (lower + upper)


def neighbour_first(values, from_above, from_below):
    upper = jnp.concatenate([from_above[:, None], values[:, :-1]], 1)
    lower = jnp.concatenate([values[:, 1:], from_below[:, None]], 1)
    beside = jnp.pad(values[:, :, 1:], ((0, 0), (0, 0), (0, 1))) + jnp.pad(
        values[:, :, :-1], ((0, 0), (0, 0), (1, 0))
    )
    return beside + 0.5 * (lower + upper)


def gray(value):
    return value + (value // 2) * (1 - 2 * (value % 2))


def gene_at_place(place, count):
    wide = 1 - ((place + count - 1) % count) // (count // 2)
    row = wide * (place - 1) + (1 - wide) * ((count - place) % count)
    return 2 * row + wide


def gene_place(index, count):
    row, wide = index // 2, index % 2
    return wide * (1 + row) + (1 - wide) * ((count - row) % count)


def bin_at_place(place, count):
    plane, step = place // 4, place % 4
    turned = step + (plane % 2) * (3 - 2 * step)
    return plane * 4 + gray(turned)


def bin_place(index, count):
    plane = index // 4
    turned = gray(index % 4)
    return plane * 4 + turned + (plane % 2) * (3 - 2 * turned)


RINGS = {"gene": (gene_at_place, gene_place), "bin": (bin_at_place, bin_place)}


def ring_peers(axis, count):
    at_place, place_of = RINGS[axis]
    place = place_of(lax.axis_index(axis), count)
    return place, (lambda shift: at_place((place + shift + count) % count, count))


def enter(axis, peers):
    barrier = pltpu.get_barrier_semaphore()
    for peer in peers:
        pl.semaphore_signal(barrier, inc=1, device_id={axis: peer},
                            device_id_type=pl.DeviceIdType.MESH)
    pl.semaphore_wait(barrier, len(peers))


def gather_kernel(axis, count, x_ref, out_ref, send_sem, recv_sem):
    place, member = ring_peers(axis, count)
    ahead, behind = member(1), member(-1)
    half = x_ref.shape[0] // 2
    enter(axis, (ahead, behind))
    out_ref[member(0)] = x_ref[...]

    def copy(step, way):
        rows = pl.ds(way * half, half)
        origin = member(-step) if way == 0 else member(step)
        src = x_ref.at[rows] if step == 0 else out_ref.at[origin, rows]
        return pltpu.make_async_remote_copy(
            src_ref=src,
            dst_ref=out_ref.at[origin, rows],
            send_sem=send_sem.at[way, step],
            recv_sem=recv_sem.at[way, step],
            device_id={axis: ahead if way == 0 else behind},
            device_id_type=pl.DeviceIdType.MESH,
        )

    for step in range(count - 1):
        for way in (0, 1):
            if step >= 1:
                copy(step - 1, way).wait_recv()
            copy(step, way).start()
    for way in (0, 1):
        copy(count - 2, way).wait_recv()
    for step in range(count - 1):
        for way in (0, 1):
            copy(step, way).wait_send()


def ring_gather(x, axis, collective_id):
    count = lax.axis_size(axis)
    return pl.pallas_call(
        functools.partial(gather_kernel, axis, count),
        out_shape=jax.ShapeDtypeStruct((count,) + x.shape, x.dtype),
        in_specs=[pl.BlockSpec(memory_space=pltpu.VMEM)],
        out_specs=pl.BlockSpec(memory_space=pltpu.VMEM),
        scratch_shapes=[
            pltpu.SemaphoreType.DMA((2, count - 1)),
            pltpu.SemaphoreType.DMA((2, count - 1)),
        ],
        compiler_params=pltpu.CompilerParams(
            collective_id=collective_id, has_side_effects=True
        ),
    )(x)


def scatter_kernel(axis, count, x_ref, out_ref, got, sent, send_sem, recv_sem):
    place, member = ring_peers(axis, count)
    ahead, behind = member(1), member(-1)
    half = x_ref.shape[2] // 2
    enter(axis, (ahead, behind))

    def copy(step, way):
        lanes = pl.ds(way * half, half)
        if step == 0:
            source = x_ref.at[member(-1) if way == 0 else member(1), :, lanes]
        else:
            source = sent.at[way, step]
        return pltpu.make_async_remote_copy(
            src_ref=source,
            dst_ref=got.at[way, step],
            send_sem=send_sem.at[way, step],
            recv_sem=recv_sem.at[way, step],
            device_id={axis: ahead if way == 0 else behind},
            device_id_type=pl.DeviceIdType.MESH,
        )

    for step in range(count - 1):
        for way in (0, 1):
            if step >= 1:
                lanes = pl.ds(way * half, half)
                owner = member(-step - 1) if way == 0 else member(step + 1)
                copy(step - 1, way).wait_recv()
                sent[way, step] = got[way, step - 1] + x_ref[owner, :, lanes]
            copy(step, way).start()
    for way in (0, 1):
        lanes = pl.ds(way * half, half)
        copy(count - 2, way).wait_recv()
        out_ref[:, lanes] = got[way, count - 2] + x_ref[member(0), :, lanes]
    for step in range(count - 1):
        for way in (0, 1):
            copy(step, way).wait_send()


def ring_scatter(x, axis, collective_id):
    count, rows, lanes = x.shape
    return pl.pallas_call(
        functools.partial(scatter_kernel, axis, count),
        out_shape=jax.ShapeDtypeStruct((rows, lanes), x.dtype),
        in_specs=[pl.BlockSpec(memory_space=pltpu.VMEM)],
        out_specs=pl.BlockSpec(memory_space=pltpu.VMEM),
        scratch_shapes=[
            pltpu.VMEM((2, count - 1, rows, lanes // 2), x.dtype),
            pltpu.VMEM((2, count - 1, rows, lanes // 2), x.dtype),
            pltpu.SemaphoreType.DMA((2, count - 1)),
            pltpu.SemaphoreType.DMA((2, count - 1)),
        ],
        compiler_params=pltpu.CompilerParams(
            collective_id=collective_id, has_side_effects=True
        ),
    )(x)


def greet_all(axis, me, count):
    barrier = pltpu.get_barrier_semaphore()
    for shift in range(1, count):
        pl.semaphore_signal(barrier, inc=1, device_id={axis: (me + shift) % count},
                            device_id_type=pl.DeviceIdType.MESH)
    pl.semaphore_wait(barrier, count - 1)


def exchange_kernel(axis, count, summed, x_ref, out_ref, *rest):
    if summed:
        got, send_sem, recv_sem = rest
    else:
        got, (send_sem, recv_sem) = out_ref, rest
    me = lax.axis_index(axis)
    greet_all(axis, me, count)

    def copy(shift):
        target = (me + shift) % count
        return pltpu.make_async_remote_copy(
            src_ref=x_ref.at[target] if summed else x_ref,
            dst_ref=got.at[me],
            send_sem=send_sem.at[shift],
            recv_sem=recv_sem.at[me],
            device_id={axis: target},
            device_id_type=pl.DeviceIdType.MESH,
        )

    def arrival(shift):
        origin = (me + count - shift) % count
        return pltpu.make_async_remote_copy(
            src_ref=x_ref.at[origin] if summed else x_ref,
            dst_ref=got.at[origin],
            send_sem=send_sem.at[shift],
            recv_sem=recv_sem.at[origin],
            device_id={axis: origin},
            device_id_type=pl.DeviceIdType.MESH,
        )

    for shift in range(1, count):
        copy(shift).start()
    if summed:
        total = x_ref[me]
        for shift in range(1, count):
            arrival(shift).wait_recv()
            total = total + got[(me + count - shift) % count]
        out_ref[...] = total
    else:
        out_ref[me] = x_ref[...]
        for shift in range(1, count):
            arrival(shift).wait_recv()
    for shift in range(1, count):
        copy(shift).wait_send()


def exchange(x, axis, collective_id, summed):
    count = lax.axis_size(axis)
    if summed:
        out_shape = x.shape[1:]
        scratch = [pltpu.VMEM(x.shape, x.dtype)]
    else:
        out_shape = (count,) + x.shape
        scratch = []
    return pl.pallas_call(
        functools.partial(exchange_kernel, axis, count, summed),
        out_shape=jax.ShapeDtypeStruct(out_shape, x.dtype),
        in_specs=[pl.BlockSpec(memory_space=pltpu.VMEM)],
        out_specs=pl.BlockSpec(memory_space=pltpu.VMEM),
        scratch_shapes=scratch + [
            pltpu.SemaphoreType.DMA((count,)),
            pltpu.SemaphoreType.DMA((count,)),
        ],
        compiler_params=pltpu.CompilerParams(
            collective_id=collective_id, has_side_effects=True
        ),
    )(x)


def loadings_kernel(count, x_ref, own_ref, load_ref, out_ref, got, sem_a, sem_b, sem_c, sem_d):
    me = lax.axis_index("bin")
    greet_all("bin", me, count)

    def partial_copy(shift):
        target = (me + shift) % count
        return pltpu.make_async_remote_copy(
            src_ref=x_ref.at[target],
            dst_ref=got.at[me],
            send_sem=sem_a.at[shift],
            recv_sem=sem_b.at[me],
            device_id={"bin": target},
            device_id_type=pl.DeviceIdType.MESH,
        )

    def partial_arrival(shift):
        origin = (me + count - shift) % count
        return pltpu.make_async_remote_copy(
            src_ref=x_ref.at[origin],
            dst_ref=got.at[origin],
            send_sem=sem_a.at[shift],
            recv_sem=sem_b.at[origin],
            device_id={"bin": origin},
            device_id_type=pl.DeviceIdType.MESH,
        )

    def result_copy(shift):
        target = (me + shift) % count
        return pltpu.make_async_remote_copy(
            src_ref=out_ref.at[me],
            dst_ref=out_ref.at[me],
            send_sem=sem_c.at[shift],
            recv_sem=sem_d.at[me],
            device_id={"bin": target},
            device_id_type=pl.DeviceIdType.MESH,
        )

    def result_arrival(shift):
        origin = (me + count - shift) % count
        return pltpu.make_async_remote_copy(
            src_ref=out_ref.at[origin],
            dst_ref=out_ref.at[origin],
            send_sem=sem_c.at[shift],
            recv_sem=sem_d.at[origin],
            device_id={"bin": origin},
            device_id_type=pl.DeviceIdType.MESH,
        )

    for shift in range(1, count):
        partial_copy(shift).start()
    total = x_ref[me]
    for shift in range(1, count):
        partial_arrival(shift).wait_recv()
        total = total + got[(me + count - shift) % count]
    genes = own_ref.shape[1]
    denom = jnp.dot(
        total[:, genes:], load_ref[...], precision=lax.Precision.HIGHEST,
        preferred_element_type=jnp.float32,
    )
    out_ref[me] = own_ref[...] * total[:, :genes] / denom
    for shift in range(1, count):
        partial_copy(shift).wait_send()
    for shift in range(1, count):
        result_copy(shift).start()
    for shift in range(1, count):
        result_arrival(shift).wait_recv()
    for shift in range(1, count):
        result_copy(shift).wait_send()


def loadings_update(parts, own_load, loadings, collective_id):
    count = lax.axis_size("bin")
    vmem = pl.BlockSpec(memory_space=pltpu.VMEM)
    return pl.pallas_call(
        functools.partial(loadings_kernel, count),
        out_shape=jax.ShapeDtypeStruct((count,) + own_load.shape, own_load.dtype),
        in_specs=[vmem, vmem, vmem],
        out_specs=vmem,
        scratch_shapes=[pltpu.VMEM(parts.shape, parts.dtype)]
        + [pltpu.SemaphoreType.DMA((count,))] * 4,
        compiler_params=pltpu.CompilerParams(
            collective_id=collective_id, has_side_effects=True
        ),
    )(parts, own_load, loadings)


def split_three(values):
    high = lax.reduce_precision(values, exponent_bits=8, mantissa_bits=7)
    rest = values - high
    mid = lax.reduce_precision(rest, exponent_bits=8, mantissa_bits=7)
    low = rest - mid
    return jnp.concatenate([high, mid, low], 1).astype(jnp.bfloat16)


def join_three(parts, width):
    return (parts[:, :width] + parts[:, width : 2 * width]) + parts[:, 2 * width :]


def stencil_term(own, position, edge_codes):
    bin_count = lax.axis_size("bin")
    row_count, width = own.shape
    group_size = row_count // bin_count
    grid_rows, grid_cols = edge_codes.shape
    payload = jnp.concatenate([own, position.astype(jnp.float32)[:, None]], 1)
    got = lax.all_to_all(
        payload.reshape(bin_count, group_size * (width + 1)), "bin", 0, 0, tiled=True
    ).reshape(row_count, width + 1)
    tile_slot = got[:, width].astype(jnp.int32) - lax.axis_index("bin") * row_count
    cells = lax.broadcasted_iota(jnp.int32, (row_count, row_count), 1)
    onehot = (tile_slot[:, None] == cells).astype(jnp.bfloat16)
    placed = lax.dot_general(
        onehot, split_three(got[:, :width]), (((0,), (0,)), ((), ())),
        preferred_element_type=jnp.float32,
    )
    tile_rows = join_three(placed, width)
    cell_scale = edge_codes.astype(jnp.float32) / 8.0
    weighted = cell_scale[:, :, None] * tile_rows.reshape(grid_rows, grid_cols, width)
    rim_last, rim_first = (weighted[-1], weighted[0])
    upper_rows, upper_scale = passed_along((rim_last, cell_scale[-1]), "bin", 1)
    lower_rows, lower_scale = passed_along((rim_first, cell_scale[0]), "bin", -1)
    degree_grid = (
        cell_scale * neighbour_first(cell_scale[None], upper_scale[None], lower_scale[None])[0]
    )
    smooth_grid = cell_scale[:, :, None] * neighbour_sum(weighted, upper_rows, lower_rows)
    back = jnp.concatenate(
        [smooth_grid.reshape(row_count, width), degree_grid.reshape(row_count, 1)], 1
    )
    back_rows = join_three(
        jnp.dot(onehot, split_three(back), preferred_element_type=jnp.float32), width + 1
    )
    ret = lax.all_to_all(
        back_rows.reshape(bin_count, group_size * (width + 1)), "bin", 0, 0, tiled=True
    ).reshape(row_count, width + 1)
    return (ret[:, :width], ret[:, width])


def on_device(counts, factors, loadings, position, edge_codes):
    bin_count = lax.axis_size("bin")
    gene_count = lax.axis_size("gene")
    row_count, width_all = factors.shape
    width = width_all // gene_count
    k_rows = width_all // bin_count
    gene_at = lax.axis_index("gene")
    bin_at = lax.axis_index("bin")
    load_bf = loadings.astype(jnp.bfloat16)
    right_dims = (((1,), (1,)), ((), ()))
    numer_part = lax.dot_general(load_bf, counts, right_dims, preferred_element_type=jnp.float32)
    gram_part = lax.dot_general(load_bf, load_bf, right_dims, preferred_element_type=jnp.float32)
    both = jnp.concatenate([numer_part, gram_part], 1)
    both = lax.psum_scatter(
        both.reshape(gene_count, width, -1), "gene", scatter_dimension=0, tiled=True
    ).reshape(width, -1)
    numer_t, gram_rows = both[:, :row_count], both[:, row_count:]
    own = lax.dynamic_slice_in_dim(factors, gene_at * width, width, 1)
    smooth, degree = stencil_term(own, position, edge_codes)
    penalty = float(G * K) / 64.0
    own_t = own.T
    denom_t = (
        lax.dot_general(gram_rows, factors, right_dims, precision=lax.Precision.HIGHEST)
        + penalty * degree[None, :] * own_t
    )
    new_t = own_t * (numer_t + penalty * smooth.T) / denom_t
    factors_t = exchange(new_t, "gene", 0, False).reshape(width_all, row_count)
    factors_new = factors_t.T
    fac_bf_t = factors_t.astype(jnp.bfloat16)
    cross_part = jnp.dot(fac_bf_t, counts, preferred_element_type=jnp.float32)
    fgram_part = lax.dot_general(fac_bf_t, fac_bf_t, right_dims, preferred_element_type=jnp.float32)
    both_bin = jnp.concatenate([cross_part, fgram_part], 1)
    own_load = lax.dynamic_slice_in_dim(loadings, bin_at * k_rows, k_rows, 0)
    loadings_new = loadings_update(
        both_bin.reshape(bin_count, k_rows, -1), own_load, loadings, 2
    ).reshape(width_all, -1)
    return (factors_new, loadings_new)


def solution(mesh):
    placed = (P("bin", "gene"), P("bin", None), P(None, "gene"), P("bin"), P("bin", None))
    return jax.shard_map(
        on_device,
        mesh=mesh,
        in_specs=placed,
        out_specs=(P("bin", None), P(None, "gene")),
        check_vma=False,
    )
```

```python
import functools

import jax
import jax.numpy as jnp
from jax import lax
from jax.experimental import pallas as pl
from jax.experimental.pallas import tpu as pltpu
from jax.sharding import PartitionSpec as P

K = 256
G = 18432


def passed_along(block, axis, distance):
    devices = range(lax.axis_size(axis))
    route = [(i - distance, i) for i in devices if i - distance in devices]
    return lax.ppermute(block, axis, route)


def neighbour_sum(values, from_above, from_below):
    upper = jnp.concatenate([from_above[None], values[:-1]], 0)
    lower = jnp.concatenate([values[1:], from_below[None]], 0)
    beside = jnp.pad(values[:, 1:], ((0, 0), (0, 1), (0, 0))) + jnp.pad(
        values[:, :-1], ((0, 0), (1, 0), (0, 0))
    )
    return beside + 0.5 * (lower + upper)


def neighbour_first(values, from_above, from_below):
    upper = jnp.concatenate([from_above[:, None], values[:, :-1]], 1)
    lower = jnp.concatenate([values[:, 1:], from_below[:, None]], 1)
    beside = jnp.pad(values[:, :, 1:], ((0, 0), (0, 0), (0, 1))) + jnp.pad(
        values[:, :, :-1], ((0, 0), (0, 0), (1, 0))
    )
    return beside + 0.5 * (lower + upper)


def gray(value):
    return value + (value // 2) * (1 - 2 * (value % 2))


def gene_at_place(place, count):
    wide = 1 - ((place + count - 1) % count) // (count // 2)
    row = wide * (place - 1) + (1 - wide) * ((count - place) % count)
    return 2 * row + wide


def gene_place(index, count):
    row, wide = index // 2, index % 2
    return wide * (1 + row) + (1 - wide) * ((count - row) % count)


def bin_at_place(place, count):
    plane, step = place // 4, place % 4
    turned = step + (plane % 2) * (3 - 2 * step)
    return plane * 4 + gray(turned)


def bin_place(index, count):
    plane = index // 4
    turned = gray(index % 4)
    return plane * 4 + turned + (plane % 2) * (3 - 2 * turned)


RINGS = {"gene": (gene_at_place, gene_place), "bin": (bin_at_place, bin_place)}


def ring_peers(axis, count):
    at_place, place_of = RINGS[axis]
    place = place_of(lax.axis_index(axis), count)
    return place, (lambda shift: at_place((place + shift + count) % count, count))


def enter(axis, peers):
    barrier = pltpu.get_barrier_semaphore()
    for peer in peers:
        pl.semaphore_signal(barrier, inc=1, device_id={axis: peer},
                            device_id_type=pl.DeviceIdType.MESH)
    pl.semaphore_wait(barrier, len(peers))


def gather_kernel(axis, count, x_ref, out_ref, send_sem, recv_sem):
    place, member = ring_peers(axis, count)
    ahead, behind = member(1), member(-1)
    half = x_ref.shape[0] // 2
    enter(axis, (ahead, behind))
    out_ref[member(0)] = x_ref[...]

    def copy(step, way):
        rows = pl.ds(way * half, half)
        origin = member(-step) if way == 0 else member(step)
        src = x_ref.at[rows] if step == 0 else out_ref.at[origin, rows]
        return pltpu.make_async_remote_copy(
            src_ref=src,
            dst_ref=out_ref.at[origin, rows],
            send_sem=send_sem.at[way, step],
            recv_sem=recv_sem.at[way, step],
            device_id={axis: ahead if way == 0 else behind},
            device_id_type=pl.DeviceIdType.MESH,
        )

    for step in range(count - 1):
        for way in (0, 1):
            if step >= 1:
                copy(step - 1, way).wait_recv()
            copy(step, way).start()
    for way in (0, 1):
        copy(count - 2, way).wait_recv()
    for step in range(count - 1):
        for way in (0, 1):
            copy(step, way).wait_send()


def ring_gather(x, axis, collective_id):
    count = lax.axis_size(axis)
    return pl.pallas_call(
        functools.partial(gather_kernel, axis, count),
        out_shape=jax.ShapeDtypeStruct((count,) + x.shape, x.dtype),
        in_specs=[pl.BlockSpec(memory_space=pltpu.VMEM)],
        out_specs=pl.BlockSpec(memory_space=pltpu.VMEM),
        scratch_shapes=[
            pltpu.SemaphoreType.DMA((2, count - 1)),
            pltpu.SemaphoreType.DMA((2, count - 1)),
        ],
        compiler_params=pltpu.CompilerParams(
            collective_id=collective_id, has_side_effects=True
        ),
    )(x)


def scatter_kernel(axis, count, x_ref, out_ref, got, sent, send_sem, recv_sem):
    place, member = ring_peers(axis, count)
    ahead, behind = member(1), member(-1)
    half = x_ref.shape[2] // 2
    enter(axis, (ahead, behind))

    def copy(step, way):
        lanes = pl.ds(way * half, half)
        if step == 0:
            source = x_ref.at[member(-1) if way == 0 else member(1), :, lanes]
        else:
            source = sent.at[way, step]
        return pltpu.make_async_remote_copy(
            src_ref=source,
            dst_ref=got.at[way, step],
            send_sem=send_sem.at[way, step],
            recv_sem=recv_sem.at[way, step],
            device_id={axis: ahead if way == 0 else behind},
            device_id_type=pl.DeviceIdType.MESH,
        )

    for step in range(count - 1):
        for way in (0, 1):
            if step >= 1:
                lanes = pl.ds(way * half, half)
                owner = member(-step - 1) if way == 0 else member(step + 1)
                copy(step - 1, way).wait_recv()
                sent[way, step] = got[way, step - 1] + x_ref[owner, :, lanes]
            copy(step, way).start()
    for way in (0, 1):
        lanes = pl.ds(way * half, half)
        copy(count - 2, way).wait_recv()
        out_ref[:, lanes] = got[way, count - 2] + x_ref[member(0), :, lanes]
    for step in range(count - 1):
        for way in (0, 1):
            copy(step, way).wait_send()


def ring_scatter(x, axis, collective_id):
    count, rows, lanes = x.shape
    return pl.pallas_call(
        functools.partial(scatter_kernel, axis, count),
        out_shape=jax.ShapeDtypeStruct((rows, lanes), x.dtype),
        in_specs=[pl.BlockSpec(memory_space=pltpu.VMEM)],
        out_specs=pl.BlockSpec(memory_space=pltpu.VMEM),
        scratch_shapes=[
            pltpu.VMEM((2, count - 1, rows, lanes // 2), x.dtype),
            pltpu.VMEM((2, count - 1, rows, lanes // 2), x.dtype),
            pltpu.SemaphoreType.DMA((2, count - 1)),
            pltpu.SemaphoreType.DMA((2, count - 1)),
        ],
        compiler_params=pltpu.CompilerParams(
            collective_id=collective_id, has_side_effects=True
        ),
    )(x)


def greet_all(axis, me, count):
    barrier = pltpu.get_barrier_semaphore()
    for shift in range(1, count):
        pl.semaphore_signal(barrier, inc=1, device_id={axis: (me + shift) % count},
                            device_id_type=pl.DeviceIdType.MESH)
    pl.semaphore_wait(barrier, count - 1)


def exchange_kernel(axis, count, summed, x_ref, out_ref, *rest):
    if summed:
        got, send_sem, recv_sem = rest
    else:
        got, (send_sem, recv_sem) = out_ref, rest
    me = lax.axis_index(axis)
    greet_all(axis, me, count)

    def copy(shift):
        target = (me + shift) % count
        return pltpu.make_async_remote_copy(
            src_ref=x_ref.at[target] if summed else x_ref,
            dst_ref=got.at[me],
            send_sem=send_sem.at[shift],
            recv_sem=recv_sem.at[me],
            device_id={axis: target},
            device_id_type=pl.DeviceIdType.MESH,
        )

    def arrival(shift):
        origin = (me + count - shift) % count
        return pltpu.make_async_remote_copy(
            src_ref=x_ref.at[origin] if summed else x_ref,
            dst_ref=got.at[origin],
            send_sem=send_sem.at[shift],
            recv_sem=recv_sem.at[origin],
            device_id={axis: origin},
            device_id_type=pl.DeviceIdType.MESH,
        )

    for shift in range(1, count):
        copy(shift).start()
    if summed:
        total = x_ref[me]
        for shift in range(1, count):
            arrival(shift).wait_recv()
            total = total + got[(me + count - shift) % count]
        out_ref[...] = total
    else:
        out_ref[me] = x_ref[...]
        for shift in range(1, count):
            arrival(shift).wait_recv()
    for shift in range(1, count):
        copy(shift).wait_send()


def exchange(x, axis, collective_id, summed):
    count = lax.axis_size(axis)
    if summed:
        out_shape = x.shape[1:]
        scratch = [pltpu.VMEM(x.shape, x.dtype)]
    else:
        out_shape = (count,) + x.shape
        scratch = []
    return pl.pallas_call(
        functools.partial(exchange_kernel, axis, count, summed),
        out_shape=jax.ShapeDtypeStruct(out_shape, x.dtype),
        in_specs=[pl.BlockSpec(memory_space=pltpu.VMEM)],
        out_specs=pl.BlockSpec(memory_space=pltpu.VMEM),
        scratch_shapes=scratch + [
            pltpu.SemaphoreType.DMA((count,)),
            pltpu.SemaphoreType.DMA((count,)),
        ],
        compiler_params=pltpu.CompilerParams(
            collective_id=collective_id, has_side_effects=True
        ),
    )(x)


def loadings_kernel(count, cross_ref, gram_ref, load_ref, out_ref, got, got_gram, sem_a, sem_b, sem_c, sem_d):
    me = lax.axis_index("bin")
    greet_all("bin", me, count)

    def remote(src, dst, send, recv, shift, index, peer):
        return pltpu.make_async_remote_copy(
            src_ref=src.at[index],
            dst_ref=dst.at[index],
            send_sem=send.at[shift],
            recv_sem=recv.at[index],
            device_id={"bin": peer},
            device_id_type=pl.DeviceIdType.MESH,
        )

    def partial_copies(shift):
        target = (me + shift) % count
        return (
            pltpu.make_async_remote_copy(
                src_ref=cross_ref.at[target], dst_ref=got.at[me], send_sem=sem_a.at[0, shift],
                recv_sem=sem_b.at[0, me], device_id={"bin": target},
                device_id_type=pl.DeviceIdType.MESH,
            ),
            pltpu.make_async_remote_copy(
                src_ref=gram_ref.at[target], dst_ref=got_gram.at[me], send_sem=sem_a.at[1, shift],
                recv_sem=sem_b.at[1, me], device_id={"bin": target},
                device_id_type=pl.DeviceIdType.MESH,
            ),
        )

    def partial_arrivals(shift):
        origin = (me + count - shift) % count
        return (
            pltpu.make_async_remote_copy(
                src_ref=cross_ref.at[origin], dst_ref=got.at[origin], send_sem=sem_a.at[0, shift],
                recv_sem=sem_b.at[0, origin], device_id={"bin": origin},
                device_id_type=pl.DeviceIdType.MESH,
            ),
            pltpu.make_async_remote_copy(
                src_ref=gram_ref.at[origin], dst_ref=got_gram.at[origin], send_sem=sem_a.at[1, shift],
                recv_sem=sem_b.at[1, origin], device_id={"bin": origin},
                device_id_type=pl.DeviceIdType.MESH,
            ),
        )

    def result_copy(shift):
        target = (me + shift) % count
        return remote(out_ref, out_ref, sem_c, sem_d, shift, me, target)

    def result_arrival(shift):
        origin = (me + count - shift) % count
        return remote(out_ref, out_ref, sem_c, sem_d, shift, origin, origin)

    for shift in range(1, count):
        for copy in partial_copies(shift):
            copy.start()
    cross = cross_ref[me]
    fac_gram = gram_ref[me]
    for shift in range(1, count):
        origin = (me + count - shift) % count
        for copy in partial_arrivals(shift):
            copy.wait_recv()
        cross = cross + got[origin]
        fac_gram = fac_gram + got_gram[origin]
    rows = cross.shape[0]
    own = load_ref[pl.ds(pl.multiple_of(me * rows, rows), rows), :]
    denom = jnp.dot(
        fac_gram, load_ref[...], precision=lax.Precision.HIGHEST,
        preferred_element_type=jnp.float32,
    )
    out_ref[me] = own * cross / denom
    for shift in range(1, count):
        for copy in partial_copies(shift):
            copy.wait_send()
    for shift in range(1, count):
        result_copy(shift).start()
    for shift in range(1, count):
        result_arrival(shift).wait_recv()
    for shift in range(1, count):
        result_copy(shift).wait_send()


def loadings_update(cross_parts, gram_parts, loadings, collective_id):
    count, rows, genes = cross_parts.shape
    vmem = pl.BlockSpec(memory_space=pltpu.VMEM)
    return pl.pallas_call(
        functools.partial(loadings_kernel, count),
        out_shape=jax.ShapeDtypeStruct((count, rows, genes), loadings.dtype),
        in_specs=[vmem, vmem, vmem],
        out_specs=vmem,
        scratch_shapes=[
            pltpu.VMEM(cross_parts.shape, cross_parts.dtype),
            pltpu.VMEM(gram_parts.shape, gram_parts.dtype),
            pltpu.SemaphoreType.DMA((2, count)),
            pltpu.SemaphoreType.DMA((2, count)),
            pltpu.SemaphoreType.DMA((count,)),
            pltpu.SemaphoreType.DMA((count,)),
        ],
        compiler_params=pltpu.CompilerParams(
            collective_id=collective_id, has_side_effects=True
        ),
    )(cross_parts, gram_parts, loadings)


def split_three(values):
    high = lax.reduce_precision(values, exponent_bits=8, mantissa_bits=7)
    rest = values - high
    mid = lax.reduce_precision(rest, exponent_bits=8, mantissa_bits=7)
    low = rest - mid
    return jnp.concatenate([high, mid, low], 1).astype(jnp.bfloat16)


def join_three(parts, width):
    return (parts[:, :width] + parts[:, width : 2 * width]) + parts[:, 2 * width :]


def stencil_term(own, position, edge_codes):
    bin_count = lax.axis_size("bin")
    row_count, width = own.shape
    group_size = row_count // bin_count
    grid_rows, grid_cols = edge_codes.shape
    payload = jnp.concatenate([own, position.astype(jnp.float32)[:, None]], 1)
    got = lax.all_to_all(
        payload.reshape(bin_count, group_size * (width + 1)), "bin", 0, 0, tiled=True
    ).reshape(row_count, width + 1)
    tile_slot = got[:, width].astype(jnp.int32) - lax.axis_index("bin") * row_count
    cells = lax.broadcasted_iota(jnp.int32, (row_count, row_count), 1)
    onehot = (tile_slot[:, None] == cells).astype(jnp.bfloat16)
    placed = lax.dot_general(
        onehot, split_three(got[:, :width]), (((0,), (0,)), ((), ())),
        preferred_element_type=jnp.float32,
    )
    tile_rows = join_three(placed, width)
    cell_scale = edge_codes.astype(jnp.float32) / 8.0
    weighted = cell_scale[:, :, None] * tile_rows.reshape(grid_rows, grid_cols, width)
    rim_last, rim_first = (weighted[-1], weighted[0])
    upper_rows, upper_scale = passed_along((rim_last, cell_scale[-1]), "bin", 1)
    lower_rows, lower_scale = passed_along((rim_first, cell_scale[0]), "bin", -1)
    degree_grid = (
        cell_scale * neighbour_first(cell_scale[None], upper_scale[None], lower_scale[None])[0]
    )
    smooth_grid = cell_scale[:, :, None] * neighbour_sum(weighted, upper_rows, lower_rows)
    back = jnp.concatenate(
        [smooth_grid.reshape(row_count, width), degree_grid.reshape(row_count, 1)], 1
    )
    back_rows = join_three(
        jnp.dot(onehot, split_three(back), preferred_element_type=jnp.float32), width + 1
    )
    ret = lax.all_to_all(
        back_rows.reshape(bin_count, group_size * (width + 1)), "bin", 0, 0, tiled=True
    ).reshape(row_count, width + 1)
    return (ret[:, :width], ret[:, width])


def on_device(counts, factors, loadings, position, edge_codes):
    bin_count = lax.axis_size("bin")
    gene_count = lax.axis_size("gene")
    row_count, width_all = factors.shape
    width = width_all // gene_count
    k_rows = width_all // bin_count
    gene_at = lax.axis_index("gene")
    bin_at = lax.axis_index("bin")
    load_bf = loadings.astype(jnp.bfloat16)
    right_dims = (((1,), (1,)), ((), ()))
    numer_part = lax.dot_general(load_bf, counts, right_dims, preferred_element_type=jnp.float32)
    gram_part = lax.dot_general(load_bf, load_bf, right_dims, preferred_element_type=jnp.float32)
    both = jnp.concatenate([numer_part, gram_part], 1)
    both = lax.psum_scatter(
        both.reshape(gene_count, width, -1), "gene", scatter_dimension=0, tiled=True
    ).reshape(width, -1)
    numer_t, gram_rows = both[:, :row_count], both[:, row_count:]
    own = lax.dynamic_slice_in_dim(factors, gene_at * width, width, 1)
    smooth, degree = stencil_term(own, position, edge_codes)
    penalty = float(G * K) / 64.0
    own_t = own.T
    denom_t = (
        lax.dot_general(gram_rows, factors, right_dims, precision=lax.Precision.HIGHEST)
        + penalty * degree[None, :] * own_t
    )
    new_t = own_t * (numer_t + penalty * smooth.T) / denom_t
    factors_t = exchange(new_t, "gene", 0, False).reshape(width_all, row_count)
    factors_new = factors_t.T
    fac_bf_t = factors_t.astype(jnp.bfloat16)
    cross_part = jnp.dot(fac_bf_t, counts, preferred_element_type=jnp.float32)
    fgram_part = lax.dot_general(fac_bf_t, fac_bf_t, right_dims, preferred_element_type=jnp.float32)
    loadings_new = loadings_update(
        cross_part.reshape(bin_count, k_rows, -1),
        fgram_part.reshape(bin_count, k_rows, -1),
        loadings,
        2,
    ).reshape(width_all, -1)
    return (factors_new, loadings_new)


def solution(mesh):
    placed = (P("bin", "gene"), P("bin", None), P(None, "gene"), P("bin"), P("bin", None))
    return jax.shard_map(
        on_device,
        mesh=mesh,
        in_specs=placed,
        out_specs=(P("bin", None), P(None, "gene")),
        check_vma=False,
    )
```

```python
import functools

import jax
import jax.numpy as jnp
from jax import lax
from jax.experimental import pallas as pl
from jax.experimental.pallas import tpu as pltpu
from jax.sharding import PartitionSpec as P

K = 256
G = 18432


def passed_along(block, axis, distance):
    devices = range(lax.axis_size(axis))
    route = [(i - distance, i) for i in devices if i - distance in devices]
    return lax.ppermute(block, axis, route)


def neighbour_sum(values, from_above, from_below):
    upper = jnp.concatenate([from_above[None], values[:-1]], 0)
    lower = jnp.concatenate([values[1:], from_below[None]], 0)
    beside = jnp.pad(values[:, 1:], ((0, 0), (0, 1), (0, 0))) + jnp.pad(
        values[:, :-1], ((0, 0), (1, 0), (0, 0))
    )
    return beside + 0.5 * (lower + upper)


def neighbour_first(values, from_above, from_below):
    upper = jnp.concatenate([from_above[:, None], values[:, :-1]], 1)
    lower = jnp.concatenate([values[:, 1:], from_below[:, None]], 1)
    beside = jnp.pad(values[:, :, 1:], ((0, 0), (0, 0), (0, 1))) + jnp.pad(
        values[:, :, :-1], ((0, 0), (0, 0), (1, 0))
    )
    return beside + 0.5 * (lower + upper)


def gray(value):
    return value + (value // 2) * (1 - 2 * (value % 2))


def gene_at_place(place, count):
    wide = 1 - ((place + count - 1) % count) // (count // 2)
    row = wide * (place - 1) + (1 - wide) * ((count - place) % count)
    return 2 * row + wide


def gene_place(index, count):
    row, wide = index // 2, index % 2
    return wide * (1 + row) + (1 - wide) * ((count - row) % count)


def bin_at_place(place, count):
    plane, step = place // 4, place % 4
    turned = step + (plane % 2) * (3 - 2 * step)
    return plane * 4 + gray(turned)


def bin_place(index, count):
    plane = index // 4
    turned = gray(index % 4)
    return plane * 4 + turned + (plane % 2) * (3 - 2 * turned)


RINGS = {"gene": (gene_at_place, gene_place), "bin": (bin_at_place, bin_place)}


def ring_peers(axis, count):
    at_place, place_of = RINGS[axis]
    place = place_of(lax.axis_index(axis), count)
    return place, (lambda shift: at_place((place + shift + count) % count, count))


def enter(axis, peers):
    barrier = pltpu.get_barrier_semaphore()
    for peer in peers:
        pl.semaphore_signal(barrier, inc=1, device_id={axis: peer},
                            device_id_type=pl.DeviceIdType.MESH)
    pl.semaphore_wait(barrier, len(peers))


def gather_kernel(axis, count, x_ref, out_ref, send_sem, recv_sem):
    place, member = ring_peers(axis, count)
    ahead, behind = member(1), member(-1)
    half = x_ref.shape[0] // 2
    enter(axis, (ahead, behind))
    out_ref[member(0)] = x_ref[...]

    def copy(step, way):
        rows = pl.ds(way * half, half)
        origin = member(-step) if way == 0 else member(step)
        src = x_ref.at[rows] if step == 0 else out_ref.at[origin, rows]
        return pltpu.make_async_remote_copy(
            src_ref=src,
            dst_ref=out_ref.at[origin, rows],
            send_sem=send_sem.at[way, step],
            recv_sem=recv_sem.at[way, step],
            device_id={axis: ahead if way == 0 else behind},
            device_id_type=pl.DeviceIdType.MESH,
        )

    for step in range(count - 1):
        for way in (0, 1):
            if step >= 1:
                copy(step - 1, way).wait_recv()
            copy(step, way).start()
    for way in (0, 1):
        copy(count - 2, way).wait_recv()
    for step in range(count - 1):
        for way in (0, 1):
            copy(step, way).wait_send()


def ring_gather(x, axis, collective_id):
    count = lax.axis_size(axis)
    return pl.pallas_call(
        functools.partial(gather_kernel, axis, count),
        out_shape=jax.ShapeDtypeStruct((count,) + x.shape, x.dtype),
        in_specs=[pl.BlockSpec(memory_space=pltpu.VMEM)],
        out_specs=pl.BlockSpec(memory_space=pltpu.VMEM),
        scratch_shapes=[
            pltpu.SemaphoreType.DMA((2, count - 1)),
            pltpu.SemaphoreType.DMA((2, count - 1)),
        ],
        compiler_params=pltpu.CompilerParams(
            collective_id=collective_id, has_side_effects=True
        ),
    )(x)


def scatter_kernel(axis, count, x_ref, out_ref, got, sent, send_sem, recv_sem):
    place, member = ring_peers(axis, count)
    ahead, behind = member(1), member(-1)
    half = x_ref.shape[2] // 2
    enter(axis, (ahead, behind))

    def copy(step, way):
        lanes = pl.ds(way * half, half)
        if step == 0:
            source = x_ref.at[member(-1) if way == 0 else member(1), :, lanes]
        else:
            source = sent.at[way, step]
        return pltpu.make_async_remote_copy(
            src_ref=source,
            dst_ref=got.at[way, step],
            send_sem=send_sem.at[way, step],
            recv_sem=recv_sem.at[way, step],
            device_id={axis: ahead if way == 0 else behind},
            device_id_type=pl.DeviceIdType.MESH,
        )

    for step in range(count - 1):
        for way in (0, 1):
            if step >= 1:
                lanes = pl.ds(way * half, half)
                owner = member(-step - 1) if way == 0 else member(step + 1)
                copy(step - 1, way).wait_recv()
                sent[way, step] = got[way, step - 1] + x_ref[owner, :, lanes]
            copy(step, way).start()
    for way in (0, 1):
        lanes = pl.ds(way * half, half)
        copy(count - 2, way).wait_recv()
        out_ref[:, lanes] = got[way, count - 2] + x_ref[member(0), :, lanes]
    for step in range(count - 1):
        for way in (0, 1):
            copy(step, way).wait_send()


def ring_scatter(x, axis, collective_id):
    count, rows, lanes = x.shape
    return pl.pallas_call(
        functools.partial(scatter_kernel, axis, count),
        out_shape=jax.ShapeDtypeStruct((rows, lanes), x.dtype),
        in_specs=[pl.BlockSpec(memory_space=pltpu.VMEM)],
        out_specs=pl.BlockSpec(memory_space=pltpu.VMEM),
        scratch_shapes=[
            pltpu.VMEM((2, count - 1, rows, lanes // 2), x.dtype),
            pltpu.VMEM((2, count - 1, rows, lanes // 2), x.dtype),
            pltpu.SemaphoreType.DMA((2, count - 1)),
            pltpu.SemaphoreType.DMA((2, count - 1)),
        ],
        compiler_params=pltpu.CompilerParams(
            collective_id=collective_id, has_side_effects=True
        ),
    )(x)


def greet_all(axis, me, count):
    barrier = pltpu.get_barrier_semaphore()
    for shift in range(1, count):
        pl.semaphore_signal(barrier, inc=1, device_id={axis: (me + shift) % count},
                            device_id_type=pl.DeviceIdType.MESH)
    pl.semaphore_wait(barrier, count - 1)


def exchange_kernel(axis, count, summed, x_ref, out_ref, *rest):
    if summed:
        got, send_sem, recv_sem = rest
    else:
        got, (send_sem, recv_sem) = out_ref, rest
    me = lax.axis_index(axis)
    greet_all(axis, me, count)

    def copy(shift):
        target = (me + shift) % count
        return pltpu.make_async_remote_copy(
            src_ref=x_ref.at[target] if summed else x_ref,
            dst_ref=got.at[me],
            send_sem=send_sem.at[shift],
            recv_sem=recv_sem.at[me],
            device_id={axis: target},
            device_id_type=pl.DeviceIdType.MESH,
        )

    def arrival(shift):
        origin = (me + count - shift) % count
        return pltpu.make_async_remote_copy(
            src_ref=x_ref.at[origin] if summed else x_ref,
            dst_ref=got.at[origin],
            send_sem=send_sem.at[shift],
            recv_sem=recv_sem.at[origin],
            device_id={axis: origin},
            device_id_type=pl.DeviceIdType.MESH,
        )

    for shift in range(1, count):
        copy(shift).start()
    if summed:
        total = x_ref[me]
        for shift in range(1, count):
            arrival(shift).wait_recv()
            total = total + got[(me + count - shift) % count]
        out_ref[...] = total
    else:
        out_ref[me] = x_ref[...]
        for shift in range(1, count):
            arrival(shift).wait_recv()
    for shift in range(1, count):
        copy(shift).wait_send()


def exchange(x, axis, collective_id, summed):
    count = lax.axis_size(axis)
    if summed:
        out_shape = x.shape[1:]
        scratch = [pltpu.VMEM(x.shape, x.dtype)]
    else:
        out_shape = (count,) + x.shape
        scratch = []
    return pl.pallas_call(
        functools.partial(exchange_kernel, axis, count, summed),
        out_shape=jax.ShapeDtypeStruct(out_shape, x.dtype),
        in_specs=[pl.BlockSpec(memory_space=pltpu.VMEM)],
        out_specs=pl.BlockSpec(memory_space=pltpu.VMEM),
        scratch_shapes=scratch + [
            pltpu.SemaphoreType.DMA((count,)),
            pltpu.SemaphoreType.DMA((count,)),
        ],
        compiler_params=pltpu.CompilerParams(
            collective_id=collective_id, has_side_effects=True
        ),
    )(x)


def loadings_kernel(count, cross_ref, gram_ref, load_ref, out_ref, got, got_gram, sem_a, sem_b, sem_c, sem_d):
    me = lax.axis_index("bin")
    greet_all("bin", me, count)

    def remote(src, dst, send, recv, shift, index, peer):
        return pltpu.make_async_remote_copy(
            src_ref=src.at[index],
            dst_ref=dst.at[index],
            send_sem=send.at[shift],
            recv_sem=recv.at[index],
            device_id={"bin": peer},
            device_id_type=pl.DeviceIdType.MESH,
        )

    def partial_copies(shift):
        target = (me + shift) % count
        return (
            pltpu.make_async_remote_copy(
                src_ref=cross_ref.at[target], dst_ref=got.at[me], send_sem=sem_a.at[0, shift],
                recv_sem=sem_b.at[0, me], device_id={"bin": target},
                device_id_type=pl.DeviceIdType.MESH,
            ),
            pltpu.make_async_remote_copy(
                src_ref=gram_ref.at[target], dst_ref=got_gram.at[me], send_sem=sem_a.at[1, shift],
                recv_sem=sem_b.at[1, me], device_id={"bin": target},
                device_id_type=pl.DeviceIdType.MESH,
            ),
        )

    def partial_arrivals(shift):
        origin = (me + count - shift) % count
        return (
            pltpu.make_async_remote_copy(
                src_ref=cross_ref.at[origin], dst_ref=got.at[origin], send_sem=sem_a.at[0, shift],
                recv_sem=sem_b.at[0, origin], device_id={"bin": origin},
                device_id_type=pl.DeviceIdType.MESH,
            ),
            pltpu.make_async_remote_copy(
                src_ref=gram_ref.at[origin], dst_ref=got_gram.at[origin], send_sem=sem_a.at[1, shift],
                recv_sem=sem_b.at[1, origin], device_id={"bin": origin},
                device_id_type=pl.DeviceIdType.MESH,
            ),
        )

    def result_copy(shift):
        target = (me + shift) % count
        return remote(out_ref, out_ref, sem_c, sem_d, shift, me, target)

    def result_arrival(shift):
        origin = (me + count - shift) % count
        return remote(out_ref, out_ref, sem_c, sem_d, shift, origin, origin)

    for shift in range(1, count):
        for copy in partial_copies(shift):
            copy.start()
    cross = cross_ref[me]
    fac_gram = gram_ref[me]
    for shift in range(1, count):
        origin = (me + count - shift) % count
        for copy in partial_arrivals(shift):
            copy.wait_recv()
        cross = cross + got[origin]
        fac_gram = fac_gram + got_gram[origin]
    rows = cross.shape[0]
    own = load_ref[pl.ds(pl.multiple_of(me * rows, rows), rows), :]
    denom = jnp.dot(
        fac_gram, load_ref[...], precision=lax.Precision.HIGHEST,
        preferred_element_type=jnp.float32,
    )
    out_ref[me] = own * cross / denom
    for shift in range(1, count):
        for copy in partial_copies(shift):
            copy.wait_send()
    for shift in range(1, count):
        result_copy(shift).start()
    for shift in range(1, count):
        result_arrival(shift).wait_recv()
    for shift in range(1, count):
        result_copy(shift).wait_send()


def loadings_update(cross_parts, gram_parts, loadings, collective_id):
    count, rows, genes = cross_parts.shape
    vmem = pl.BlockSpec(memory_space=pltpu.VMEM)
    return pl.pallas_call(
        functools.partial(loadings_kernel, count),
        out_shape=jax.ShapeDtypeStruct((count, rows, genes), loadings.dtype),
        in_specs=[vmem, vmem, vmem],
        out_specs=vmem,
        scratch_shapes=[
            pltpu.VMEM(cross_parts.shape, cross_parts.dtype),
            pltpu.VMEM(gram_parts.shape, gram_parts.dtype),
            pltpu.SemaphoreType.DMA((2, count)),
            pltpu.SemaphoreType.DMA((2, count)),
            pltpu.SemaphoreType.DMA((count,)),
            pltpu.SemaphoreType.DMA((count,)),
        ],
        compiler_params=pltpu.CompilerParams(
            collective_id=collective_id, has_side_effects=True
        ),
    )(cross_parts, gram_parts, loadings)


def split_three(values):
    high = lax.reduce_precision(values, exponent_bits=8, mantissa_bits=7)
    rest = values - high
    mid = lax.reduce_precision(rest, exponent_bits=8, mantissa_bits=7)
    low = rest - mid
    return jnp.concatenate([high, mid, low], 0).astype(jnp.bfloat16)


def join_three(parts, width):
    return (parts[:width] + parts[width : 2 * width]) + parts[2 * width :]


def stencil_term(own_t, position, edge_codes):
    bin_count = lax.axis_size("bin")
    width, row_count = own_t.shape
    group_size = row_count // bin_count
    lanes = -(-group_size // 128) * 128
    grid_rows, grid_cols = edge_codes.shape
    payload = jnp.concatenate([own_t, position.astype(jnp.float32)[None, :]], 0)
    payload = jnp.pad(
        payload.reshape(width + 1, bin_count, group_size),
        ((0, 0), (0, 0), (0, lanes - group_size)),
        constant_values=-1.0,
    )
    got = lax.all_to_all(payload.transpose(1, 0, 2), "bin", 0, 0, tiled=True)
    got = got.transpose(1, 0, 2).reshape(width + 1, bin_count * lanes)
    tile_slot = got[width].astype(jnp.int32) - lax.axis_index("bin") * row_count
    cells = lax.broadcasted_iota(jnp.int32, (bin_count * lanes, row_count), 1)
    onehot = (tile_slot[:, None] == cells).astype(jnp.bfloat16)
    placed = jnp.dot(split_three(got[:width]), onehot, preferred_element_type=jnp.float32)
    tile_t = join_three(placed, width)
    cell_scale = edge_codes.astype(jnp.float32) / 8.0
    weighted = cell_scale[None] * tile_t.reshape(width, grid_rows, grid_cols)
    rim_last, rim_first = (weighted[:, -1], weighted[:, 0])
    upper_rows, upper_scale = passed_along((rim_last, cell_scale[-1]), "bin", 1)
    lower_rows, lower_scale = passed_along((rim_first, cell_scale[0]), "bin", -1)
    degree_grid = (
        cell_scale * neighbour_first(cell_scale[None], upper_scale[None], lower_scale[None])[0]
    )
    smooth_grid = cell_scale[None] * neighbour_first(weighted, upper_rows, lower_rows)
    back = jnp.concatenate(
        [smooth_grid.reshape(width, row_count), degree_grid.reshape(1, row_count)], 0
    )
    back_in = lax.dot_general(
        split_three(back), onehot, (((1,), (1,)), ((), ())), preferred_element_type=jnp.float32
    )
    back_in = join_three(back_in, width + 1).reshape(width + 1, bin_count, lanes)
    ret = lax.all_to_all(back_in.transpose(1, 0, 2), "bin", 0, 0, tiled=True)
    ret = ret[:, :, :group_size].transpose(1, 0, 2).reshape(width + 1, row_count)
    return (ret[:width], ret[width])


def on_device(counts, factors, loadings, position, edge_codes):
    bin_count = lax.axis_size("bin")
    gene_count = lax.axis_size("gene")
    row_count, width_all = factors.shape
    width = width_all // gene_count
    k_rows = width_all // bin_count
    gene_at = lax.axis_index("gene")
    bin_at = lax.axis_index("bin")
    load_bf = loadings.astype(jnp.bfloat16)
    right_dims = (((1,), (1,)), ((), ()))
    numer_part = lax.dot_general(load_bf, counts, right_dims, preferred_element_type=jnp.float32)
    gram_part = lax.dot_general(load_bf, load_bf, right_dims, preferred_element_type=jnp.float32)
    both = jnp.concatenate([numer_part, gram_part], 1)
    both = lax.psum_scatter(
        both.reshape(gene_count, width, -1), "gene", scatter_dimension=0, tiled=True
    ).reshape(width, -1)
    numer_t, gram_rows = both[:, :row_count], both[:, row_count:]
    own_t = lax.dynamic_slice_in_dim(factors, gene_at * width, width, 1).T
    smooth_t, degree = stencil_term(own_t, position, edge_codes)
    penalty = float(G * K) / 64.0
    denom_t = (
        lax.dot_general(gram_rows, factors, right_dims, precision=lax.Precision.HIGHEST)
        + penalty * degree[None, :] * own_t
    )
    new_t = own_t * (numer_t + penalty * smooth_t) / denom_t
    factors_t = exchange(new_t, "gene", 0, False).reshape(width_all, row_count)
    factors_new = factors_t.T
    fac_bf_t = factors_t.astype(jnp.bfloat16)
    cross_part = jnp.dot(fac_bf_t, counts, preferred_element_type=jnp.float32)
    fgram_part = lax.dot_general(fac_bf_t, fac_bf_t, right_dims, preferred_element_type=jnp.float32)
    loadings_new = loadings_update(
        cross_part.reshape(bin_count, k_rows, -1),
        fgram_part.reshape(bin_count, k_rows, -1),
        loadings,
        2,
    ).reshape(width_all, -1)
    return (factors_new, loadings_new)


def solution(mesh):
    placed = (P("bin", "gene"), P("bin", None), P(None, "gene"), P("bin"), P("bin", None))
    return jax.shard_map(
        on_device,
        mesh=mesh,
        in_specs=placed,
        out_specs=(P("bin", None), P(None, "gene")),
        check_vma=False,
    )
```

```python
import functools

import jax
import jax.numpy as jnp
from jax import lax
from jax.experimental import pallas as pl
from jax.experimental.pallas import tpu as pltpu
from jax.sharding import PartitionSpec as P

K = 256
G = 18432


def passed_along(block, axis, distance):
    devices = range(lax.axis_size(axis))
    route = [(i - distance, i) for i in devices if i - distance in devices]
    return lax.ppermute(block, axis, route)


def neighbour_sum(values, from_above, from_below):
    upper = jnp.concatenate([from_above[None], values[:-1]], 0)
    lower = jnp.concatenate([values[1:], from_below[None]], 0)
    beside = jnp.pad(values[:, 1:], ((0, 0), (0, 1), (0, 0))) + jnp.pad(
        values[:, :-1], ((0, 0), (1, 0), (0, 0))
    )
    return beside + 0.5 * (lower + upper)


def neighbour_first(values, from_above, from_below):
    upper = jnp.concatenate([from_above[:, None], values[:, :-1]], 1)
    lower = jnp.concatenate([values[:, 1:], from_below[:, None]], 1)
    beside = jnp.pad(values[:, :, 1:], ((0, 0), (0, 0), (0, 1))) + jnp.pad(
        values[:, :, :-1], ((0, 0), (0, 0), (1, 0))
    )
    return beside + 0.5 * (lower + upper)


def gray(value):
    return value + (value // 2) * (1 - 2 * (value % 2))


def gene_at_place(place, count):
    wide = 1 - ((place + count - 1) % count) // (count // 2)
    row = wide * (place - 1) + (1 - wide) * ((count - place) % count)
    return 2 * row + wide


def gene_place(index, count):
    row, wide = index // 2, index % 2
    return wide * (1 + row) + (1 - wide) * ((count - row) % count)


def bin_at_place(place, count):
    plane, step = place // 4, place % 4
    turned = step + (plane % 2) * (3 - 2 * step)
    return plane * 4 + gray(turned)


def bin_place(index, count):
    plane = index // 4
    turned = gray(index % 4)
    return plane * 4 + turned + (plane % 2) * (3 - 2 * turned)


RINGS = {"gene": (gene_at_place, gene_place), "bin": (bin_at_place, bin_place)}


def ring_peers(axis, count):
    at_place, place_of = RINGS[axis]
    place = place_of(lax.axis_index(axis), count)
    return place, (lambda shift: at_place((place + shift + count) % count, count))


def enter(axis, peers):
    barrier = pltpu.get_barrier_semaphore()
    for peer in peers:
        pl.semaphore_signal(barrier, inc=1, device_id={axis: peer},
                            device_id_type=pl.DeviceIdType.MESH)
    pl.semaphore_wait(barrier, len(peers))


def gather_kernel(axis, count, x_ref, out_ref, send_sem, recv_sem):
    place, member = ring_peers(axis, count)
    ahead, behind = member(1), member(-1)
    half = x_ref.shape[0] // 2
    enter(axis, (ahead, behind))
    out_ref[member(0)] = x_ref[...]

    def copy(step, way):
        rows = pl.ds(way * half, half)
        origin = member(-step) if way == 0 else member(step)
        src = x_ref.at[rows] if step == 0 else out_ref.at[origin, rows]
        return pltpu.make_async_remote_copy(
            src_ref=src,
            dst_ref=out_ref.at[origin, rows],
            send_sem=send_sem.at[way, step],
            recv_sem=recv_sem.at[way, step],
            device_id={axis: ahead if way == 0 else behind},
            device_id_type=pl.DeviceIdType.MESH,
        )

    for step in range(count - 1):
        for way in (0, 1):
            if step >= 1:
                copy(step - 1, way).wait_recv()
            copy(step, way).start()
    for way in (0, 1):
        copy(count - 2, way).wait_recv()
    for step in range(count - 1):
        for way in (0, 1):
            copy(step, way).wait_send()


def ring_gather(x, axis, collective_id):
    count = lax.axis_size(axis)
    return pl.pallas_call(
        functools.partial(gather_kernel, axis, count),
        out_shape=jax.ShapeDtypeStruct((count,) + x.shape, x.dtype),
        in_specs=[pl.BlockSpec(memory_space=pltpu.VMEM)],
        out_specs=pl.BlockSpec(memory_space=pltpu.VMEM),
        scratch_shapes=[
            pltpu.SemaphoreType.DMA((2, count - 1)),
            pltpu.SemaphoreType.DMA((2, count - 1)),
        ],
        compiler_params=pltpu.CompilerParams(
            collective_id=collective_id, has_side_effects=True
        ),
    )(x)


def scatter_kernel(axis, count, x_ref, out_ref, got, sent, send_sem, recv_sem):
    place, member = ring_peers(axis, count)
    ahead, behind = member(1), member(-1)
    half = x_ref.shape[2] // 2
    enter(axis, (ahead, behind))

    def copy(step, way):
        lanes = pl.ds(way * half, half)
        if step == 0:
            source = x_ref.at[member(-1) if way == 0 else member(1), :, lanes]
        else:
            source = sent.at[way, step]
        return pltpu.make_async_remote_copy(
            src_ref=source,
            dst_ref=got.at[way, step],
            send_sem=send_sem.at[way, step],
            recv_sem=recv_sem.at[way, step],
            device_id={axis: ahead if way == 0 else behind},
            device_id_type=pl.DeviceIdType.MESH,
        )

    for step in range(count - 1):
        for way in (0, 1):
            if step >= 1:
                lanes = pl.ds(way * half, half)
                owner = member(-step - 1) if way == 0 else member(step + 1)
                copy(step - 1, way).wait_recv()
                sent[way, step] = got[way, step - 1] + x_ref[owner, :, lanes]
            copy(step, way).start()
    for way in (0, 1):
        lanes = pl.ds(way * half, half)
        copy(count - 2, way).wait_recv()
        out_ref[:, lanes] = got[way, count - 2] + x_ref[member(0), :, lanes]
    for step in range(count - 1):
        for way in (0, 1):
            copy(step, way).wait_send()


def ring_scatter(x, axis, collective_id):
    count, rows, lanes = x.shape
    return pl.pallas_call(
        functools.partial(scatter_kernel, axis, count),
        out_shape=jax.ShapeDtypeStruct((rows, lanes), x.dtype),
        in_specs=[pl.BlockSpec(memory_space=pltpu.VMEM)],
        out_specs=pl.BlockSpec(memory_space=pltpu.VMEM),
        scratch_shapes=[
            pltpu.VMEM((2, count - 1, rows, lanes // 2), x.dtype),
            pltpu.VMEM((2, count - 1, rows, lanes // 2), x.dtype),
            pltpu.SemaphoreType.DMA((2, count - 1)),
            pltpu.SemaphoreType.DMA((2, count - 1)),
        ],
        compiler_params=pltpu.CompilerParams(
            collective_id=collective_id, has_side_effects=True
        ),
    )(x)


def greet_all(axis, me, count):
    barrier = pltpu.get_barrier_semaphore()
    for shift in range(1, count):
        pl.semaphore_signal(barrier, inc=1, device_id={axis: (me + shift) % count},
                            device_id_type=pl.DeviceIdType.MESH)
    pl.semaphore_wait(barrier, count - 1)


def exchange_kernel(axis, count, summed, x_ref, out_ref, *rest):
    if summed:
        got, send_sem, recv_sem = rest
    else:
        got, (send_sem, recv_sem) = out_ref, rest
    me = lax.axis_index(axis)
    greet_all(axis, me, count)

    def copy(shift):
        target = (me + shift) % count
        return pltpu.make_async_remote_copy(
            src_ref=x_ref.at[target] if summed else x_ref,
            dst_ref=got.at[me],
            send_sem=send_sem.at[shift],
            recv_sem=recv_sem.at[me],
            device_id={axis: target},
            device_id_type=pl.DeviceIdType.MESH,
        )

    def arrival(shift):
        origin = (me + count - shift) % count
        return pltpu.make_async_remote_copy(
            src_ref=x_ref.at[origin] if summed else x_ref,
            dst_ref=got.at[origin],
            send_sem=send_sem.at[shift],
            recv_sem=recv_sem.at[origin],
            device_id={axis: origin},
            device_id_type=pl.DeviceIdType.MESH,
        )

    for shift in range(1, count):
        copy(shift).start()
    if summed:
        total = x_ref[me]
        for shift in range(1, count):
            arrival(shift).wait_recv()
            total = total + got[(me + count - shift) % count]
        out_ref[...] = total
    else:
        out_ref[me] = x_ref[...]
        for shift in range(1, count):
            arrival(shift).wait_recv()
    for shift in range(1, count):
        copy(shift).wait_send()


def exchange(x, axis, collective_id, summed):
    count = lax.axis_size(axis)
    if summed:
        out_shape = x.shape[1:]
        scratch = [pltpu.VMEM(x.shape, x.dtype)]
    else:
        out_shape = (count,) + x.shape
        scratch = []
    return pl.pallas_call(
        functools.partial(exchange_kernel, axis, count, summed),
        out_shape=jax.ShapeDtypeStruct(out_shape, x.dtype),
        in_specs=[pl.BlockSpec(memory_space=pltpu.VMEM)],
        out_specs=pl.BlockSpec(memory_space=pltpu.VMEM),
        scratch_shapes=scratch + [
            pltpu.SemaphoreType.DMA((count,)),
            pltpu.SemaphoreType.DMA((count,)),
        ],
        compiler_params=pltpu.CompilerParams(
            collective_id=collective_id, has_side_effects=True
        ),
    )(x)


def factor_gather_kernel(count, x_ref, out_ref, half_ref, send_sem, recv_sem):
    me = lax.axis_index("gene")
    greet_all("gene", me, count)

    def copy(shift, index, peer):
        return pltpu.make_async_remote_copy(
            src_ref=x_ref,
            dst_ref=out_ref.at[index],
            send_sem=send_sem.at[shift],
            recv_sem=recv_sem.at[index],
            device_id={"gene": peer},
            device_id_type=pl.DeviceIdType.MESH,
        )

    for shift in range(1, count):
        copy(shift, me, (me + shift) % count).start()
    out_ref[me] = x_ref[...]
    for shift in range(1, count):
        origin = (me + count - shift) % count
        copy(shift, origin, origin).wait_recv()
    half_ref[...] = out_ref[...].astype(half_ref.dtype)
    for shift in range(1, count):
        copy(shift, me, (me + shift) % count).wait_send()


def factor_gather(x, collective_id):
    count = lax.axis_size("gene")
    vmem = pl.BlockSpec(memory_space=pltpu.VMEM)
    shape = (count,) + x.shape
    return pl.pallas_call(
        functools.partial(factor_gather_kernel, count),
        out_shape=(
            jax.ShapeDtypeStruct(shape, x.dtype),
            jax.ShapeDtypeStruct(shape, jnp.bfloat16),
        ),
        in_specs=[vmem],
        out_specs=(vmem, vmem),
        scratch_shapes=[pltpu.SemaphoreType.DMA((count,))] * 2,
        compiler_params=pltpu.CompilerParams(
            collective_id=collective_id, has_side_effects=True
        ),
    )(x)


def loadings_kernel(count, cross_ref, gram_ref, load_ref, out_ref, got, got_gram, sem_a, sem_b, sem_c, sem_d):
    me = lax.axis_index("bin")
    greet_all("bin", me, count)

    def remote(src, dst, send, recv, shift, index, peer):
        return pltpu.make_async_remote_copy(
            src_ref=src.at[index],
            dst_ref=dst.at[index],
            send_sem=send.at[shift],
            recv_sem=recv.at[index],
            device_id={"bin": peer},
            device_id_type=pl.DeviceIdType.MESH,
        )

    def partial_copies(shift):
        target = (me + shift) % count
        return (
            pltpu.make_async_remote_copy(
                src_ref=cross_ref.at[target], dst_ref=got.at[me], send_sem=sem_a.at[0, shift],
                recv_sem=sem_b.at[0, me], device_id={"bin": target},
                device_id_type=pl.DeviceIdType.MESH,
            ),
            pltpu.make_async_remote_copy(
                src_ref=gram_ref.at[target], dst_ref=got_gram.at[me], send_sem=sem_a.at[1, shift],
                recv_sem=sem_b.at[1, me], device_id={"bin": target},
                device_id_type=pl.DeviceIdType.MESH,
            ),
        )

    def partial_arrivals(shift):
        origin = (me + count - shift) % count
        return (
            pltpu.make_async_remote_copy(
                src_ref=cross_ref.at[origin], dst_ref=got.at[origin], send_sem=sem_a.at[0, shift],
                recv_sem=sem_b.at[0, origin], device_id={"bin": origin},
                device_id_type=pl.DeviceIdType.MESH,
            ),
            pltpu.make_async_remote_copy(
                src_ref=gram_ref.at[origin], dst_ref=got_gram.at[origin], send_sem=sem_a.at[1, shift],
                recv_sem=sem_b.at[1, origin], device_id={"bin": origin},
                device_id_type=pl.DeviceIdType.MESH,
            ),
        )

    def result_copy(shift):
        target = (me + shift) % count
        return remote(out_ref, out_ref, sem_c, sem_d, shift, me, target)

    def result_arrival(shift):
        origin = (me + count - shift) % count
        return remote(out_ref, out_ref, sem_c, sem_d, shift, origin, origin)

    for shift in range(1, count):
        for copy in partial_copies(shift):
            copy.start()
    cross = cross_ref[me]
    fac_gram = gram_ref[me]
    for shift in range(1, count):
        origin = (me + count - shift) % count
        for copy in partial_arrivals(shift):
            copy.wait_recv()
        cross = cross + got[origin]
        fac_gram = fac_gram + got_gram[origin]
    rows = cross.shape[0]
    own = load_ref[pl.ds(pl.multiple_of(me * rows, rows), rows), :]
    denom = jnp.dot(
        fac_gram, load_ref[...], precision=lax.Precision.HIGHEST,
        preferred_element_type=jnp.float32,
    )
    out_ref[me] = own * cross / denom
    for shift in range(1, count):
        for copy in partial_copies(shift):
            copy.wait_send()
    for shift in range(1, count):
        result_copy(shift).start()
    for shift in range(1, count):
        result_arrival(shift).wait_recv()
    for shift in range(1, count):
        result_copy(shift).wait_send()


def loadings_update(cross_parts, gram_parts, loadings, collective_id):
    count, rows, genes = cross_parts.shape
    vmem = pl.BlockSpec(memory_space=pltpu.VMEM)
    return pl.pallas_call(
        functools.partial(loadings_kernel, count),
        out_shape=jax.ShapeDtypeStruct((count, rows, genes), loadings.dtype),
        in_specs=[vmem, vmem, vmem],
        out_specs=vmem,
        scratch_shapes=[
            pltpu.VMEM(cross_parts.shape, cross_parts.dtype),
            pltpu.VMEM(gram_parts.shape, gram_parts.dtype),
            pltpu.SemaphoreType.DMA((2, count)),
            pltpu.SemaphoreType.DMA((2, count)),
            pltpu.SemaphoreType.DMA((count,)),
            pltpu.SemaphoreType.DMA((count,)),
        ],
        compiler_params=pltpu.CompilerParams(
            collective_id=collective_id, has_side_effects=True
        ),
    )(cross_parts, gram_parts, loadings)


def split_three(values):
    high = lax.reduce_precision(values, exponent_bits=8, mantissa_bits=7)
    rest = values - high
    mid = lax.reduce_precision(rest, exponent_bits=8, mantissa_bits=7)
    low = rest - mid
    return jnp.concatenate([high, mid, low], 1).astype(jnp.bfloat16)


def join_three(parts, width):
    return (parts[:, :width] + parts[:, width : 2 * width]) + parts[:, 2 * width :]


def stencil_term(own, position, edge_codes):
    bin_count = lax.axis_size("bin")
    row_count, width = own.shape
    group_size = row_count // bin_count
    grid_rows, grid_cols = edge_codes.shape
    payload = jnp.concatenate([own, position.astype(jnp.float32)[:, None]], 1)
    got = lax.all_to_all(
        payload.reshape(bin_count, group_size * (width + 1)), "bin", 0, 0, tiled=True
    ).reshape(row_count, width + 1)
    tile_slot = got[:, width].astype(jnp.int32) - lax.axis_index("bin") * row_count
    cells = lax.broadcasted_iota(jnp.int32, (row_count, row_count), 1)
    onehot = (tile_slot[:, None] == cells).astype(jnp.bfloat16)
    placed = lax.dot_general(
        onehot, split_three(got[:, :width]), (((0,), (0,)), ((), ())),
        preferred_element_type=jnp.float32,
    )
    tile_rows = join_three(placed, width)
    cell_scale = edge_codes.astype(jnp.float32) / 8.0
    weighted = cell_scale[:, :, None] * tile_rows.reshape(grid_rows, grid_cols, width)
    rim_last, rim_first = (weighted[-1], weighted[0])
    upper_rows, upper_scale = passed_along((rim_last, cell_scale[-1]), "bin", 1)
    lower_rows, lower_scale = passed_along((rim_first, cell_scale[0]), "bin", -1)
    degree_grid = (
        cell_scale * neighbour_first(cell_scale[None], upper_scale[None], lower_scale[None])[0]
    )
    smooth_grid = cell_scale[:, :, None] * neighbour_sum(weighted, upper_rows, lower_rows)
    back = jnp.concatenate(
        [smooth_grid.reshape(row_count, width), degree_grid.reshape(row_count, 1)], 1
    )
    back_rows = join_three(
        jnp.dot(onehot, split_three(back), preferred_element_type=jnp.float32), width + 1
    )
    ret = lax.all_to_all(
        back_rows.reshape(bin_count, group_size * (width + 1)), "bin", 0, 0, tiled=True
    ).reshape(row_count, width + 1)
    return (ret[:, :width], ret[:, width])


def on_device(counts, factors, loadings, position, edge_codes):
    bin_count = lax.axis_size("bin")
    gene_count = lax.axis_size("gene")
    row_count, width_all = factors.shape
    width = width_all // gene_count
    k_rows = width_all // bin_count
    gene_at = lax.axis_index("gene")
    bin_at = lax.axis_index("bin")
    load_bf = loadings.astype(jnp.bfloat16)
    right_dims = (((1,), (1,)), ((), ()))
    numer_part = lax.dot_general(load_bf, counts, right_dims, preferred_element_type=jnp.float32)
    gram_part = lax.dot_general(load_bf, load_bf, right_dims, preferred_element_type=jnp.float32)
    both = jnp.concatenate([numer_part, gram_part], 1)
    both = lax.psum_scatter(
        both.reshape(gene_count, width, -1), "gene", scatter_dimension=0, tiled=True
    ).reshape(width, -1)
    numer_t, gram_rows = both[:, :row_count], both[:, row_count:]
    own = lax.dynamic_slice_in_dim(factors, gene_at * width, width, 1)
    smooth, degree = stencil_term(own, position, edge_codes)
    penalty = float(G * K) / 64.0
    own_t = own.T
    denom_t = (
        lax.dot_general(gram_rows, factors, right_dims, precision=lax.Precision.HIGHEST)
        + penalty * degree[None, :] * own_t
    )
    new_t = own_t * (numer_t + penalty * smooth.T) / denom_t
    factors_t, fac_bf_t = factor_gather(new_t, 0)
    factors_new = factors_t.reshape(width_all, row_count).T
    fac_bf_t = fac_bf_t.reshape(width_all, row_count)
    cross_part = jnp.dot(fac_bf_t, counts, preferred_element_type=jnp.float32)
    fgram_part = lax.dot_general(fac_bf_t, fac_bf_t, right_dims, preferred_element_type=jnp.float32)
    loadings_new = loadings_update(
        cross_part.reshape(bin_count, k_rows, -1),
        fgram_part.reshape(bin_count, k_rows, -1),
        loadings,
        2,
    ).reshape(width_all, -1)
    return (factors_new, loadings_new)


def solution(mesh):
    placed = (P("bin", "gene"), P("bin", None), P(None, "gene"), P("bin"), P("bin", None))
    return jax.shard_map(
        on_device,
        mesh=mesh,
        in_specs=placed,
        out_specs=(P("bin", None), P(None, "gene")),
        check_vma=False,
    )
```

```python
import functools

import jax
import jax.numpy as jnp
from jax import lax
from jax.experimental import pallas as pl
from jax.experimental.pallas import tpu as pltpu
from jax.sharding import PartitionSpec as P

K = 256
G = 18432


def passed_along(block, axis, distance):
    devices = range(lax.axis_size(axis))
    route = [(i - distance, i) for i in devices if i - distance in devices]
    return lax.ppermute(block, axis, route)


def neighbour_sum(values, from_above, from_below):
    upper = jnp.concatenate([from_above[None], values[:-1]], 0)
    lower = jnp.concatenate([values[1:], from_below[None]], 0)
    beside = jnp.pad(values[:, 1:], ((0, 0), (0, 1), (0, 0))) + jnp.pad(
        values[:, :-1], ((0, 0), (1, 0), (0, 0))
    )
    return beside + 0.5 * (lower + upper)


def neighbour_first(values, from_above, from_below):
    upper = jnp.concatenate([from_above[:, None], values[:, :-1]], 1)
    lower = jnp.concatenate([values[:, 1:], from_below[:, None]], 1)
    beside = jnp.pad(values[:, :, 1:], ((0, 0), (0, 0), (0, 1))) + jnp.pad(
        values[:, :, :-1], ((0, 0), (0, 0), (1, 0))
    )
    return beside + 0.5 * (lower + upper)


def gray(value):
    return value + (value // 2) * (1 - 2 * (value % 2))


def gene_at_place(place, count):
    wide = 1 - ((place + count - 1) % count) // (count // 2)
    row = wide * (place - 1) + (1 - wide) * ((count - place) % count)
    return 2 * row + wide


def gene_place(index, count):
    row, wide = index // 2, index % 2
    return wide * (1 + row) + (1 - wide) * ((count - row) % count)


def bin_at_place(place, count):
    plane, step = place // 4, place % 4
    turned = step + (plane % 2) * (3 - 2 * step)
    return plane * 4 + gray(turned)


def bin_place(index, count):
    plane = index // 4
    turned = gray(index % 4)
    return plane * 4 + turned + (plane % 2) * (3 - 2 * turned)


RINGS = {"gene": (gene_at_place, gene_place), "bin": (bin_at_place, bin_place)}


def ring_peers(axis, count):
    at_place, place_of = RINGS[axis]
    place = place_of(lax.axis_index(axis), count)
    return place, (lambda shift: at_place((place + shift + count) % count, count))


def enter(axis, peers):
    barrier = pltpu.get_barrier_semaphore()
    for peer in peers:
        pl.semaphore_signal(barrier, inc=1, device_id={axis: peer},
                            device_id_type=pl.DeviceIdType.MESH)
    pl.semaphore_wait(barrier, len(peers))


def gather_kernel(axis, count, x_ref, out_ref, send_sem, recv_sem):
    place, member = ring_peers(axis, count)
    ahead, behind = member(1), member(-1)
    half = x_ref.shape[0] // 2
    enter(axis, (ahead, behind))
    out_ref[member(0)] = x_ref[...]

    def copy(step, way):
        rows = pl.ds(way * half, half)
        origin = member(-step) if way == 0 else member(step)
        src = x_ref.at[rows] if step == 0 else out_ref.at[origin, rows]
        return pltpu.make_async_remote_copy(
            src_ref=src,
            dst_ref=out_ref.at[origin, rows],
            send_sem=send_sem.at[way, step],
            recv_sem=recv_sem.at[way, step],
            device_id={axis: ahead if way == 0 else behind},
            device_id_type=pl.DeviceIdType.MESH,
        )

    for step in range(count - 1):
        for way in (0, 1):
            if step >= 1:
                copy(step - 1, way).wait_recv()
            copy(step, way).start()
    for way in (0, 1):
        copy(count - 2, way).wait_recv()
    for step in range(count - 1):
        for way in (0, 1):
            copy(step, way).wait_send()


def ring_gather(x, axis, collective_id):
    count = lax.axis_size(axis)
    return pl.pallas_call(
        functools.partial(gather_kernel, axis, count),
        out_shape=jax.ShapeDtypeStruct((count,) + x.shape, x.dtype),
        in_specs=[pl.BlockSpec(memory_space=pltpu.VMEM)],
        out_specs=pl.BlockSpec(memory_space=pltpu.VMEM),
        scratch_shapes=[
            pltpu.SemaphoreType.DMA((2, count - 1)),
            pltpu.SemaphoreType.DMA((2, count - 1)),
        ],
        compiler_params=pltpu.CompilerParams(
            collective_id=collective_id, has_side_effects=True
        ),
    )(x)


def scatter_kernel(axis, count, x_ref, out_ref, got, sent, send_sem, recv_sem):
    place, member = ring_peers(axis, count)
    ahead, behind = member(1), member(-1)
    half = x_ref.shape[2] // 2
    enter(axis, (ahead, behind))

    def copy(step, way):
        lanes = pl.ds(way * half, half)
        if step == 0:
            source = x_ref.at[member(-1) if way == 0 else member(1), :, lanes]
        else:
            source = sent.at[way, step]
        return pltpu.make_async_remote_copy(
            src_ref=source,
            dst_ref=got.at[way, step],
            send_sem=send_sem.at[way, step],
            recv_sem=recv_sem.at[way, step],
            device_id={axis: ahead if way == 0 else behind},
            device_id_type=pl.DeviceIdType.MESH,
        )

    for step in range(count - 1):
        for way in (0, 1):
            if step >= 1:
                lanes = pl.ds(way * half, half)
                owner = member(-step - 1) if way == 0 else member(step + 1)
                copy(step - 1, way).wait_recv()
                sent[way, step] = got[way, step - 1] + x_ref[owner, :, lanes]
            copy(step, way).start()
    for way in (0, 1):
        lanes = pl.ds(way * half, half)
        copy(count - 2, way).wait_recv()
        out_ref[:, lanes] = got[way, count - 2] + x_ref[member(0), :, lanes]
    for step in range(count - 1):
        for way in (0, 1):
            copy(step, way).wait_send()


def ring_scatter(x, axis, collective_id):
    count, rows, lanes = x.shape
    return pl.pallas_call(
        functools.partial(scatter_kernel, axis, count),
        out_shape=jax.ShapeDtypeStruct((rows, lanes), x.dtype),
        in_specs=[pl.BlockSpec(memory_space=pltpu.VMEM)],
        out_specs=pl.BlockSpec(memory_space=pltpu.VMEM),
        scratch_shapes=[
            pltpu.VMEM((2, count - 1, rows, lanes // 2), x.dtype),
            pltpu.VMEM((2, count - 1, rows, lanes // 2), x.dtype),
            pltpu.SemaphoreType.DMA((2, count - 1)),
            pltpu.SemaphoreType.DMA((2, count - 1)),
        ],
        compiler_params=pltpu.CompilerParams(
            collective_id=collective_id, has_side_effects=True
        ),
    )(x)


def greet_all(axis, me, count):
    barrier = pltpu.get_barrier_semaphore()
    for shift in range(1, count):
        pl.semaphore_signal(barrier, inc=1, device_id={axis: (me + shift) % count},
                            device_id_type=pl.DeviceIdType.MESH)
    pl.semaphore_wait(barrier, count - 1)


def exchange_kernel(axis, count, summed, x_ref, out_ref, *rest):
    if summed:
        got, send_sem, recv_sem = rest
    else:
        got, (send_sem, recv_sem) = out_ref, rest
    me = lax.axis_index(axis)
    greet_all(axis, me, count)

    def copy(shift):
        target = (me + shift) % count
        return pltpu.make_async_remote_copy(
            src_ref=x_ref.at[target] if summed else x_ref,
            dst_ref=got.at[me],
            send_sem=send_sem.at[shift],
            recv_sem=recv_sem.at[me],
            device_id={axis: target},
            device_id_type=pl.DeviceIdType.MESH,
        )

    def arrival(shift):
        origin = (me + count - shift) % count
        return pltpu.make_async_remote_copy(
            src_ref=x_ref.at[origin] if summed else x_ref,
            dst_ref=got.at[origin],
            send_sem=send_sem.at[shift],
            recv_sem=recv_sem.at[origin],
            device_id={axis: origin},
            device_id_type=pl.DeviceIdType.MESH,
        )

    for shift in range(1, count):
        copy(shift).start()
    if summed:
        total = x_ref[me]
        for shift in range(1, count):
            arrival(shift).wait_recv()
            total = total + got[(me + count - shift) % count]
        out_ref[...] = total
    else:
        out_ref[me] = x_ref[...]
        for shift in range(1, count):
            arrival(shift).wait_recv()
    for shift in range(1, count):
        copy(shift).wait_send()


def exchange(x, axis, collective_id, summed):
    count = lax.axis_size(axis)
    if summed:
        out_shape = x.shape[1:]
        scratch = [pltpu.VMEM(x.shape, x.dtype)]
    else:
        out_shape = (count,) + x.shape
        scratch = []
    return pl.pallas_call(
        functools.partial(exchange_kernel, axis, count, summed),
        out_shape=jax.ShapeDtypeStruct(out_shape, x.dtype),
        in_specs=[pl.BlockSpec(memory_space=pltpu.VMEM)],
        out_specs=pl.BlockSpec(memory_space=pltpu.VMEM),
        scratch_shapes=scratch + [
            pltpu.SemaphoreType.DMA((count,)),
            pltpu.SemaphoreType.DMA((count,)),
        ],
        compiler_params=pltpu.CompilerParams(
            collective_id=collective_id, has_side_effects=True
        ),
    )(x)


def loadings_kernel(count, cross_ref, gram_ref, load_ref, out_ref, got, got_gram, sem_a, sem_b, sem_c, sem_d):
    me = lax.axis_index("bin")
    greet_all("bin", me, count)

    def remote(src, dst, send, recv, shift, index, peer):
        return pltpu.make_async_remote_copy(
            src_ref=src.at[index],
            dst_ref=dst.at[index],
            send_sem=send.at[shift],
            recv_sem=recv.at[index],
            device_id={"bin": peer},
            device_id_type=pl.DeviceIdType.MESH,
        )

    def partial_copies(shift):
        target = (me + shift) % count
        return (
            pltpu.make_async_remote_copy(
                src_ref=cross_ref.at[target], dst_ref=got.at[me], send_sem=sem_a.at[0, shift],
                recv_sem=sem_b.at[0, me], device_id={"bin": target},
                device_id_type=pl.DeviceIdType.MESH,
            ),
            pltpu.make_async_remote_copy(
                src_ref=gram_ref.at[target], dst_ref=got_gram.at[me], send_sem=sem_a.at[1, shift],
                recv_sem=sem_b.at[1, me], device_id={"bin": target},
                device_id_type=pl.DeviceIdType.MESH,
            ),
        )

    def partial_arrivals(shift):
        origin = (me + count - shift) % count
        return (
            pltpu.make_async_remote_copy(
                src_ref=cross_ref.at[origin], dst_ref=got.at[origin], send_sem=sem_a.at[0, shift],
                recv_sem=sem_b.at[0, origin], device_id={"bin": origin},
                device_id_type=pl.DeviceIdType.MESH,
            ),
            pltpu.make_async_remote_copy(
                src_ref=gram_ref.at[origin], dst_ref=got_gram.at[origin], send_sem=sem_a.at[1, shift],
                recv_sem=sem_b.at[1, origin], device_id={"bin": origin},
                device_id_type=pl.DeviceIdType.MESH,
            ),
        )

    def result_copy(shift):
        target = (me + shift) % count
        return remote(out_ref, out_ref, sem_c, sem_d, shift, me, target)

    def result_arrival(shift):
        origin = (me + count - shift) % count
        return remote(out_ref, out_ref, sem_c, sem_d, shift, origin, origin)

    for shift in range(1, count):
        for copy in partial_copies(shift):
            copy.start()
    cross = cross_ref[me]
    fac_gram = gram_ref[me]
    for shift in range(1, count):
        origin = (me + count - shift) % count
        for copy in partial_arrivals(shift):
            copy.wait_recv()
        cross = cross + got[origin]
        fac_gram = fac_gram + got_gram[origin]
    rows = cross.shape[0]
    own = load_ref[pl.ds(pl.multiple_of(me * rows, rows), rows), :]
    denom = jnp.dot(
        fac_gram, load_ref[...], precision=lax.Precision.HIGHEST,
        preferred_element_type=jnp.float32,
    )
    out_ref[me] = own * cross / denom
    for shift in range(1, count):
        for copy in partial_copies(shift):
            copy.wait_send()
    for shift in range(1, count):
        result_copy(shift).start()
    for shift in range(1, count):
        result_arrival(shift).wait_recv()
    for shift in range(1, count):
        result_copy(shift).wait_send()


def loadings_update(cross_parts, gram_parts, loadings, collective_id):
    count, rows, genes = cross_parts.shape
    vmem = pl.BlockSpec(memory_space=pltpu.VMEM)
    return pl.pallas_call(
        functools.partial(loadings_kernel, count),
        out_shape=jax.ShapeDtypeStruct((count, rows, genes), loadings.dtype),
        in_specs=[vmem, vmem, vmem],
        out_specs=vmem,
        scratch_shapes=[
            pltpu.VMEM(cross_parts.shape, cross_parts.dtype),
            pltpu.VMEM(gram_parts.shape, gram_parts.dtype),
            pltpu.SemaphoreType.DMA((2, count)),
            pltpu.SemaphoreType.DMA((2, count)),
            pltpu.SemaphoreType.DMA((count,)),
            pltpu.SemaphoreType.DMA((count,)),
        ],
        compiler_params=pltpu.CompilerParams(
            collective_id=collective_id, has_side_effects=True
        ),
    )(cross_parts, gram_parts, loadings)


def split_three(values):
    high = lax.reduce_precision(values, exponent_bits=8, mantissa_bits=7)
    rest = values - high
    mid = lax.reduce_precision(rest, exponent_bits=8, mantissa_bits=7)
    low = rest - mid
    return jnp.concatenate([high, mid, low], 1).astype(jnp.bfloat16)


def join_three(parts, width):
    return (parts[:, :width] + parts[:, width : 2 * width]) + parts[:, 2 * width :]


def stencil_term(own, position, edge_codes):
    bin_count = lax.axis_size("bin")
    row_count, width = own.shape
    group_size = row_count // bin_count
    grid_rows, grid_cols = edge_codes.shape
    payload = jnp.concatenate([own, position.astype(jnp.float32)[:, None]], 1)
    got = lax.all_to_all(
        payload.reshape(bin_count, group_size * (width + 1)), "bin", 0, 0, tiled=True
    ).reshape(row_count, width + 1)
    tile_slot = got[:, width].astype(jnp.int32) - lax.axis_index("bin") * row_count
    cells = lax.broadcasted_iota(jnp.int32, (row_count, row_count), 1)
    onehot = (tile_slot[:, None] == cells).astype(jnp.bfloat16)
    placed = lax.dot_general(
        onehot, split_three(got[:, :width]), (((0,), (0,)), ((), ())),
        preferred_element_type=jnp.float32,
    )
    tile_rows = join_three(placed, width)
    cell_scale = edge_codes.astype(jnp.float32) / 8.0
    weighted = cell_scale[:, :, None] * tile_rows.reshape(grid_rows, grid_cols, width)
    rim_last, rim_first = (weighted[-1], weighted[0])
    upper = passed_along(jnp.concatenate([rim_last, cell_scale[-1][:, None]], 1), "bin", 1)
    lower = passed_along(jnp.concatenate([rim_first, cell_scale[0][:, None]], 1), "bin", -1)
    upper_rows, upper_scale = upper[:, :width], upper[:, width]
    lower_rows, lower_scale = lower[:, :width], lower[:, width]
    degree_grid = (
        cell_scale * neighbour_first(cell_scale[None], upper_scale[None], lower_scale[None])[0]
    )
    smooth_grid = cell_scale[:, :, None] * neighbour_sum(weighted, upper_rows, lower_rows)
    back = jnp.concatenate(
        [smooth_grid.reshape(row_count, width), degree_grid.reshape(row_count, 1)], 1
    )
    back_rows = join_three(
        jnp.dot(onehot, split_three(back), preferred_element_type=jnp.float32), width + 1
    )
    ret = lax.all_to_all(
        back_rows.reshape(bin_count, group_size * (width + 1)), "bin", 0, 0, tiled=True
    ).reshape(row_count, width + 1)
    return (ret[:, :width], ret[:, width])


def on_device(counts, factors, loadings, position, edge_codes):
    bin_count = lax.axis_size("bin")
    gene_count = lax.axis_size("gene")
    row_count, width_all = factors.shape
    width = width_all // gene_count
    k_rows = width_all // bin_count
    gene_at = lax.axis_index("gene")
    bin_at = lax.axis_index("bin")
    load_bf = loadings.astype(jnp.bfloat16)
    right_dims = (((1,), (1,)), ((), ()))
    numer_part = lax.dot_general(load_bf, counts, right_dims, preferred_element_type=jnp.float32)
    gram_part = lax.dot_general(load_bf, load_bf, right_dims, preferred_element_type=jnp.float32)
    both = jnp.concatenate([numer_part, gram_part], 1)
    both = lax.psum_scatter(
        both.reshape(gene_count, width, -1), "gene", scatter_dimension=0, tiled=True
    ).reshape(width, -1)
    numer_t, gram_rows = both[:, :row_count], both[:, row_count:]
    own = lax.dynamic_slice_in_dim(factors, gene_at * width, width, 1)
    smooth, degree = stencil_term(own, position, edge_codes)
    penalty = float(G * K) / 64.0
    own_t = own.T
    denom_t = (
        lax.dot_general(gram_rows, factors, right_dims, precision=lax.Precision.HIGHEST)
        + penalty * degree[None, :] * own_t
    )
    new_t = own_t * (numer_t + penalty * smooth.T) / denom_t
    factors_t = exchange(new_t, "gene", 0, False).reshape(width_all, row_count)
    factors_new = factors_t.T
    fac_bf_t = factors_t.astype(jnp.bfloat16)
    cross_part = jnp.dot(fac_bf_t, counts, preferred_element_type=jnp.float32)
    fgram_part = lax.dot_general(fac_bf_t, fac_bf_t, right_dims, preferred_element_type=jnp.float32)
    loadings_new = loadings_update(
        cross_part.reshape(bin_count, k_rows, -1),
        fgram_part.reshape(bin_count, k_rows, -1),
        loadings,
        2,
    ).reshape(width_all, -1)
    return (factors_new, loadings_new)


def solution(mesh):
    placed = (P("bin", "gene"), P("bin", None), P(None, "gene"), P("bin"), P("bin", None))
    return jax.shard_map(
        on_device,
        mesh=mesh,
        in_specs=placed,
        out_specs=(P("bin", None), P(None, "gene")),
        check_vma=False,
    )
```

```python
import functools

import jax
import jax.numpy as jnp
from jax import lax
from jax.experimental import pallas as pl
from jax.experimental.pallas import tpu as pltpu
from jax.sharding import PartitionSpec as P

K = 256
G = 18432


def passed_along(block, axis, distance):
    devices = range(lax.axis_size(axis))
    route = [(i - distance, i) for i in devices if i - distance in devices]
    return lax.ppermute(block, axis, route)


def neighbour_sum(values, from_above, from_below):
    upper = jnp.concatenate([from_above[None], values[:-1]], 0)
    lower = jnp.concatenate([values[1:], from_below[None]], 0)
    beside = jnp.pad(values[:, 1:], ((0, 0), (0, 1), (0, 0))) + jnp.pad(
        values[:, :-1], ((0, 0), (1, 0), (0, 0))
    )
    return beside + 0.5 * (lower + upper)


def neighbour_first(values, from_above, from_below):
    upper = jnp.concatenate([from_above[:, None], values[:, :-1]], 1)
    lower = jnp.concatenate([values[:, 1:], from_below[:, None]], 1)
    beside = jnp.pad(values[:, :, 1:], ((0, 0), (0, 0), (0, 1))) + jnp.pad(
        values[:, :, :-1], ((0, 0), (0, 0), (1, 0))
    )
    return beside + 0.5 * (lower + upper)


def gray(value):
    return value + (value // 2) * (1 - 2 * (value % 2))


def gene_at_place(place, count):
    wide = 1 - ((place + count - 1) % count) // (count // 2)
    row = wide * (place - 1) + (1 - wide) * ((count - place) % count)
    return 2 * row + wide


def gene_place(index, count):
    row, wide = index // 2, index % 2
    return wide * (1 + row) + (1 - wide) * ((count - row) % count)


def bin_at_place(place, count):
    plane, step = place // 4, place % 4
    turned = step + (plane % 2) * (3 - 2 * step)
    return plane * 4 + gray(turned)


def bin_place(index, count):
    plane = index // 4
    turned = gray(index % 4)
    return plane * 4 + turned + (plane % 2) * (3 - 2 * turned)


RINGS = {"gene": (gene_at_place, gene_place), "bin": (bin_at_place, bin_place)}


def ring_peers(axis, count):
    at_place, place_of = RINGS[axis]
    place = place_of(lax.axis_index(axis), count)
    return place, (lambda shift: at_place((place + shift + count) % count, count))


def enter(axis, peers):
    barrier = pltpu.get_barrier_semaphore()
    for peer in peers:
        pl.semaphore_signal(barrier, inc=1, device_id={axis: peer},
                            device_id_type=pl.DeviceIdType.MESH)
    pl.semaphore_wait(barrier, len(peers))


def gather_kernel(axis, count, x_ref, out_ref, send_sem, recv_sem):
    place, member = ring_peers(axis, count)
    ahead, behind = member(1), member(-1)
    half = x_ref.shape[0] // 2
    enter(axis, (ahead, behind))
    out_ref[member(0)] = x_ref[...]

    def copy(step, way):
        rows = pl.ds(way * half, half)
        origin = member(-step) if way == 0 else member(step)
        src = x_ref.at[rows] if step == 0 else out_ref.at[origin, rows]
        return pltpu.make_async_remote_copy(
            src_ref=src,
            dst_ref=out_ref.at[origin, rows],
            send_sem=send_sem.at[way, step],
            recv_sem=recv_sem.at[way, step],
            device_id={axis: ahead if way == 0 else behind},
            device_id_type=pl.DeviceIdType.MESH,
        )

    for step in range(count - 1):
        for way in (0, 1):
            if step >= 1:
                copy(step - 1, way).wait_recv()
            copy(step, way).start()
    for way in (0, 1):
        copy(count - 2, way).wait_recv()
    for step in range(count - 1):
        for way in (0, 1):
            copy(step, way).wait_send()


def ring_gather(x, axis, collective_id):
    count = lax.axis_size(axis)
    return pl.pallas_call(
        functools.partial(gather_kernel, axis, count),
        out_shape=jax.ShapeDtypeStruct((count,) + x.shape, x.dtype),
        in_specs=[pl.BlockSpec(memory_space=pltpu.VMEM)],
        out_specs=pl.BlockSpec(memory_space=pltpu.VMEM),
        scratch_shapes=[
            pltpu.SemaphoreType.DMA((2, count - 1)),
            pltpu.SemaphoreType.DMA((2, count - 1)),
        ],
        compiler_params=pltpu.CompilerParams(
            collective_id=collective_id, has_side_effects=True
        ),
    )(x)


def scatter_kernel(axis, count, x_ref, out_ref, got, sent, send_sem, recv_sem):
    place, member = ring_peers(axis, count)
    ahead, behind = member(1), member(-1)
    half = x_ref.shape[2] // 2
    enter(axis, (ahead, behind))

    def copy(step, way):
        lanes = pl.ds(way * half, half)
        if step == 0:
            source = x_ref.at[member(-1) if way == 0 else member(1), :, lanes]
        else:
            source = sent.at[way, step]
        return pltpu.make_async_remote_copy(
            src_ref=source,
            dst_ref=got.at[way, step],
            send_sem=send_sem.at[way, step],
            recv_sem=recv_sem.at[way, step],
            device_id={axis: ahead if way == 0 else behind},
            device_id_type=pl.DeviceIdType.MESH,
        )

    for step in range(count - 1):
        for way in (0, 1):
            if step >= 1:
                lanes = pl.ds(way * half, half)
                owner = member(-step - 1) if way == 0 else member(step + 1)
                copy(step - 1, way).wait_recv()
                sent[way, step] = got[way, step - 1] + x_ref[owner, :, lanes]
            copy(step, way).start()
    for way in (0, 1):
        lanes = pl.ds(way * half, half)
        copy(count - 2, way).wait_recv()
        out_ref[:, lanes] = got[way, count - 2] + x_ref[member(0), :, lanes]
    for step in range(count - 1):
        for way in (0, 1):
            copy(step, way).wait_send()


def ring_scatter(x, axis, collective_id):
    count, rows, lanes = x.shape
    return pl.pallas_call(
        functools.partial(scatter_kernel, axis, count),
        out_shape=jax.ShapeDtypeStruct((rows, lanes), x.dtype),
        in_specs=[pl.BlockSpec(memory_space=pltpu.VMEM)],
        out_specs=pl.BlockSpec(memory_space=pltpu.VMEM),
        scratch_shapes=[
            pltpu.VMEM((2, count - 1, rows, lanes // 2), x.dtype),
            pltpu.VMEM((2, count - 1, rows, lanes // 2), x.dtype),
            pltpu.SemaphoreType.DMA((2, count - 1)),
            pltpu.SemaphoreType.DMA((2, count - 1)),
        ],
        compiler_params=pltpu.CompilerParams(
            collective_id=collective_id, has_side_effects=True
        ),
    )(x)


def greet_all(axis, me, count):
    barrier = pltpu.get_barrier_semaphore()
    for shift in range(1, count):
        pl.semaphore_signal(barrier, inc=1, device_id={axis: (me + shift) % count},
                            device_id_type=pl.DeviceIdType.MESH)
    pl.semaphore_wait(barrier, count - 1)


def exchange_kernel(axis, count, summed, x_ref, out_ref, *rest):
    if summed:
        got, send_sem, recv_sem = rest
    else:
        got, (send_sem, recv_sem) = out_ref, rest
    me = lax.axis_index(axis)
    greet_all(axis, me, count)

    def copy(shift):
        target = (me + shift) % count
        return pltpu.make_async_remote_copy(
            src_ref=x_ref.at[target] if summed else x_ref,
            dst_ref=got.at[me],
            send_sem=send_sem.at[shift],
            recv_sem=recv_sem.at[me],
            device_id={axis: target},
            device_id_type=pl.DeviceIdType.MESH,
        )

    def arrival(shift):
        origin = (me + count - shift) % count
        return pltpu.make_async_remote_copy(
            src_ref=x_ref.at[origin] if summed else x_ref,
            dst_ref=got.at[origin],
            send_sem=send_sem.at[shift],
            recv_sem=recv_sem.at[origin],
            device_id={axis: origin},
            device_id_type=pl.DeviceIdType.MESH,
        )

    for shift in range(1, count):
        copy(shift).start()
    if summed:
        total = x_ref[me]
        for shift in range(1, count):
            arrival(shift).wait_recv()
            total = total + got[(me + count - shift) % count]
        out_ref[...] = total
    else:
        out_ref[me] = x_ref[...]
        for shift in range(1, count):
            arrival(shift).wait_recv()
    for shift in range(1, count):
        copy(shift).wait_send()


def exchange(x, axis, collective_id, summed):
    count = lax.axis_size(axis)
    if summed:
        out_shape = x.shape[1:]
        scratch = [pltpu.VMEM(x.shape, x.dtype)]
    else:
        out_shape = (count,) + x.shape
        scratch = []
    return pl.pallas_call(
        functools.partial(exchange_kernel, axis, count, summed),
        out_shape=jax.ShapeDtypeStruct(out_shape, x.dtype),
        in_specs=[pl.BlockSpec(memory_space=pltpu.VMEM)],
        out_specs=pl.BlockSpec(memory_space=pltpu.VMEM),
        scratch_shapes=scratch + [
            pltpu.SemaphoreType.DMA((count,)),
            pltpu.SemaphoreType.DMA((count,)),
        ],
        compiler_params=pltpu.CompilerParams(
            collective_id=collective_id, has_side_effects=True
        ),
    )(x)


def loadings_kernel(count, cross_ref, gram_ref, load_ref, out_ref, got, got_gram, sem_a, sem_b, sem_c, sem_d):
    me = lax.axis_index("bin")
    greet_all("bin", me, count)

    def remote(src, dst, send, recv, shift, index, peer):
        return pltpu.make_async_remote_copy(
            src_ref=src.at[index],
            dst_ref=dst.at[index],
            send_sem=send.at[shift],
            recv_sem=recv.at[index],
            device_id={"bin": peer},
            device_id_type=pl.DeviceIdType.MESH,
        )

    def partial_copies(shift):
        target = (me + shift) % count
        return (
            pltpu.make_async_remote_copy(
                src_ref=cross_ref.at[target], dst_ref=got.at[me], send_sem=sem_a.at[0, shift],
                recv_sem=sem_b.at[0, me], device_id={"bin": target},
                device_id_type=pl.DeviceIdType.MESH,
            ),
            pltpu.make_async_remote_copy(
                src_ref=gram_ref.at[target], dst_ref=got_gram.at[me], send_sem=sem_a.at[1, shift],
                recv_sem=sem_b.at[1, me], device_id={"bin": target},
                device_id_type=pl.DeviceIdType.MESH,
            ),
        )

    def partial_arrivals(shift):
        origin = (me + count - shift) % count
        return (
            pltpu.make_async_remote_copy(
                src_ref=cross_ref.at[origin], dst_ref=got.at[origin], send_sem=sem_a.at[0, shift],
                recv_sem=sem_b.at[0, origin], device_id={"bin": origin},
                device_id_type=pl.DeviceIdType.MESH,
            ),
            pltpu.make_async_remote_copy(
                src_ref=gram_ref.at[origin], dst_ref=got_gram.at[origin], send_sem=sem_a.at[1, shift],
                recv_sem=sem_b.at[1, origin], device_id={"bin": origin},
                device_id_type=pl.DeviceIdType.MESH,
            ),
        )

    def result_copy(shift):
        target = (me + shift) % count
        return remote(out_ref, out_ref, sem_c, sem_d, shift, me, target)

    def result_arrival(shift):
        origin = (me + count - shift) % count
        return remote(out_ref, out_ref, sem_c, sem_d, shift, origin, origin)

    for shift in range(1, count):
        for copy in partial_copies(shift):
            copy.start()
    cross = cross_ref[me]
    fac_gram = gram_ref[me]
    for shift in range(1, count):
        origin = (me + count - shift) % count
        for copy in partial_arrivals(shift):
            copy.wait_recv()
        cross = cross + got[origin]
        fac_gram = fac_gram + got_gram[origin]
    rows = cross.shape[0]
    own = load_ref[pl.ds(pl.multiple_of(me * rows, rows), rows), :]
    denom = jnp.dot(
        fac_gram, load_ref[...], precision=lax.Precision.HIGHEST,
        preferred_element_type=jnp.float32,
    )
    out_ref[me] = own * cross / denom
    for shift in range(1, count):
        for copy in partial_copies(shift):
            copy.wait_send()
    for shift in range(1, count):
        result_copy(shift).start()
    for shift in range(1, count):
        result_arrival(shift).wait_recv()
    for shift in range(1, count):
        result_copy(shift).wait_send()


def loadings_update(cross_parts, gram_parts, loadings, collective_id):
    count, rows, genes = cross_parts.shape
    vmem = pl.BlockSpec(memory_space=pltpu.VMEM)
    return pl.pallas_call(
        functools.partial(loadings_kernel, count),
        out_shape=jax.ShapeDtypeStruct((count, rows, genes), loadings.dtype),
        in_specs=[vmem, vmem, vmem],
        out_specs=vmem,
        scratch_shapes=[
            pltpu.VMEM(cross_parts.shape, cross_parts.dtype),
            pltpu.VMEM(gram_parts.shape, gram_parts.dtype),
            pltpu.SemaphoreType.DMA((2, count)),
            pltpu.SemaphoreType.DMA((2, count)),
            pltpu.SemaphoreType.DMA((count,)),
            pltpu.SemaphoreType.DMA((count,)),
        ],
        compiler_params=pltpu.CompilerParams(
            collective_id=collective_id, has_side_effects=True
        ),
    )(cross_parts, gram_parts, loadings)


def split_three(values):
    high = lax.reduce_precision(values, exponent_bits=8, mantissa_bits=7)
    rest = values - high
    mid = lax.reduce_precision(rest, exponent_bits=8, mantissa_bits=7)
    low = rest - mid
    return jnp.concatenate([high, mid, low], 1).astype(jnp.bfloat16)


def join_three(parts, width):
    return (parts[:, :width] + parts[:, width : 2 * width]) + parts[:, 2 * width :]


def place_kernel(tile, slot_ref, parts_ref, out_ref):
    count = slot_ref.shape[1]

    def body(step, carry):
        start = pl.multiple_of(step * tile, tile)
        cells = start + lax.broadcasted_iota(jnp.int32, (tile, count), 0)
        onehot = (cells == slot_ref[...]).astype(jnp.bfloat16)
        out_ref[pl.ds(start, tile), :] = jnp.dot(
            onehot, parts_ref[...], preferred_element_type=jnp.float32
        )
        return carry

    lax.fori_loop(0, out_ref.shape[0] // tile, body, 0)


def fetch_kernel(tile, slot_ref, parts_ref, out_ref):
    count = slot_ref.shape[0]
    out_ref[...] = jnp.zeros(out_ref.shape, out_ref.dtype)

    def body(step, carry):
        start = pl.multiple_of(step * tile, tile)
        cells = start + lax.broadcasted_iota(jnp.int32, (count, tile), 1)
        onehot = (slot_ref[...] == cells).astype(jnp.bfloat16)
        out_ref[...] += jnp.dot(
            onehot, parts_ref[pl.ds(start, tile), :], preferred_element_type=jnp.float32
        )
        return carry

    lax.fori_loop(0, parts_ref.shape[0] // tile, body, 0)


def onehot_move(kernel, slot, parts, rows):
    vmem = pl.BlockSpec(memory_space=pltpu.VMEM)
    return pl.pallas_call(
        functools.partial(kernel, 256),
        out_shape=jax.ShapeDtypeStruct((rows, parts.shape[1]), jnp.float32),
        in_specs=[vmem, vmem],
        out_specs=vmem,
    )(slot, parts)


def stencil_term(own, position, edge_codes):
    bin_count = lax.axis_size("bin")
    row_count, width = own.shape
    group_size = row_count // bin_count
    grid_rows, grid_cols = edge_codes.shape
    payload = jnp.concatenate([own, position.astype(jnp.float32)[:, None]], 1)
    got = lax.all_to_all(
        payload.reshape(bin_count, group_size * (width + 1)), "bin", 0, 0, tiled=True
    ).reshape(row_count, width + 1)
    tile_slot = got[:, width].astype(jnp.int32) - lax.axis_index("bin") * row_count
    placed = onehot_move(place_kernel, tile_slot[None, :], split_three(got[:, :width]), row_count)
    tile_rows = join_three(placed, width)
    cell_scale = edge_codes.astype(jnp.float32) / 8.0
    weighted = cell_scale[:, :, None] * tile_rows.reshape(grid_rows, grid_cols, width)
    rim_last, rim_first = (weighted[-1], weighted[0])
    upper_rows, upper_scale = passed_along((rim_last, cell_scale[-1]), "bin", 1)
    lower_rows, lower_scale = passed_along((rim_first, cell_scale[0]), "bin", -1)
    degree_grid = (
        cell_scale * neighbour_first(cell_scale[None], upper_scale[None], lower_scale[None])[0]
    )
    smooth_grid = cell_scale[:, :, None] * neighbour_sum(weighted, upper_rows, lower_rows)
    back = jnp.concatenate(
        [smooth_grid.reshape(row_count, width), degree_grid.reshape(row_count, 1)], 1
    )
    back_rows = join_three(
        onehot_move(fetch_kernel, tile_slot[:, None], split_three(back), row_count), width + 1
    )
    ret = lax.all_to_all(
        back_rows.reshape(bin_count, group_size * (width + 1)), "bin", 0, 0, tiled=True
    ).reshape(row_count, width + 1)
    return (ret[:, :width], ret[:, width])


def on_device(counts, factors, loadings, position, edge_codes):
    bin_count = lax.axis_size("bin")
    gene_count = lax.axis_size("gene")
    row_count, width_all = factors.shape
    width = width_all // gene_count
    k_rows = width_all // bin_count
    gene_at = lax.axis_index("gene")
    bin_at = lax.axis_index("bin")
    load_bf = loadings.astype(jnp.bfloat16)
    right_dims = (((1,), (1,)), ((), ()))
    numer_part = lax.dot_general(load_bf, counts, right_dims, preferred_element_type=jnp.float32)
    gram_part = lax.dot_general(load_bf, load_bf, right_dims, preferred_element_type=jnp.float32)
    both = jnp.concatenate([numer_part, gram_part], 1)
    both = lax.psum_scatter(
        both.reshape(gene_count, width, -1), "gene", scatter_dimension=0, tiled=True
    ).reshape(width, -1)
    numer_t, gram_rows = both[:, :row_count], both[:, row_count:]
    own = lax.dynamic_slice_in_dim(factors, gene_at * width, width, 1)
    smooth, degree = stencil_term(own, position, edge_codes)
    penalty = float(G * K) / 64.0
    own_t = own.T
    denom_t = (
        lax.dot_general(gram_rows, factors, right_dims, precision=lax.Precision.HIGHEST)
        + penalty * degree[None, :] * own_t
    )
    new_t = own_t * (numer_t + penalty * smooth.T) / denom_t
    factors_t = exchange(new_t, "gene", 0, False).reshape(width_all, row_count)
    factors_new = factors_t.T
    fac_bf_t = factors_t.astype(jnp.bfloat16)
    cross_part = jnp.dot(fac_bf_t, counts, preferred_element_type=jnp.float32)
    fgram_part = lax.dot_general(fac_bf_t, fac_bf_t, right_dims, preferred_element_type=jnp.float32)
    loadings_new = loadings_update(
        cross_part.reshape(bin_count, k_rows, -1),
        fgram_part.reshape(bin_count, k_rows, -1),
        loadings,
        2,
    ).reshape(width_all, -1)
    return (factors_new, loadings_new)


def solution(mesh):
    placed = (P("bin", "gene"), P("bin", None), P(None, "gene"), P("bin"), P("bin", None))
    return jax.shard_map(
        on_device,
        mesh=mesh,
        in_specs=placed,
        out_specs=(P("bin", None), P(None, "gene")),
        check_vma=False,
    )
```

```python
import functools

import jax
import jax.numpy as jnp
from jax import lax
from jax.experimental import pallas as pl
from jax.experimental.pallas import tpu as pltpu
from jax.sharding import PartitionSpec as P

K = 256
G = 18432


def passed_along(block, axis, distance):
    devices = range(lax.axis_size(axis))
    route = [(i - distance, i) for i in devices if i - distance in devices]
    return lax.ppermute(block, axis, route)


def neighbour_sum(values, from_above, from_below):
    upper = jnp.concatenate([from_above[None], values[:-1]], 0)
    lower = jnp.concatenate([values[1:], from_below[None]], 0)
    beside = jnp.pad(values[:, 1:], ((0, 0), (0, 1), (0, 0))) + jnp.pad(
        values[:, :-1], ((0, 0), (1, 0), (0, 0))
    )
    return beside + 0.5 * (lower + upper)


def neighbour_first(values, from_above, from_below):
    upper = jnp.concatenate([from_above[:, None], values[:, :-1]], 1)
    lower = jnp.concatenate([values[:, 1:], from_below[:, None]], 1)
    beside = jnp.pad(values[:, :, 1:], ((0, 0), (0, 0), (0, 1))) + jnp.pad(
        values[:, :, :-1], ((0, 0), (0, 0), (1, 0))
    )
    return beside + 0.5 * (lower + upper)


def gray(value):
    return value + (value // 2) * (1 - 2 * (value % 2))


def gene_at_place(place, count):
    wide = 1 - ((place + count - 1) % count) // (count // 2)
    row = wide * (place - 1) + (1 - wide) * ((count - place) % count)
    return 2 * row + wide


def gene_place(index, count):
    row, wide = index // 2, index % 2
    return wide * (1 + row) + (1 - wide) * ((count - row) % count)


def bin_at_place(place, count):
    plane, step = place // 4, place % 4
    turned = step + (plane % 2) * (3 - 2 * step)
    return plane * 4 + gray(turned)


def bin_place(index, count):
    plane = index // 4
    turned = gray(index % 4)
    return plane * 4 + turned + (plane % 2) * (3 - 2 * turned)


RINGS = {"gene": (gene_at_place, gene_place), "bin": (bin_at_place, bin_place)}


def ring_peers(axis, count):
    at_place, place_of = RINGS[axis]
    place = place_of(lax.axis_index(axis), count)
    return place, (lambda shift: at_place((place + shift + count) % count, count))


def enter(axis, peers):
    barrier = pltpu.get_barrier_semaphore()
    for peer in peers:
        pl.semaphore_signal(barrier, inc=1, device_id={axis: peer},
                            device_id_type=pl.DeviceIdType.MESH)
    pl.semaphore_wait(barrier, len(peers))


def gather_kernel(axis, count, x_ref, out_ref, send_sem, recv_sem):
    place, member = ring_peers(axis, count)
    ahead, behind = member(1), member(-1)
    half = x_ref.shape[0] // 2
    enter(axis, (ahead, behind))
    out_ref[member(0)] = x_ref[...]

    def copy(step, way):
        rows = pl.ds(way * half, half)
        origin = member(-step) if way == 0 else member(step)
        src = x_ref.at[rows] if step == 0 else out_ref.at[origin, rows]
        return pltpu.make_async_remote_copy(
            src_ref=src,
            dst_ref=out_ref.at[origin, rows],
            send_sem=send_sem.at[way, step],
            recv_sem=recv_sem.at[way, step],
            device_id={axis: ahead if way == 0 else behind},
            device_id_type=pl.DeviceIdType.MESH,
        )

    for step in range(count - 1):
        for way in (0, 1):
            if step >= 1:
                copy(step - 1, way).wait_recv()
            copy(step, way).start()
    for way in (0, 1):
        copy(count - 2, way).wait_recv()
    for step in range(count - 1):
        for way in (0, 1):
            copy(step, way).wait_send()


def ring_gather(x, axis, collective_id):
    count = lax.axis_size(axis)
    return pl.pallas_call(
        functools.partial(gather_kernel, axis, count),
        out_shape=jax.ShapeDtypeStruct((count,) + x.shape, x.dtype),
        in_specs=[pl.BlockSpec(memory_space=pltpu.VMEM)],
        out_specs=pl.BlockSpec(memory_space=pltpu.VMEM),
        scratch_shapes=[
            pltpu.SemaphoreType.DMA((2, count - 1)),
            pltpu.SemaphoreType.DMA((2, count - 1)),
        ],
        compiler_params=pltpu.CompilerParams(
            collective_id=collective_id, has_side_effects=True
        ),
    )(x)


def scatter_kernel(axis, count, x_ref, out_ref, got, sent, send_sem, recv_sem):
    place, member = ring_peers(axis, count)
    ahead, behind = member(1), member(-1)
    half = x_ref.shape[2] // 2
    enter(axis, (ahead, behind))

    def copy(step, way):
        lanes = pl.ds(way * half, half)
        if step == 0:
            source = x_ref.at[member(-1) if way == 0 else member(1), :, lanes]
        else:
            source = sent.at[way, step]
        return pltpu.make_async_remote_copy(
            src_ref=source,
            dst_ref=got.at[way, step],
            send_sem=send_sem.at[way, step],
            recv_sem=recv_sem.at[way, step],
            device_id={axis: ahead if way == 0 else behind},
            device_id_type=pl.DeviceIdType.MESH,
        )

    for step in range(count - 1):
        for way in (0, 1):
            if step >= 1:
                lanes = pl.ds(way * half, half)
                owner = member(-step - 1) if way == 0 else member(step + 1)
                copy(step - 1, way).wait_recv()
                sent[way, step] = got[way, step - 1] + x_ref[owner, :, lanes]
            copy(step, way).start()
    for way in (0, 1):
        lanes = pl.ds(way * half, half)
        copy(count - 2, way).wait_recv()
        out_ref[:, lanes] = got[way, count - 2] + x_ref[member(0), :, lanes]
    for step in range(count - 1):
        for way in (0, 1):
            copy(step, way).wait_send()


def ring_scatter(x, axis, collective_id):
    count, rows, lanes = x.shape
    return pl.pallas_call(
        functools.partial(scatter_kernel, axis, count),
        out_shape=jax.ShapeDtypeStruct((rows, lanes), x.dtype),
        in_specs=[pl.BlockSpec(memory_space=pltpu.VMEM)],
        out_specs=pl.BlockSpec(memory_space=pltpu.VMEM),
        scratch_shapes=[
            pltpu.VMEM((2, count - 1, rows, lanes // 2), x.dtype),
            pltpu.VMEM((2, count - 1, rows, lanes // 2), x.dtype),
            pltpu.SemaphoreType.DMA((2, count - 1)),
            pltpu.SemaphoreType.DMA((2, count - 1)),
        ],
        compiler_params=pltpu.CompilerParams(
            collective_id=collective_id, has_side_effects=True
        ),
    )(x)


def greet_all(axis, me, count):
    barrier = pltpu.get_barrier_semaphore()
    for shift in range(1, count):
        pl.semaphore_signal(barrier, inc=1, device_id={axis: (me + shift) % count},
                            device_id_type=pl.DeviceIdType.MESH)
    pl.semaphore_wait(barrier, count - 1)


def exchange_kernel(axis, count, summed, x_ref, out_ref, *rest):
    if summed:
        got, send_sem, recv_sem = rest
    else:
        got, (send_sem, recv_sem) = out_ref, rest
    me = lax.axis_index(axis)
    greet_all(axis, me, count)

    def copy(shift):
        target = (me + shift) % count
        return pltpu.make_async_remote_copy(
            src_ref=x_ref.at[target] if summed else x_ref,
            dst_ref=got.at[me],
            send_sem=send_sem.at[shift],
            recv_sem=recv_sem.at[me],
            device_id={axis: target},
            device_id_type=pl.DeviceIdType.MESH,
        )

    def arrival(shift):
        origin = (me + count - shift) % count
        return pltpu.make_async_remote_copy(
            src_ref=x_ref.at[origin] if summed else x_ref,
            dst_ref=got.at[origin],
            send_sem=send_sem.at[shift],
            recv_sem=recv_sem.at[origin],
            device_id={axis: origin},
            device_id_type=pl.DeviceIdType.MESH,
        )

    for shift in range(1, count):
        copy(shift).start()
    if summed:
        total = x_ref[me]
        for shift in range(1, count):
            arrival(shift).wait_recv()
            total = total + got[(me + count - shift) % count]
        out_ref[...] = total
    else:
        out_ref[me] = x_ref[...]
        for shift in range(1, count):
            arrival(shift).wait_recv()
    for shift in range(1, count):
        copy(shift).wait_send()


def exchange(x, axis, collective_id, summed):
    count = lax.axis_size(axis)
    if summed:
        out_shape = x.shape[1:]
        scratch = [pltpu.VMEM(x.shape, x.dtype)]
    else:
        out_shape = (count,) + x.shape
        scratch = []
    return pl.pallas_call(
        functools.partial(exchange_kernel, axis, count, summed),
        out_shape=jax.ShapeDtypeStruct(out_shape, x.dtype),
        in_specs=[pl.BlockSpec(memory_space=pltpu.VMEM)],
        out_specs=pl.BlockSpec(memory_space=pltpu.VMEM),
        scratch_shapes=scratch + [
            pltpu.SemaphoreType.DMA((count,)),
            pltpu.SemaphoreType.DMA((count,)),
        ],
        compiler_params=pltpu.CompilerParams(
            collective_id=collective_id, has_side_effects=True
        ),
    )(x)


def factor_gather_kernel(count, x_ref, out_ref, half_ref, send_sem, recv_sem):
    me = lax.axis_index("gene")
    greet_all("gene", me, count)

    def copy(shift, index, peer):
        return pltpu.make_async_remote_copy(
            src_ref=x_ref,
            dst_ref=out_ref.at[index],
            send_sem=send_sem.at[shift],
            recv_sem=recv_sem.at[index],
            device_id={"gene": peer},
            device_id_type=pl.DeviceIdType.MESH,
        )

    for shift in range(1, count):
        copy(shift, me, (me + shift) % count).start()
    out_ref[me] = x_ref[...]
    for shift in range(1, count):
        origin = (me + count - shift) % count
        copy(shift, origin, origin).wait_recv()
    half_ref[...] = out_ref[...].astype(half_ref.dtype)
    for shift in range(1, count):
        copy(shift, me, (me + shift) % count).wait_send()


def factor_gather(x, collective_id):
    count = lax.axis_size("gene")
    vmem = pl.BlockSpec(memory_space=pltpu.VMEM)
    shape = (count,) + x.shape
    return pl.pallas_call(
        functools.partial(factor_gather_kernel, count),
        out_shape=(
            jax.ShapeDtypeStruct(shape, x.dtype),
            jax.ShapeDtypeStruct(shape, jnp.bfloat16),
        ),
        in_specs=[vmem],
        out_specs=(vmem, vmem),
        scratch_shapes=[pltpu.SemaphoreType.DMA((count,))] * 2,
        compiler_params=pltpu.CompilerParams(
            collective_id=collective_id, has_side_effects=True
        ),
    )(x)


def loadings_kernel(count, cross_ref, gram_ref, load_ref, out_ref, got, got_gram, sem_a, sem_b, sem_c, sem_d):
    me = lax.axis_index("bin")
    greet_all("bin", me, count)

    def remote(src, dst, send, recv, shift, index, peer):
        return pltpu.make_async_remote_copy(
            src_ref=src.at[index],
            dst_ref=dst.at[index],
            send_sem=send.at[shift],
            recv_sem=recv.at[index],
            device_id={"bin": peer},
            device_id_type=pl.DeviceIdType.MESH,
        )

    def partial_copies(shift):
        target = (me + shift) % count
        return (
            pltpu.make_async_remote_copy(
                src_ref=cross_ref.at[target], dst_ref=got.at[me], send_sem=sem_a.at[0, shift],
                recv_sem=sem_b.at[0, me], device_id={"bin": target},
                device_id_type=pl.DeviceIdType.MESH,
            ),
            pltpu.make_async_remote_copy(
                src_ref=gram_ref.at[target], dst_ref=got_gram.at[me], send_sem=sem_a.at[1, shift],
                recv_sem=sem_b.at[1, me], device_id={"bin": target},
                device_id_type=pl.DeviceIdType.MESH,
            ),
        )

    def partial_arrivals(shift):
        origin = (me + count - shift) % count
        return (
            pltpu.make_async_remote_copy(
                src_ref=cross_ref.at[origin], dst_ref=got.at[origin], send_sem=sem_a.at[0, shift],
                recv_sem=sem_b.at[0, origin], device_id={"bin": origin},
                device_id_type=pl.DeviceIdType.MESH,
            ),
            pltpu.make_async_remote_copy(
                src_ref=gram_ref.at[origin], dst_ref=got_gram.at[origin], send_sem=sem_a.at[1, shift],
                recv_sem=sem_b.at[1, origin], device_id={"bin": origin},
                device_id_type=pl.DeviceIdType.MESH,
            ),
        )

    def result_copy(shift):
        target = (me + shift) % count
        return remote(out_ref, out_ref, sem_c, sem_d, shift, me, target)

    def result_arrival(shift):
        origin = (me + count - shift) % count
        return remote(out_ref, out_ref, sem_c, sem_d, shift, origin, origin)

    for shift in range(1, count):
        for copy in partial_copies(shift):
            copy.start()
    cross = cross_ref[me]
    fac_gram = gram_ref[me]
    for shift in range(1, count):
        origin = (me + count - shift) % count
        for copy in partial_arrivals(shift):
            copy.wait_recv()
        cross = cross + got[origin]
        fac_gram = fac_gram + got_gram[origin]
    rows = cross.shape[0]
    own = load_ref[pl.ds(pl.multiple_of(me * rows, rows), rows), :]
    denom = jnp.dot(
        fac_gram, load_ref[...], precision=lax.Precision.HIGHEST,
        preferred_element_type=jnp.float32,
    )
    out_ref[me] = own * cross / denom
    for shift in range(1, count):
        result_copy(shift).start()
    for shift in range(1, count):
        for copy in partial_copies(shift):
            copy.wait_send()
    for shift in range(1, count):
        result_arrival(shift).wait_recv()
    for shift in range(1, count):
        result_copy(shift).wait_send()


def loadings_update(cross_parts, gram_parts, loadings, collective_id):
    count, rows, genes = cross_parts.shape
    vmem = pl.BlockSpec(memory_space=pltpu.VMEM)
    return pl.pallas_call(
        functools.partial(loadings_kernel, count),
        out_shape=jax.ShapeDtypeStruct((count, rows, genes), loadings.dtype),
        in_specs=[vmem, vmem, vmem],
        out_specs=vmem,
        scratch_shapes=[
            pltpu.VMEM(cross_parts.shape, cross_parts.dtype),
            pltpu.VMEM(gram_parts.shape, gram_parts.dtype),
            pltpu.SemaphoreType.DMA((2, count)),
            pltpu.SemaphoreType.DMA((2, count)),
            pltpu.SemaphoreType.DMA((count,)),
            pltpu.SemaphoreType.DMA((count,)),
        ],
        compiler_params=pltpu.CompilerParams(
            collective_id=collective_id, has_side_effects=True
        ),
    )(cross_parts, gram_parts, loadings)


def split_three(values):
    high = lax.reduce_precision(values, exponent_bits=8, mantissa_bits=7)
    rest = values - high
    mid = lax.reduce_precision(rest, exponent_bits=8, mantissa_bits=7)
    low = rest - mid
    return jnp.concatenate([high, mid, low], 1).astype(jnp.bfloat16)


def join_three(parts, width):
    return (parts[:, :width] + parts[:, width : 2 * width]) + parts[:, 2 * width :]


def stencil_term(own, position, edge_codes):
    bin_count = lax.axis_size("bin")
    row_count, width = own.shape
    group_size = row_count // bin_count
    grid_rows, grid_cols = edge_codes.shape
    payload = jnp.concatenate([own, position.astype(jnp.float32)[:, None]], 1)
    got = lax.all_to_all(
        payload.reshape(bin_count, group_size * (width + 1)), "bin", 0, 0, tiled=True
    ).reshape(row_count, width + 1)
    tile_slot = got[:, width].astype(jnp.int32) - lax.axis_index("bin") * row_count
    cells = lax.broadcasted_iota(jnp.int32, (row_count, row_count), 1)
    onehot = (tile_slot[:, None] == cells).astype(jnp.bfloat16)
    placed = lax.dot_general(
        onehot, split_three(got[:, :width]), (((0,), (0,)), ((), ())),
        preferred_element_type=jnp.float32,
    )
    tile_rows = join_three(placed, width)
    cell_scale = edge_codes.astype(jnp.float32) / 8.0
    weighted = cell_scale[:, :, None] * tile_rows.reshape(grid_rows, grid_cols, width)
    rim_last, rim_first = (weighted[-1], weighted[0])
    upper_rows, upper_scale = passed_along((rim_last, cell_scale[-1]), "bin", 1)
    lower_rows, lower_scale = passed_along((rim_first, cell_scale[0]), "bin", -1)
    degree_grid = (
        cell_scale * neighbour_first(cell_scale[None], upper_scale[None], lower_scale[None])[0]
    )
    smooth_grid = cell_scale[:, :, None] * neighbour_sum(weighted, upper_rows, lower_rows)
    back = jnp.concatenate(
        [smooth_grid.reshape(row_count, width), degree_grid.reshape(row_count, 1)], 1
    )
    back_rows = join_three(
        jnp.dot(onehot, split_three(back), preferred_element_type=jnp.float32), width + 1
    )
    ret = lax.all_to_all(
        back_rows.reshape(bin_count, group_size * (width + 1)), "bin", 0, 0, tiled=True
    ).reshape(row_count, width + 1)
    return (ret[:, :width], ret[:, width])


def on_device(counts, factors, loadings, position, edge_codes):
    bin_count = lax.axis_size("bin")
    gene_count = lax.axis_size("gene")
    row_count, width_all = factors.shape
    width = width_all // gene_count
    k_rows = width_all // bin_count
    gene_at = lax.axis_index("gene")
    bin_at = lax.axis_index("bin")
    load_bf = loadings.astype(jnp.bfloat16)
    right_dims = (((1,), (1,)), ((), ()))
    numer_part = lax.dot_general(load_bf, counts, right_dims, preferred_element_type=jnp.float32)
    gram_part = lax.dot_general(load_bf, load_bf, right_dims, preferred_element_type=jnp.float32)
    both = jnp.concatenate([numer_part, gram_part], 1)
    both = lax.psum_scatter(
        both.reshape(gene_count, width, -1), "gene", scatter_dimension=0, tiled=True
    ).reshape(width, -1)
    numer_t, gram_rows = both[:, :row_count], both[:, row_count:]
    own = lax.dynamic_slice_in_dim(factors, gene_at * width, width, 1)
    smooth, degree = stencil_term(own, position, edge_codes)
    penalty = float(G * K) / 64.0
    own_t = own.T
    denom_t = (
        lax.dot_general(gram_rows, factors, right_dims, precision=lax.Precision.HIGHEST)
        + penalty * degree[None, :] * own_t
    )
    new_t = own_t * (numer_t + penalty * smooth.T) / denom_t
    factors_t, fac_bf_t = factor_gather(new_t, 0)
    factors_new = factors_t.reshape(width_all, row_count).T
    fac_bf_t = fac_bf_t.reshape(width_all, row_count)
    cross_part = jnp.dot(fac_bf_t, counts, preferred_element_type=jnp.float32)
    fgram_part = lax.dot_general(fac_bf_t, fac_bf_t, right_dims, preferred_element_type=jnp.float32)
    loadings_new = loadings_update(
        cross_part.reshape(bin_count, k_rows, -1),
        fgram_part.reshape(bin_count, k_rows, -1),
        loadings,
        2,
    ).reshape(width_all, -1)
    return (factors_new, loadings_new)


def solution(mesh):
    placed = (P("bin", "gene"), P("bin", None), P(None, "gene"), P("bin"), P("bin", None))
    return jax.shard_map(
        on_device,
        mesh=mesh,
        in_specs=placed,
        out_specs=(P("bin", None), P(None, "gene")),
        check_vma=False,
    )
```

```python
import functools

import jax
import jax.numpy as jnp
from jax import lax
from jax.experimental import pallas as pl
from jax.experimental.pallas import tpu as pltpu
from jax.sharding import PartitionSpec as P

K = 256
G = 18432


def passed_along(block, axis, distance):
    devices = range(lax.axis_size(axis))
    route = [(i - distance, i) for i in devices if i - distance in devices]
    return lax.ppermute(block, axis, route)


def neighbour_sum(values, from_above, from_below):
    upper = jnp.concatenate([from_above[None], values[:-1]], 0)
    lower = jnp.concatenate([values[1:], from_below[None]], 0)
    beside = jnp.pad(values[:, 1:], ((0, 0), (0, 1), (0, 0))) + jnp.pad(
        values[:, :-1], ((0, 0), (1, 0), (0, 0))
    )
    return beside + 0.5 * (lower + upper)


def neighbour_first(values, from_above, from_below):
    upper = jnp.concatenate([from_above[:, None], values[:, :-1]], 1)
    lower = jnp.concatenate([values[:, 1:], from_below[:, None]], 1)
    beside = jnp.pad(values[:, :, 1:], ((0, 0), (0, 0), (0, 1))) + jnp.pad(
        values[:, :, :-1], ((0, 0), (0, 0), (1, 0))
    )
    return beside + 0.5 * (lower + upper)


def gray(value):
    return value + (value // 2) * (1 - 2 * (value % 2))


def gene_at_place(place, count):
    wide = 1 - ((place + count - 1) % count) // (count // 2)
    row = wide * (place - 1) + (1 - wide) * ((count - place) % count)
    return 2 * row + wide


def gene_place(index, count):
    row, wide = index // 2, index % 2
    return wide * (1 + row) + (1 - wide) * ((count - row) % count)


def bin_at_place(place, count):
    plane, step = place // 4, place % 4
    turned = step + (plane % 2) * (3 - 2 * step)
    return plane * 4 + gray(turned)


def bin_place(index, count):
    plane = index // 4
    turned = gray(index % 4)
    return plane * 4 + turned + (plane % 2) * (3 - 2 * turned)


RINGS = {"gene": (gene_at_place, gene_place), "bin": (bin_at_place, bin_place)}


def ring_peers(axis, count):
    at_place, place_of = RINGS[axis]
    place = place_of(lax.axis_index(axis), count)
    return place, (lambda shift: at_place((place + shift + count) % count, count))


def enter(axis, peers):
    barrier = pltpu.get_barrier_semaphore()
    for peer in peers:
        pl.semaphore_signal(barrier, inc=1, device_id={axis: peer},
                            device_id_type=pl.DeviceIdType.MESH)
    pl.semaphore_wait(barrier, len(peers))


def gather_kernel(axis, count, x_ref, out_ref, send_sem, recv_sem):
    place, member = ring_peers(axis, count)
    ahead, behind = member(1), member(-1)
    half = x_ref.shape[0] // 2
    enter(axis, (ahead, behind))
    out_ref[member(0)] = x_ref[...]

    def copy(step, way):
        rows = pl.ds(way * half, half)
        origin = member(-step) if way == 0 else member(step)
        src = x_ref.at[rows] if step == 0 else out_ref.at[origin, rows]
        return pltpu.make_async_remote_copy(
            src_ref=src,
            dst_ref=out_ref.at[origin, rows],
            send_sem=send_sem.at[way, step],
            recv_sem=recv_sem.at[way, step],
            device_id={axis: ahead if way == 0 else behind},
            device_id_type=pl.DeviceIdType.MESH,
        )

    for step in range(count - 1):
        for way in (0, 1):
            if step >= 1:
                copy(step - 1, way).wait_recv()
            copy(step, way).start()
    for way in (0, 1):
        copy(count - 2, way).wait_recv()
    for step in range(count - 1):
        for way in (0, 1):
            copy(step, way).wait_send()


def ring_gather(x, axis, collective_id):
    count = lax.axis_size(axis)
    return pl.pallas_call(
        functools.partial(gather_kernel, axis, count),
        out_shape=jax.ShapeDtypeStruct((count,) + x.shape, x.dtype),
        in_specs=[pl.BlockSpec(memory_space=pltpu.VMEM)],
        out_specs=pl.BlockSpec(memory_space=pltpu.VMEM),
        scratch_shapes=[
            pltpu.SemaphoreType.DMA((2, count - 1)),
            pltpu.SemaphoreType.DMA((2, count - 1)),
        ],
        compiler_params=pltpu.CompilerParams(
            collective_id=collective_id, has_side_effects=True
        ),
    )(x)


def scatter_kernel(axis, count, x_ref, out_ref, got, sent, send_sem, recv_sem):
    place, member = ring_peers(axis, count)
    ahead, behind = member(1), member(-1)
    half = x_ref.shape[2] // 2
    enter(axis, (ahead, behind))

    def copy(step, way):
        lanes = pl.ds(way * half, half)
        if step == 0:
            source = x_ref.at[member(-1) if way == 0 else member(1), :, lanes]
        else:
            source = sent.at[way, step]
        return pltpu.make_async_remote_copy(
            src_ref=source,
            dst_ref=got.at[way, step],
            send_sem=send_sem.at[way, step],
            recv_sem=recv_sem.at[way, step],
            device_id={axis: ahead if way == 0 else behind},
            device_id_type=pl.DeviceIdType.MESH,
        )

    for step in range(count - 1):
        for way in (0, 1):
            if step >= 1:
                lanes = pl.ds(way * half, half)
                owner = member(-step - 1) if way == 0 else member(step + 1)
                copy(step - 1, way).wait_recv()
                sent[way, step] = got[way, step - 1] + x_ref[owner, :, lanes]
            copy(step, way).start()
    for way in (0, 1):
        lanes = pl.ds(way * half, half)
        copy(count - 2, way).wait_recv()
        out_ref[:, lanes] = got[way, count - 2] + x_ref[member(0), :, lanes]
    for step in range(count - 1):
        for way in (0, 1):
            copy(step, way).wait_send()


def ring_scatter(x, axis, collective_id):
    count, rows, lanes = x.shape
    return pl.pallas_call(
        functools.partial(scatter_kernel, axis, count),
        out_shape=jax.ShapeDtypeStruct((rows, lanes), x.dtype),
        in_specs=[pl.BlockSpec(memory_space=pltpu.VMEM)],
        out_specs=pl.BlockSpec(memory_space=pltpu.VMEM),
        scratch_shapes=[
            pltpu.VMEM((2, count - 1, rows, lanes // 2), x.dtype),
            pltpu.VMEM((2, count - 1, rows, lanes // 2), x.dtype),
            pltpu.SemaphoreType.DMA((2, count - 1)),
            pltpu.SemaphoreType.DMA((2, count - 1)),
        ],
        compiler_params=pltpu.CompilerParams(
            collective_id=collective_id, has_side_effects=True
        ),
    )(x)


def greet_all(axis, me, count):
    barrier = pltpu.get_barrier_semaphore()
    for shift in range(1, count):
        pl.semaphore_signal(barrier, inc=1, device_id={axis: (me + shift) % count},
                            device_id_type=pl.DeviceIdType.MESH)
    pl.semaphore_wait(barrier, count - 1)


def exchange_kernel(axis, count, summed, x_ref, out_ref, *rest):
    if summed:
        got, send_sem, recv_sem = rest
    else:
        got, (send_sem, recv_sem) = out_ref, rest
    me = lax.axis_index(axis)
    greet_all(axis, me, count)

    def copy(shift):
        target = (me + shift) % count
        return pltpu.make_async_remote_copy(
            src_ref=x_ref.at[target] if summed else x_ref,
            dst_ref=got.at[me],
            send_sem=send_sem.at[shift],
            recv_sem=recv_sem.at[me],
            device_id={axis: target},
            device_id_type=pl.DeviceIdType.MESH,
        )

    def arrival(shift):
        origin = (me + count - shift) % count
        return pltpu.make_async_remote_copy(
            src_ref=x_ref.at[origin] if summed else x_ref,
            dst_ref=got.at[origin],
            send_sem=send_sem.at[shift],
            recv_sem=recv_sem.at[origin],
            device_id={axis: origin},
            device_id_type=pl.DeviceIdType.MESH,
        )

    for shift in range(1, count):
        copy(shift).start()
    if summed:
        total = x_ref[me]
        for shift in range(1, count):
            arrival(shift).wait_recv()
            total = total + got[(me + count - shift) % count]
        out_ref[...] = total
    else:
        out_ref[me] = x_ref[...]
        for shift in range(1, count):
            arrival(shift).wait_recv()
    for shift in range(1, count):
        copy(shift).wait_send()


def exchange(x, axis, collective_id, summed):
    count = lax.axis_size(axis)
    if summed:
        out_shape = x.shape[1:]
        scratch = [pltpu.VMEM(x.shape, x.dtype)]
    else:
        out_shape = (count,) + x.shape
        scratch = []
    return pl.pallas_call(
        functools.partial(exchange_kernel, axis, count, summed),
        out_shape=jax.ShapeDtypeStruct(out_shape, x.dtype),
        in_specs=[pl.BlockSpec(memory_space=pltpu.VMEM)],
        out_specs=pl.BlockSpec(memory_space=pltpu.VMEM),
        scratch_shapes=scratch + [
            pltpu.SemaphoreType.DMA((count,)),
            pltpu.SemaphoreType.DMA((count,)),
        ],
        compiler_params=pltpu.CompilerParams(
            collective_id=collective_id, has_side_effects=True
        ),
    )(x)


def loadings_kernel(count, cross_ref, gram_ref, load_ref, out_ref, got, got_gram, sem_a, sem_b, sem_c, sem_d):
    me = lax.axis_index("bin")
    greet_all("bin", me, count)

    def remote(src, dst, send, recv, shift, index, peer):
        return pltpu.make_async_remote_copy(
            src_ref=src.at[index],
            dst_ref=dst.at[index],
            send_sem=send.at[shift],
            recv_sem=recv.at[index],
            device_id={"bin": peer},
            device_id_type=pl.DeviceIdType.MESH,
        )

    def partial_copies(shift):
        target = (me + shift) % count
        return (
            pltpu.make_async_remote_copy(
                src_ref=cross_ref.at[target], dst_ref=got.at[me], send_sem=sem_a.at[0, shift],
                recv_sem=sem_b.at[0, me], device_id={"bin": target},
                device_id_type=pl.DeviceIdType.MESH,
            ),
            pltpu.make_async_remote_copy(
                src_ref=gram_ref.at[target], dst_ref=got_gram.at[me], send_sem=sem_a.at[1, shift],
                recv_sem=sem_b.at[1, me], device_id={"bin": target},
                device_id_type=pl.DeviceIdType.MESH,
            ),
        )

    def partial_arrivals(shift):
        origin = (me + count - shift) % count
        return (
            pltpu.make_async_remote_copy(
                src_ref=cross_ref.at[origin], dst_ref=got.at[origin], send_sem=sem_a.at[0, shift],
                recv_sem=sem_b.at[0, origin], device_id={"bin": origin},
                device_id_type=pl.DeviceIdType.MESH,
            ),
            pltpu.make_async_remote_copy(
                src_ref=gram_ref.at[origin], dst_ref=got_gram.at[origin], send_sem=sem_a.at[1, shift],
                recv_sem=sem_b.at[1, origin], device_id={"bin": origin},
                device_id_type=pl.DeviceIdType.MESH,
            ),
        )

    def result_copy(shift):
        target = (me + shift) % count
        return remote(out_ref, out_ref, sem_c, sem_d, shift, me, target)

    def result_arrival(shift):
        origin = (me + count - shift) % count
        return remote(out_ref, out_ref, sem_c, sem_d, shift, origin, origin)

    for shift in range(1, count):
        for copy in partial_copies(shift):
            copy.start()
    cross = cross_ref[me]
    fac_gram = gram_ref[me]
    for shift in range(1, count):
        origin = (me + count - shift) % count
        for copy in partial_arrivals(shift):
            copy.wait_recv()
        cross = cross + got[origin]
        fac_gram = fac_gram + got_gram[origin]
    rows = cross.shape[0]
    own = load_ref[pl.ds(pl.multiple_of(me * rows, rows), rows), :]
    denom = jnp.dot(
        fac_gram, load_ref[...], precision=lax.Precision.HIGHEST,
        preferred_element_type=jnp.float32,
    )
    out_ref[me] = own * cross / denom
    for shift in range(1, count):
        result_copy(shift).start()
    for shift in range(1, count):
        for copy in partial_copies(shift):
            copy.wait_send()
    for shift in range(1, count):
        result_arrival(shift).wait_recv()
    for shift in range(1, count):
        result_copy(shift).wait_send()


def loadings_update(cross_parts, gram_parts, loadings, collective_id):
    count, rows, genes = cross_parts.shape
    vmem = pl.BlockSpec(memory_space=pltpu.VMEM)
    return pl.pallas_call(
        functools.partial(loadings_kernel, count),
        out_shape=jax.ShapeDtypeStruct((count, rows, genes), loadings.dtype),
        in_specs=[vmem, vmem, vmem],
        out_specs=vmem,
        scratch_shapes=[
            pltpu.VMEM(cross_parts.shape, cross_parts.dtype),
            pltpu.VMEM(gram_parts.shape, gram_parts.dtype),
            pltpu.SemaphoreType.DMA((2, count)),
            pltpu.SemaphoreType.DMA((2, count)),
            pltpu.SemaphoreType.DMA((count,)),
            pltpu.SemaphoreType.DMA((count,)),
        ],
        compiler_params=pltpu.CompilerParams(
            collective_id=collective_id, has_side_effects=True
        ),
    )(cross_parts, gram_parts, loadings)


def split_three(values):
    high = lax.reduce_precision(values, exponent_bits=8, mantissa_bits=7)
    rest = values - high
    mid = lax.reduce_precision(rest, exponent_bits=8, mantissa_bits=7)
    low = rest - mid
    return jnp.concatenate([high, mid, low], 1).astype(jnp.bfloat16)


def join_three(parts, width):
    return (parts[:, :width] + parts[:, width : 2 * width]) + parts[:, 2 * width :]


def stencil_term(own, position, edge_codes):
    bin_count = lax.axis_size("bin")
    row_count, width = own.shape
    group_size = row_count // bin_count
    grid_rows, grid_cols = edge_codes.shape
    payload = jnp.concatenate([own, position.astype(jnp.float32)[:, None]], 1)
    got = lax.all_to_all(
        payload.reshape(bin_count, group_size * (width + 1)), "bin", 0, 0, tiled=True
    ).reshape(row_count, width + 1)
    tile_slot = got[:, width].astype(jnp.int32) - lax.axis_index("bin") * row_count
    cells = lax.broadcasted_iota(jnp.int32, (row_count, row_count), 1)
    onehot = (tile_slot[:, None] == cells).astype(jnp.bfloat16)
    placed = lax.dot_general(
        onehot, split_three(got[:, :width]), (((0,), (0,)), ((), ())),
        preferred_element_type=jnp.float32,
    )
    tile_rows = join_three(placed, width)
    cell_scale = edge_codes.astype(jnp.float32) / 8.0
    weighted = cell_scale[:, :, None] * tile_rows.reshape(grid_rows, grid_cols, width)
    rim_last, rim_first = (weighted[-1], weighted[0])
    upper_rows, upper_scale = passed_along((rim_last, cell_scale[-1]), "bin", 1)
    lower_rows, lower_scale = passed_along((rim_first, cell_scale[0]), "bin", -1)
    degree_grid = (
        cell_scale * neighbour_first(cell_scale[None], upper_scale[None], lower_scale[None])[0]
    )
    smooth_grid = cell_scale[:, :, None] * neighbour_sum(weighted, upper_rows, lower_rows)
    back = jnp.concatenate(
        [smooth_grid.reshape(row_count, width), degree_grid.reshape(row_count, 1)], 1
    )
    back_rows = join_three(
        jnp.dot(onehot, split_three(back), preferred_element_type=jnp.float32), width + 1
    )
    ret = lax.all_to_all(
        back_rows.reshape(bin_count, group_size * (width + 1)), "bin", 0, 0, tiled=True
    ).reshape(row_count, width + 1)
    return (ret[:, :width], ret[:, width])


def on_device(counts, factors, loadings, position, edge_codes):
    bin_count = lax.axis_size("bin")
    gene_count = lax.axis_size("gene")
    row_count, width_all = factors.shape
    width = width_all // gene_count
    k_rows = width_all // bin_count
    gene_at = lax.axis_index("gene")
    bin_at = lax.axis_index("bin")
    load_bf = loadings.astype(jnp.bfloat16)
    right_dims = (((1,), (1,)), ((), ()))
    numer_part = lax.dot_general(load_bf, counts, right_dims, preferred_element_type=jnp.float32)
    gram_part = lax.dot_general(load_bf, load_bf, right_dims, preferred_element_type=jnp.float32)
    both = jnp.concatenate([numer_part, gram_part], 1)
    both = lax.psum_scatter(
        both.reshape(gene_count, width, -1), "gene", scatter_dimension=0, tiled=True
    ).reshape(width, -1)
    numer_t, gram_rows = both[:, :row_count], both[:, row_count:]
    own = lax.dynamic_slice_in_dim(factors, gene_at * width, width, 1)
    smooth, degree = stencil_term(own, position, edge_codes)
    penalty = float(G * K) / 64.0
    own_t = own.T
    denom_t = (
        lax.dot_general(gram_rows, factors, right_dims, precision=lax.Precision.HIGHEST)
        + penalty * degree[None, :] * own_t
    )
    new_t = own_t * (numer_t + penalty * smooth.T) / denom_t
    factors_t = exchange(new_t, "gene", 0, False).reshape(width_all, row_count)
    factors_new = factors_t.T
    fac_bf_t = factors_t.astype(jnp.bfloat16)
    cross_part = jnp.dot(fac_bf_t, counts, preferred_element_type=jnp.float32)
    fgram_part = lax.dot_general(fac_bf_t, fac_bf_t, right_dims, preferred_element_type=jnp.float32)
    loadings_new = loadings_update(
        cross_part.reshape(bin_count, k_rows, -1),
        fgram_part.reshape(bin_count, k_rows, -1),
        loadings,
        2,
    ).reshape(width_all, -1)
    return (factors_new, loadings_new)


def solution(mesh):
    placed = (P("bin", "gene"), P("bin", None), P(None, "gene"), P("bin"), P("bin", None))
    return jax.shard_map(
        on_device,
        mesh=mesh,
        in_specs=placed,
        out_specs=(P("bin", None), P(None, "gene")),
        check_vma=False,
    )
```

```python
import functools

import jax
import jax.numpy as jnp
from jax import lax
from jax.experimental import pallas as pl
from jax.experimental.pallas import tpu as pltpu
from jax.sharding import PartitionSpec as P

K = 256
G = 18432


def passed_along(block, axis, distance):
    devices = range(lax.axis_size(axis))
    route = [(i - distance, i) for i in devices if i - distance in devices]
    return lax.ppermute(block, axis, route)


def neighbour_sum(values, from_above, from_below):
    upper = jnp.concatenate([from_above[None], values[:-1]], 0)
    lower = jnp.concatenate([values[1:], from_below[None]], 0)
    beside = jnp.pad(values[:, 1:], ((0, 0), (0, 1), (0, 0))) + jnp.pad(
        values[:, :-1], ((0, 0), (1, 0), (0, 0))
    )
    return beside + 0.5 * (lower + upper)


def neighbour_first(values, from_above, from_below):
    upper = jnp.concatenate([from_above[:, None], values[:, :-1]], 1)
    lower = jnp.concatenate([values[:, 1:], from_below[:, None]], 1)
    beside = jnp.pad(values[:, :, 1:], ((0, 0), (0, 0), (0, 1))) + jnp.pad(
        values[:, :, :-1], ((0, 0), (0, 0), (1, 0))
    )
    return beside + 0.5 * (lower + upper)


def gray(value):
    return value + (value // 2) * (1 - 2 * (value % 2))


def gene_at_place(place, count):
    wide = 1 - ((place + count - 1) % count) // (count // 2)
    row = wide * (place - 1) + (1 - wide) * ((count - place) % count)
    return 2 * row + wide


def gene_place(index, count):
    row, wide = index // 2, index % 2
    return wide * (1 + row) + (1 - wide) * ((count - row) % count)


def bin_at_place(place, count):
    plane, step = place // 4, place % 4
    turned = step + (plane % 2) * (3 - 2 * step)
    return plane * 4 + gray(turned)


def bin_place(index, count):
    plane = index // 4
    turned = gray(index % 4)
    return plane * 4 + turned + (plane % 2) * (3 - 2 * turned)


RINGS = {"gene": (gene_at_place, gene_place), "bin": (bin_at_place, bin_place)}


def ring_peers(axis, count):
    at_place, place_of = RINGS[axis]
    place = place_of(lax.axis_index(axis), count)
    return place, (lambda shift: at_place((place + shift + count) % count, count))


def enter(axis, peers):
    barrier = pltpu.get_barrier_semaphore()
    for peer in peers:
        pl.semaphore_signal(barrier, inc=1, device_id={axis: peer},
                            device_id_type=pl.DeviceIdType.MESH)
    pl.semaphore_wait(barrier, len(peers))


def gather_kernel(axis, count, x_ref, out_ref, send_sem, recv_sem):
    place, member = ring_peers(axis, count)
    ahead, behind = member(1), member(-1)
    half = x_ref.shape[0] // 2
    enter(axis, (ahead, behind))
    out_ref[member(0)] = x_ref[...]

    def copy(step, way):
        rows = pl.ds(way * half, half)
        origin = member(-step) if way == 0 else member(step)
        src = x_ref.at[rows] if step == 0 else out_ref.at[origin, rows]
        return pltpu.make_async_remote_copy(
            src_ref=src,
            dst_ref=out_ref.at[origin, rows],
            send_sem=send_sem.at[way, step],
            recv_sem=recv_sem.at[way, step],
            device_id={axis: ahead if way == 0 else behind},
            device_id_type=pl.DeviceIdType.MESH,
        )

    for step in range(count - 1):
        for way in (0, 1):
            if step >= 1:
                copy(step - 1, way).wait_recv()
            copy(step, way).start()
    for way in (0, 1):
        copy(count - 2, way).wait_recv()
    for step in range(count - 1):
        for way in (0, 1):
            copy(step, way).wait_send()


def ring_gather(x, axis, collective_id):
    count = lax.axis_size(axis)
    return pl.pallas_call(
        functools.partial(gather_kernel, axis, count),
        out_shape=jax.ShapeDtypeStruct((count,) + x.shape, x.dtype),
        in_specs=[pl.BlockSpec(memory_space=pltpu.VMEM)],
        out_specs=pl.BlockSpec(memory_space=pltpu.VMEM),
        scratch_shapes=[
            pltpu.SemaphoreType.DMA((2, count - 1)),
            pltpu.SemaphoreType.DMA((2, count - 1)),
        ],
        compiler_params=pltpu.CompilerParams(
            collective_id=collective_id, has_side_effects=True
        ),
    )(x)


def scatter_kernel(axis, count, x_ref, out_ref, got, sent, send_sem, recv_sem):
    place, member = ring_peers(axis, count)
    ahead, behind = member(1), member(-1)
    half = x_ref.shape[2] // 2
    enter(axis, (ahead, behind))

    def copy(step, way):
        lanes = pl.ds(way * half, half)
        if step == 0:
            source = x_ref.at[member(-1) if way == 0 else member(1), :, lanes]
        else:
            source = sent.at[way, step]
        return pltpu.make_async_remote_copy(
            src_ref=source,
            dst_ref=got.at[way, step],
            send_sem=send_sem.at[way, step],
            recv_sem=recv_sem.at[way, step],
            device_id={axis: ahead if way == 0 else behind},
            device_id_type=pl.DeviceIdType.MESH,
        )

    for step in range(count - 1):
        for way in (0, 1):
            if step >= 1:
                lanes = pl.ds(way * half, half)
                owner = member(-step - 1) if way == 0 else member(step + 1)
                copy(step - 1, way).wait_recv()
                sent[way, step] = got[way, step - 1] + x_ref[owner, :, lanes]
            copy(step, way).start()
    for way in (0, 1):
        lanes = pl.ds(way * half, half)
        copy(count - 2, way).wait_recv()
        out_ref[:, lanes] = got[way, count - 2] + x_ref[member(0), :, lanes]
    for step in range(count - 1):
        for way in (0, 1):
            copy(step, way).wait_send()


def ring_scatter(x, axis, collective_id):
    count, rows, lanes = x.shape
    return pl.pallas_call(
        functools.partial(scatter_kernel, axis, count),
        out_shape=jax.ShapeDtypeStruct((rows, lanes), x.dtype),
        in_specs=[pl.BlockSpec(memory_space=pltpu.VMEM)],
        out_specs=pl.BlockSpec(memory_space=pltpu.VMEM),
        scratch_shapes=[
            pltpu.VMEM((2, count - 1, rows, lanes // 2), x.dtype),
            pltpu.VMEM((2, count - 1, rows, lanes // 2), x.dtype),
            pltpu.SemaphoreType.DMA((2, count - 1)),
            pltpu.SemaphoreType.DMA((2, count - 1)),
        ],
        compiler_params=pltpu.CompilerParams(
            collective_id=collective_id, has_side_effects=True
        ),
    )(x)


def greet_all(axis, me, count):
    barrier = pltpu.get_barrier_semaphore()
    for shift in range(1, count):
        pl.semaphore_signal(barrier, inc=1, device_id={axis: (me + shift) % count},
                            device_id_type=pl.DeviceIdType.MESH)
    pl.semaphore_wait(barrier, count - 1)


def exchange_kernel(axis, count, summed, x_ref, out_ref, *rest):
    if summed:
        got, send_sem, recv_sem = rest
    else:
        got, (send_sem, recv_sem) = out_ref, rest
    me = lax.axis_index(axis)
    greet_all(axis, me, count)

    def copy(shift):
        target = (me + shift) % count
        return pltpu.make_async_remote_copy(
            src_ref=x_ref.at[target] if summed else x_ref,
            dst_ref=got.at[me],
            send_sem=send_sem.at[shift],
            recv_sem=recv_sem.at[me],
            device_id={axis: target},
            device_id_type=pl.DeviceIdType.MESH,
        )

    def arrival(shift):
        origin = (me + count - shift) % count
        return pltpu.make_async_remote_copy(
            src_ref=x_ref.at[origin] if summed else x_ref,
            dst_ref=got.at[origin],
            send_sem=send_sem.at[shift],
            recv_sem=recv_sem.at[origin],
            device_id={axis: origin},
            device_id_type=pl.DeviceIdType.MESH,
        )

    for shift in range(1, count):
        copy(shift).start()
    if summed:
        total = x_ref[me]
        for shift in range(1, count):
            arrival(shift).wait_recv()
            total = total + got[(me + count - shift) % count]
        out_ref[...] = total
    else:
        out_ref[me] = x_ref[...]
        for shift in range(1, count):
            arrival(shift).wait_recv()
    for shift in range(1, count):
        copy(shift).wait_send()


def exchange(x, axis, collective_id, summed):
    count = lax.axis_size(axis)
    if summed:
        out_shape = x.shape[1:]
        scratch = [pltpu.VMEM(x.shape, x.dtype)]
    else:
        out_shape = (count,) + x.shape
        scratch = []
    return pl.pallas_call(
        functools.partial(exchange_kernel, axis, count, summed),
        out_shape=jax.ShapeDtypeStruct(out_shape, x.dtype),
        in_specs=[pl.BlockSpec(memory_space=pltpu.VMEM)],
        out_specs=pl.BlockSpec(memory_space=pltpu.VMEM),
        scratch_shapes=scratch + [
            pltpu.SemaphoreType.DMA((count,)),
            pltpu.SemaphoreType.DMA((count,)),
        ],
        compiler_params=pltpu.CompilerParams(
            collective_id=collective_id, has_side_effects=True
        ),
    )(x)


def loadings_kernel(count, cross_ref, gram_ref, load_ref, out_ref, got, got_gram, sem_a, sem_b, sem_c, sem_d):
    me = lax.axis_index("bin")
    greet_all("bin", me, count)

    def remote(src, dst, send, recv, shift, index, peer):
        return pltpu.make_async_remote_copy(
            src_ref=src.at[index],
            dst_ref=dst.at[index],
            send_sem=send.at[shift],
            recv_sem=recv.at[index],
            device_id={"bin": peer},
            device_id_type=pl.DeviceIdType.MESH,
        )

    def partial_copies(shift):
        target = (me + shift) % count
        return (
            pltpu.make_async_remote_copy(
                src_ref=cross_ref.at[target], dst_ref=got.at[me], send_sem=sem_a.at[0, shift],
                recv_sem=sem_b.at[0, me], device_id={"bin": target},
                device_id_type=pl.DeviceIdType.MESH,
            ),
            pltpu.make_async_remote_copy(
                src_ref=gram_ref.at[target], dst_ref=got_gram.at[me], send_sem=sem_a.at[1, shift],
                recv_sem=sem_b.at[1, me], device_id={"bin": target},
                device_id_type=pl.DeviceIdType.MESH,
            ),
        )

    def partial_arrivals(shift):
        origin = (me + count - shift) % count
        return (
            pltpu.make_async_remote_copy(
                src_ref=cross_ref.at[origin], dst_ref=got.at[origin], send_sem=sem_a.at[0, shift],
                recv_sem=sem_b.at[0, origin], device_id={"bin": origin},
                device_id_type=pl.DeviceIdType.MESH,
            ),
            pltpu.make_async_remote_copy(
                src_ref=gram_ref.at[origin], dst_ref=got_gram.at[origin], send_sem=sem_a.at[1, shift],
                recv_sem=sem_b.at[1, origin], device_id={"bin": origin},
                device_id_type=pl.DeviceIdType.MESH,
            ),
        )

    def result_copy(shift):
        target = (me + shift) % count
        return remote(out_ref, out_ref, sem_c, sem_d, shift, me, target)

    def result_arrival(shift):
        origin = (me + count - shift) % count
        return remote(out_ref, out_ref, sem_c, sem_d, shift, origin, origin)

    for shift in range(1, count):
        for copy in partial_copies(shift):
            copy.start()
    cross = cross_ref[me]
    fac_gram = gram_ref[me]
    for shift in range(1, count):
        origin = (me + count - shift) % count
        for copy in partial_arrivals(shift):
            copy.wait_recv()
        cross = cross + got[origin]
        fac_gram = fac_gram + got_gram[origin]
    rows = cross.shape[0]
    own = load_ref[pl.ds(pl.multiple_of(me * rows, rows), rows), :]
    denom = jnp.dot(
        fac_gram, load_ref[...], precision=lax.Precision.HIGHEST,
        preferred_element_type=jnp.float32,
    )
    out_ref[me] = own * cross / denom
    for shift in range(1, count):
        for copy in partial_copies(shift):
            copy.wait_send()
    for shift in range(1, count):
        result_copy(shift).start()
    for shift in range(1, count):
        result_arrival(shift).wait_recv()
    for shift in range(1, count):
        result_copy(shift).wait_send()


def loadings_update(cross_parts, gram_parts, loadings, collective_id):
    count, rows, genes = cross_parts.shape
    vmem = pl.BlockSpec(memory_space=pltpu.VMEM)
    return pl.pallas_call(
        functools.partial(loadings_kernel, count),
        out_shape=jax.ShapeDtypeStruct((count, rows, genes), loadings.dtype),
        in_specs=[vmem, vmem, vmem],
        out_specs=vmem,
        scratch_shapes=[
            pltpu.VMEM(cross_parts.shape, cross_parts.dtype),
            pltpu.VMEM(gram_parts.shape, gram_parts.dtype),
            pltpu.SemaphoreType.DMA((2, count)),
            pltpu.SemaphoreType.DMA((2, count)),
            pltpu.SemaphoreType.DMA((count,)),
            pltpu.SemaphoreType.DMA((count,)),
        ],
        compiler_params=pltpu.CompilerParams(
            collective_id=collective_id, has_side_effects=True
        ),
    )(cross_parts, gram_parts, loadings)


def split_three(values):
    high = lax.reduce_precision(values, exponent_bits=8, mantissa_bits=7)
    rest = values - high
    mid = lax.reduce_precision(rest, exponent_bits=8, mantissa_bits=7)
    low = rest - mid
    return jnp.concatenate([high, mid, low], 1).astype(jnp.bfloat16)


def join_three(parts, width):
    return (parts[:, :width] + parts[:, width : 2 * width]) + parts[:, 2 * width :]


def stencil_term(own, position, edge_codes):
    bin_count = lax.axis_size("bin")
    row_count, width = own.shape
    group_size = row_count // bin_count
    grid_rows, grid_cols = edge_codes.shape
    payload = jnp.concatenate([own, position.astype(jnp.float32)[:, None]], 1)
    got = lax.all_to_all(
        payload.reshape(bin_count, group_size, width + 1), "bin", 0, 0, tiled=True
    ).reshape(row_count, width + 1)
    tile_slot = got[:, width].astype(jnp.int32) - lax.axis_index("bin") * row_count
    cells = lax.broadcasted_iota(jnp.int32, (row_count, row_count), 1)
    onehot = (tile_slot[:, None] == cells).astype(jnp.bfloat16)
    placed = lax.dot_general(
        onehot, split_three(got[:, :width]), (((0,), (0,)), ((), ())),
        preferred_element_type=jnp.float32,
    )
    tile_rows = join_three(placed, width)
    cell_scale = edge_codes.astype(jnp.float32) / 8.0
    weighted = cell_scale[:, :, None] * tile_rows.reshape(grid_rows, grid_cols, width)
    rim_last, rim_first = (weighted[-1], weighted[0])
    upper_rows, upper_scale = passed_along((rim_last, cell_scale[-1]), "bin", 1)
    lower_rows, lower_scale = passed_along((rim_first, cell_scale[0]), "bin", -1)
    degree_grid = (
        cell_scale * neighbour_first(cell_scale[None], upper_scale[None], lower_scale[None])[0]
    )
    smooth_grid = cell_scale[:, :, None] * neighbour_sum(weighted, upper_rows, lower_rows)
    back = jnp.concatenate(
        [smooth_grid.reshape(row_count, width), degree_grid.reshape(row_count, 1)], 1
    )
    back_rows = join_three(
        jnp.dot(onehot, split_three(back), preferred_element_type=jnp.float32), width + 1
    )
    ret = lax.all_to_all(
        back_rows.reshape(bin_count, group_size, width + 1), "bin", 0, 0, tiled=True
    ).reshape(row_count, width + 1)
    return (ret[:, :width], ret[:, width])


def on_device(counts, factors, loadings, position, edge_codes):
    bin_count = lax.axis_size("bin")
    gene_count = lax.axis_size("gene")
    row_count, width_all = factors.shape
    width = width_all // gene_count
    k_rows = width_all // bin_count
    gene_at = lax.axis_index("gene")
    bin_at = lax.axis_index("bin")
    load_bf = loadings.astype(jnp.bfloat16)
    right_dims = (((1,), (1,)), ((), ()))
    numer_part = lax.dot_general(load_bf, counts, right_dims, preferred_element_type=jnp.float32)
    gram_part = lax.dot_general(load_bf, load_bf, right_dims, preferred_element_type=jnp.float32)
    both = jnp.concatenate([numer_part, gram_part], 1)
    both = lax.psum_scatter(
        both.reshape(gene_count, width, -1), "gene", scatter_dimension=0, tiled=True
    ).reshape(width, -1)
    numer_t, gram_rows = both[:, :row_count], both[:, row_count:]
    own = lax.dynamic_slice_in_dim(factors, gene_at * width, width, 1)
    smooth, degree = stencil_term(own, position, edge_codes)
    penalty = float(G * K) / 64.0
    own_t = own.T
    denom_t = (
        lax.dot_general(gram_rows, factors, right_dims, precision=lax.Precision.HIGHEST)
        + penalty * degree[None, :] * own_t
    )
    new_t = own_t * (numer_t + penalty * smooth.T) / denom_t
    factors_t = exchange(new_t, "gene", 0, False).reshape(width_all, row_count)
    factors_new = factors_t.T
    fac_bf_t = factors_t.astype(jnp.bfloat16)
    cross_part = jnp.dot(fac_bf_t, counts, preferred_element_type=jnp.float32)
    fgram_part = lax.dot_general(fac_bf_t, fac_bf_t, right_dims, preferred_element_type=jnp.float32)
    loadings_new = loadings_update(
        cross_part.reshape(bin_count, k_rows, -1),
        fgram_part.reshape(bin_count, k_rows, -1),
        loadings,
        2,
    ).reshape(width_all, -1)
    return (factors_new, loadings_new)


def solution(mesh):
    placed = (P("bin", "gene"), P("bin", None), P(None, "gene"), P("bin"), P("bin", None))
    return jax.shard_map(
        on_device,
        mesh=mesh,
        in_specs=placed,
        out_specs=(P("bin", None), P(None, "gene")),
        check_vma=False,
    )
```

```python
import functools

import jax
import jax.numpy as jnp
from jax import lax
from jax.experimental import pallas as pl
from jax.experimental.pallas import tpu as pltpu
from jax.sharding import PartitionSpec as P

K = 256
G = 18432


def passed_along(block, axis, distance):
    devices = range(lax.axis_size(axis))
    route = [(i - distance, i) for i in devices if i - distance in devices]
    return lax.ppermute(block, axis, route)


def neighbour_sum(values, from_above, from_below):
    upper = jnp.concatenate([from_above[None], values[:-1]], 0)
    lower = jnp.concatenate([values[1:], from_below[None]], 0)
    beside = jnp.pad(values[:, 1:], ((0, 0), (0, 1), (0, 0))) + jnp.pad(
        values[:, :-1], ((0, 0), (1, 0), (0, 0))
    )
    return beside + 0.5 * (lower + upper)


def neighbour_first(values, from_above, from_below):
    upper = jnp.concatenate([from_above[:, None], values[:, :-1]], 1)
    lower = jnp.concatenate([values[:, 1:], from_below[:, None]], 1)
    beside = jnp.pad(values[:, :, 1:], ((0, 0), (0, 0), (0, 1))) + jnp.pad(
        values[:, :, :-1], ((0, 0), (0, 0), (1, 0))
    )
    return beside + 0.5 * (lower + upper)


def gray(value):
    return value + (value // 2) * (1 - 2 * (value % 2))


def gene_at_place(place, count):
    wide = 1 - ((place + count - 1) % count) // (count // 2)
    row = wide * (place - 1) + (1 - wide) * ((count - place) % count)
    return 2 * row + wide


def gene_place(index, count):
    row, wide = index // 2, index % 2
    return wide * (1 + row) + (1 - wide) * ((count - row) % count)


def bin_at_place(place, count):
    plane, step = place // 4, place % 4
    turned = step + (plane % 2) * (3 - 2 * step)
    return plane * 4 + gray(turned)


def bin_place(index, count):
    plane = index // 4
    turned = gray(index % 4)
    return plane * 4 + turned + (plane % 2) * (3 - 2 * turned)


RINGS = {"gene": (gene_at_place, gene_place), "bin": (bin_at_place, bin_place)}


def ring_peers(axis, count):
    at_place, place_of = RINGS[axis]
    place = place_of(lax.axis_index(axis), count)
    return place, (lambda shift: at_place((place + shift + count) % count, count))


def enter(axis, peers):
    barrier = pltpu.get_barrier_semaphore()
    for peer in peers:
        pl.semaphore_signal(barrier, inc=1, device_id={axis: peer},
                            device_id_type=pl.DeviceIdType.MESH)
    pl.semaphore_wait(barrier, len(peers))


def gather_kernel(axis, count, x_ref, out_ref, send_sem, recv_sem):
    place, member = ring_peers(axis, count)
    ahead, behind = member(1), member(-1)
    half = x_ref.shape[0] // 2
    enter(axis, (ahead, behind))
    out_ref[member(0)] = x_ref[...]

    def copy(step, way):
        rows = pl.ds(way * half, half)
        origin = member(-step) if way == 0 else member(step)
        src = x_ref.at[rows] if step == 0 else out_ref.at[origin, rows]
        return pltpu.make_async_remote_copy(
            src_ref=src,
            dst_ref=out_ref.at[origin, rows],
            send_sem=send_sem.at[way, step],
            recv_sem=recv_sem.at[way, step],
            device_id={axis: ahead if way == 0 else behind},
            device_id_type=pl.DeviceIdType.MESH,
        )

    for step in range(count - 1):
        for way in (0, 1):
            if step >= 1:
                copy(step - 1, way).wait_recv()
            copy(step, way).start()
    for way in (0, 1):
        copy(count - 2, way).wait_recv()
    for step in range(count - 1):
        for way in (0, 1):
            copy(step, way).wait_send()


def ring_gather(x, axis, collective_id):
    count = lax.axis_size(axis)
    return pl.pallas_call(
        functools.partial(gather_kernel, axis, count),
        out_shape=jax.ShapeDtypeStruct((count,) + x.shape, x.dtype),
        in_specs=[pl.BlockSpec(memory_space=pltpu.VMEM)],
        out_specs=pl.BlockSpec(memory_space=pltpu.VMEM),
        scratch_shapes=[
            pltpu.SemaphoreType.DMA((2, count - 1)),
            pltpu.SemaphoreType.DMA((2, count - 1)),
        ],
        compiler_params=pltpu.CompilerParams(
            collective_id=collective_id, has_side_effects=True
        ),
    )(x)


def scatter_kernel(axis, count, x_ref, out_ref, got, sent, send_sem, recv_sem):
    place, member = ring_peers(axis, count)
    ahead, behind = member(1), member(-1)
    half = x_ref.shape[2] // 2
    enter(axis, (ahead, behind))

    def copy(step, way):
        lanes = pl.ds(way * half, half)
        if step == 0:
            source = x_ref.at[member(-1) if way == 0 else member(1), :, lanes]
        else:
            source = sent.at[way, step]
        return pltpu.make_async_remote_copy(
            src_ref=source,
            dst_ref=got.at[way, step],
            send_sem=send_sem.at[way, step],
            recv_sem=recv_sem.at[way, step],
            device_id={axis: ahead if way == 0 else behind},
            device_id_type=pl.DeviceIdType.MESH,
        )

    for step in range(count - 1):
        for way in (0, 1):
            if step >= 1:
                lanes = pl.ds(way * half, half)
                owner = member(-step - 1) if way == 0 else member(step + 1)
                copy(step - 1, way).wait_recv()
                sent[way, step] = got[way, step - 1] + x_ref[owner, :, lanes]
            copy(step, way).start()
    for way in (0, 1):
        lanes = pl.ds(way * half, half)
        copy(count - 2, way).wait_recv()
        out_ref[:, lanes] = got[way, count - 2] + x_ref[member(0), :, lanes]
    for step in range(count - 1):
        for way in (0, 1):
            copy(step, way).wait_send()


def ring_scatter(x, axis, collective_id):
    count, rows, lanes = x.shape
    return pl.pallas_call(
        functools.partial(scatter_kernel, axis, count),
        out_shape=jax.ShapeDtypeStruct((rows, lanes), x.dtype),
        in_specs=[pl.BlockSpec(memory_space=pltpu.VMEM)],
        out_specs=pl.BlockSpec(memory_space=pltpu.VMEM),
        scratch_shapes=[
            pltpu.VMEM((2, count - 1, rows, lanes // 2), x.dtype),
            pltpu.VMEM((2, count - 1, rows, lanes // 2), x.dtype),
            pltpu.SemaphoreType.DMA((2, count - 1)),
            pltpu.SemaphoreType.DMA((2, count - 1)),
        ],
        compiler_params=pltpu.CompilerParams(
            collective_id=collective_id, has_side_effects=True
        ),
    )(x)


def greet_all(axis, me, count):
    barrier = pltpu.get_barrier_semaphore()
    for shift in range(1, count):
        pl.semaphore_signal(barrier, inc=1, device_id={axis: (me + shift) % count},
                            device_id_type=pl.DeviceIdType.MESH)
    pl.semaphore_wait(barrier, count - 1)


def exchange_kernel(axis, count, summed, x_ref, out_ref, *rest):
    if summed:
        got, send_sem, recv_sem = rest
    else:
        got, (send_sem, recv_sem) = out_ref, rest
    me = lax.axis_index(axis)
    greet_all(axis, me, count)

    def copy(shift):
        target = (me + shift) % count
        return pltpu.make_async_remote_copy(
            src_ref=x_ref.at[target] if summed else x_ref,
            dst_ref=got.at[me],
            send_sem=send_sem.at[shift],
            recv_sem=recv_sem.at[me],
            device_id={axis: target},
            device_id_type=pl.DeviceIdType.MESH,
        )

    def arrival(shift):
        origin = (me + count - shift) % count
        return pltpu.make_async_remote_copy(
            src_ref=x_ref.at[origin] if summed else x_ref,
            dst_ref=got.at[origin],
            send_sem=send_sem.at[shift],
            recv_sem=recv_sem.at[origin],
            device_id={axis: origin},
            device_id_type=pl.DeviceIdType.MESH,
        )

    for shift in range(1, count):
        copy(shift).start()
    if summed:
        total = x_ref[me]
        for shift in range(1, count):
            arrival(shift).wait_recv()
            total = total + got[(me + count - shift) % count]
        out_ref[...] = total
    else:
        out_ref[me] = x_ref[...]
        for shift in range(1, count):
            arrival(shift).wait_recv()
    for shift in range(1, count):
        copy(shift).wait_send()


def exchange(x, axis, collective_id, summed):
    count = lax.axis_size(axis)
    if summed:
        out_shape = x.shape[1:]
        scratch = [pltpu.VMEM(x.shape, x.dtype)]
    else:
        out_shape = (count,) + x.shape
        scratch = []
    return pl.pallas_call(
        functools.partial(exchange_kernel, axis, count, summed),
        out_shape=jax.ShapeDtypeStruct(out_shape, x.dtype),
        in_specs=[pl.BlockSpec(memory_space=pltpu.VMEM)],
        out_specs=pl.BlockSpec(memory_space=pltpu.VMEM),
        scratch_shapes=scratch + [
            pltpu.SemaphoreType.DMA((count,)),
            pltpu.SemaphoreType.DMA((count,)),
        ],
        compiler_params=pltpu.CompilerParams(
            collective_id=collective_id, has_side_effects=True
        ),
    )(x)


def loadings_kernel(count, cross_ref, gram_ref, load_ref, out_ref, got, got_gram, sem_a, sem_b, sem_c, sem_d):
    me = lax.axis_index("bin")
    greet_all("bin", me, count)

    def remote(src, dst, send, recv, shift, index, peer):
        return pltpu.make_async_remote_copy(
            src_ref=src.at[index],
            dst_ref=dst.at[index],
            send_sem=send.at[shift],
            recv_sem=recv.at[index],
            device_id={"bin": peer},
            device_id_type=pl.DeviceIdType.MESH,
        )

    def partial_copies(shift):
        target = (me + shift) % count
        return (
            pltpu.make_async_remote_copy(
                src_ref=cross_ref.at[target], dst_ref=got.at[me], send_sem=sem_a.at[0, shift],
                recv_sem=sem_b.at[0, me], device_id={"bin": target},
                device_id_type=pl.DeviceIdType.MESH,
            ),
            pltpu.make_async_remote_copy(
                src_ref=gram_ref.at[target], dst_ref=got_gram.at[me], send_sem=sem_a.at[1, shift],
                recv_sem=sem_b.at[1, me], device_id={"bin": target},
                device_id_type=pl.DeviceIdType.MESH,
            ),
        )

    def partial_arrivals(shift):
        origin = (me + count - shift) % count
        return (
            pltpu.make_async_remote_copy(
                src_ref=cross_ref.at[origin], dst_ref=got.at[origin], send_sem=sem_a.at[0, shift],
                recv_sem=sem_b.at[0, origin], device_id={"bin": origin},
                device_id_type=pl.DeviceIdType.MESH,
            ),
            pltpu.make_async_remote_copy(
                src_ref=gram_ref.at[origin], dst_ref=got_gram.at[origin], send_sem=sem_a.at[1, shift],
                recv_sem=sem_b.at[1, origin], device_id={"bin": origin},
                device_id_type=pl.DeviceIdType.MESH,
            ),
        )

    def result_copy(shift):
        target = (me + shift) % count
        return remote(out_ref, out_ref, sem_c, sem_d, shift, me, target)

    def result_arrival(shift):
        origin = (me + count - shift) % count
        return remote(out_ref, out_ref, sem_c, sem_d, shift, origin, origin)

    for shift in range(1, count):
        for copy in partial_copies(shift):
            copy.start()
    cross = cross_ref[me]
    fac_gram = gram_ref[me]
    for shift in range(1, count):
        origin = (me + count - shift) % count
        for copy in partial_arrivals(shift):
            copy.wait_recv()
        cross = cross + got[origin]
        fac_gram = fac_gram + got_gram[origin]
    rows = cross.shape[0]
    own = load_ref[pl.ds(pl.multiple_of(me * rows, rows), rows), :]
    denom = jnp.dot(
        fac_gram, load_ref[...], precision=lax.Precision.HIGHEST,
        preferred_element_type=jnp.float32,
    )
    out_ref[me] = own * cross / denom
    for shift in range(1, count):
        for copy in partial_copies(shift):
            copy.wait_send()
    for shift in range(1, count):
        result_copy(shift).start()
    for shift in range(1, count):
        result_arrival(shift).wait_recv()
    for shift in range(1, count):
        result_copy(shift).wait_send()


def loadings_update(cross_parts, gram_parts, loadings, collective_id):
    count, rows, genes = cross_parts.shape
    vmem = pl.BlockSpec(memory_space=pltpu.VMEM)
    return pl.pallas_call(
        functools.partial(loadings_kernel, count),
        out_shape=jax.ShapeDtypeStruct((count, rows, genes), loadings.dtype),
        in_specs=[vmem, vmem, vmem],
        out_specs=vmem,
        scratch_shapes=[
            pltpu.VMEM(cross_parts.shape, cross_parts.dtype),
            pltpu.VMEM(gram_parts.shape, gram_parts.dtype),
            pltpu.SemaphoreType.DMA((2, count)),
            pltpu.SemaphoreType.DMA((2, count)),
            pltpu.SemaphoreType.DMA((count,)),
            pltpu.SemaphoreType.DMA((count,)),
        ],
        compiler_params=pltpu.CompilerParams(
            collective_id=collective_id, has_side_effects=True
        ),
    )(cross_parts, gram_parts, loadings)


def split_three(values):
    high = lax.reduce_precision(values, exponent_bits=8, mantissa_bits=7)
    rest = values - high
    mid = lax.reduce_precision(rest, exponent_bits=8, mantissa_bits=7)
    low = rest - mid
    return jnp.concatenate([high, mid, low], 1).astype(jnp.bfloat16)


def join_three(parts, width):
    return (parts[:, :width] + parts[:, width : 2 * width]) + parts[:, 2 * width :]


def stencil_term(own, position, edge_codes):
    bin_count = lax.axis_size("bin")
    row_count, width = own.shape
    group_size = row_count // bin_count
    grid_rows, grid_cols = edge_codes.shape
    payload = jnp.concatenate([own, position.astype(jnp.float32)[:, None]], 1)
    got = lax.all_to_all(
        payload.reshape(bin_count, group_size, width + 1), "bin", 0, 0, tiled=True
    ).reshape(row_count, width + 1)
    tile_slot = got[:, width].astype(jnp.int32) - lax.axis_index("bin") * row_count
    cells = lax.broadcasted_iota(jnp.int32, (row_count, row_count), 1)
    onehot = (tile_slot[:, None] == cells).astype(jnp.bfloat16)
    placed = lax.dot_general(
        onehot, split_three(got[:, :width]), (((0,), (0,)), ((), ())),
        preferred_element_type=jnp.float32,
    )
    tile_rows = join_three(placed, width)
    cell_scale = edge_codes.astype(jnp.float32) / 8.0
    weighted = cell_scale[:, :, None] * tile_rows.reshape(grid_rows, grid_cols, width)
    rim_last, rim_first = (weighted[-1], weighted[0])
    upper_rows, upper_scale = passed_along((rim_last, cell_scale[-1]), "bin", 1)
    lower_rows, lower_scale = passed_along((rim_first, cell_scale[0]), "bin", -1)
    degree_grid = (
        cell_scale * neighbour_first(cell_scale[None], upper_scale[None], lower_scale[None])[0]
    )
    smooth_grid = cell_scale[:, :, None] * neighbour_sum(weighted, upper_rows, lower_rows)
    back = jnp.concatenate(
        [smooth_grid.reshape(row_count, width), degree_grid.reshape(row_count, 1)], 1
    )
    back_rows = join_three(
        jnp.dot(onehot, split_three(back), preferred_element_type=jnp.float32), width + 1
    )
    ret = lax.all_to_all(
        back_rows.reshape(bin_count, group_size, width + 1), "bin", 0, 0, tiled=True
    ).reshape(row_count, width + 1)
    return (ret[:, :width], ret[:, width])


def on_device(counts, factors, loadings, position, edge_codes):
    bin_count = lax.axis_size("bin")
    gene_count = lax.axis_size("gene")
    row_count, width_all = factors.shape
    width = width_all // gene_count
    k_rows = width_all // bin_count
    gene_at = lax.axis_index("gene")
    bin_at = lax.axis_index("bin")
    load_bf = loadings.astype(jnp.bfloat16)
    right_dims = (((1,), (1,)), ((), ()))
    numer_part = lax.dot_general(load_bf, counts, right_dims, preferred_element_type=jnp.float32)
    gram_part = lax.dot_general(load_bf, load_bf, right_dims, preferred_element_type=jnp.float32)
    both = jnp.concatenate([numer_part, gram_part], 1)
    own = lax.dynamic_slice_in_dim(factors, gene_at * width, width, 1)
    both, own = lax.optimization_barrier((both, own))
    both = lax.psum_scatter(
        both.reshape(gene_count, width, -1), "gene", scatter_dimension=0, tiled=True
    ).reshape(width, -1)
    numer_t, gram_rows = both[:, :row_count], both[:, row_count:]
    smooth, degree = stencil_term(own, position, edge_codes)
    penalty = float(G * K) / 64.0
    own_t = own.T
    denom_t = (
        lax.dot_general(gram_rows, factors, right_dims, precision=lax.Precision.HIGHEST)
        + penalty * degree[None, :] * own_t
    )
    new_t = own_t * (numer_t + penalty * smooth.T) / denom_t
    factors_t = exchange(new_t, "gene", 0, False).reshape(width_all, row_count)
    factors_new = factors_t.T
    fac_bf_t = factors_t.astype(jnp.bfloat16)
    cross_part = jnp.dot(fac_bf_t, counts, preferred_element_type=jnp.float32)
    fgram_part = lax.dot_general(fac_bf_t, fac_bf_t, right_dims, preferred_element_type=jnp.float32)
    loadings_new = loadings_update(
        cross_part.reshape(bin_count, k_rows, -1),
        fgram_part.reshape(bin_count, k_rows, -1),
        loadings,
        2,
    ).reshape(width_all, -1)
    return (factors_new, loadings_new)


def solution(mesh):
    placed = (P("bin", "gene"), P("bin", None), P(None, "gene"), P("bin"), P("bin", None))
    return jax.shard_map(
        on_device,
        mesh=mesh,
        in_specs=placed,
        out_specs=(P("bin", None), P(None, "gene")),
        check_vma=False,
    )
```

```python
import functools

import jax
import jax.numpy as jnp
from jax import lax
from jax.experimental import pallas as pl
from jax.experimental.pallas import tpu as pltpu
from jax.sharding import PartitionSpec as P

K = 256
G = 18432


def passed_along(block, axis, distance):
    devices = range(lax.axis_size(axis))
    route = [(i - distance, i) for i in devices if i - distance in devices]
    return lax.ppermute(block, axis, route)


def neighbour_sum(values, from_above, from_below):
    upper = jnp.concatenate([from_above[None], values[:-1]], 0)
    lower = jnp.concatenate([values[1:], from_below[None]], 0)
    beside = jnp.pad(values[:, 1:], ((0, 0), (0, 1), (0, 0))) + jnp.pad(
        values[:, :-1], ((0, 0), (1, 0), (0, 0))
    )
    return beside + 0.5 * (lower + upper)


def neighbour_first(values, from_above, from_below):
    upper = jnp.concatenate([from_above[:, None], values[:, :-1]], 1)
    lower = jnp.concatenate([values[:, 1:], from_below[:, None]], 1)
    beside = jnp.pad(values[:, :, 1:], ((0, 0), (0, 0), (0, 1))) + jnp.pad(
        values[:, :, :-1], ((0, 0), (0, 0), (1, 0))
    )
    return beside + 0.5 * (lower + upper)


def gray(value):
    return value + (value // 2) * (1 - 2 * (value % 2))


def gene_at_place(place, count):
    wide = 1 - ((place + count - 1) % count) // (count // 2)
    row = wide * (place - 1) + (1 - wide) * ((count - place) % count)
    return 2 * row + wide


def gene_place(index, count):
    row, wide = index // 2, index % 2
    return wide * (1 + row) + (1 - wide) * ((count - row) % count)


def bin_at_place(place, count):
    plane, step = place // 4, place % 4
    turned = step + (plane % 2) * (3 - 2 * step)
    return plane * 4 + gray(turned)


def bin_place(index, count):
    plane = index // 4
    turned = gray(index % 4)
    return plane * 4 + turned + (plane % 2) * (3 - 2 * turned)


RINGS = {"gene": (gene_at_place, gene_place), "bin": (bin_at_place, bin_place)}


def ring_peers(axis, count):
    at_place, place_of = RINGS[axis]
    place = place_of(lax.axis_index(axis), count)
    return place, (lambda shift: at_place((place + shift + count) % count, count))


def enter(axis, peers):
    barrier = pltpu.get_barrier_semaphore()
    for peer in peers:
        pl.semaphore_signal(barrier, inc=1, device_id={axis: peer},
                            device_id_type=pl.DeviceIdType.MESH)
    pl.semaphore_wait(barrier, len(peers))


def gather_kernel(axis, count, x_ref, out_ref, send_sem, recv_sem):
    place, member = ring_peers(axis, count)
    ahead, behind = member(1), member(-1)
    half = x_ref.shape[0] // 2
    enter(axis, (ahead, behind))
    out_ref[member(0)] = x_ref[...]

    def copy(step, way):
        rows = pl.ds(way * half, half)
        origin = member(-step) if way == 0 else member(step)
        src = x_ref.at[rows] if step == 0 else out_ref.at[origin, rows]
        return pltpu.make_async_remote_copy(
            src_ref=src,
            dst_ref=out_ref.at[origin, rows],
            send_sem=send_sem.at[way, step],
            recv_sem=recv_sem.at[way, step],
            device_id={axis: ahead if way == 0 else behind},
            device_id_type=pl.DeviceIdType.MESH,
        )

    for step in range(count - 1):
        for way in (0, 1):
            if step >= 1:
                copy(step - 1, way).wait_recv()
            copy(step, way).start()
    for way in (0, 1):
        copy(count - 2, way).wait_recv()
    for step in range(count - 1):
        for way in (0, 1):
            copy(step, way).wait_send()


def ring_gather(x, axis, collective_id):
    count = lax.axis_size(axis)
    return pl.pallas_call(
        functools.partial(gather_kernel, axis, count),
        out_shape=jax.ShapeDtypeStruct((count,) + x.shape, x.dtype),
        in_specs=[pl.BlockSpec(memory_space=pltpu.VMEM)],
        out_specs=pl.BlockSpec(memory_space=pltpu.VMEM),
        scratch_shapes=[
            pltpu.SemaphoreType.DMA((2, count - 1)),
            pltpu.SemaphoreType.DMA((2, count - 1)),
        ],
        compiler_params=pltpu.CompilerParams(
            collective_id=collective_id, has_side_effects=True
        ),
    )(x)


def scatter_kernel(axis, count, x_ref, out_ref, got, sent, send_sem, recv_sem):
    place, member = ring_peers(axis, count)
    ahead, behind = member(1), member(-1)
    half = x_ref.shape[2] // 2
    enter(axis, (ahead, behind))

    def copy(step, way):
        lanes = pl.ds(way * half, half)
        if step == 0:
            source = x_ref.at[member(-1) if way == 0 else member(1), :, lanes]
        else:
            source = sent.at[way, step]
        return pltpu.make_async_remote_copy(
            src_ref=source,
            dst_ref=got.at[way, step],
            send_sem=send_sem.at[way, step],
            recv_sem=recv_sem.at[way, step],
            device_id={axis: ahead if way == 0 else behind},
            device_id_type=pl.DeviceIdType.MESH,
        )

    for step in range(count - 1):
        for way in (0, 1):
            if step >= 1:
                lanes = pl.ds(way * half, half)
                owner = member(-step - 1) if way == 0 else member(step + 1)
                copy(step - 1, way).wait_recv()
                sent[way, step] = got[way, step - 1] + x_ref[owner, :, lanes]
            copy(step, way).start()
    for way in (0, 1):
        lanes = pl.ds(way * half, half)
        copy(count - 2, way).wait_recv()
        out_ref[:, lanes] = got[way, count - 2] + x_ref[member(0), :, lanes]
    for step in range(count - 1):
        for way in (0, 1):
            copy(step, way).wait_send()


def ring_scatter(x, axis, collective_id):
    count, rows, lanes = x.shape
    return pl.pallas_call(
        functools.partial(scatter_kernel, axis, count),
        out_shape=jax.ShapeDtypeStruct((rows, lanes), x.dtype),
        in_specs=[pl.BlockSpec(memory_space=pltpu.VMEM)],
        out_specs=pl.BlockSpec(memory_space=pltpu.VMEM),
        scratch_shapes=[
            pltpu.VMEM((2, count - 1, rows, lanes // 2), x.dtype),
            pltpu.VMEM((2, count - 1, rows, lanes // 2), x.dtype),
            pltpu.SemaphoreType.DMA((2, count - 1)),
            pltpu.SemaphoreType.DMA((2, count - 1)),
        ],
        compiler_params=pltpu.CompilerParams(
            collective_id=collective_id, has_side_effects=True
        ),
    )(x)


def greet_all(axis, me, count):
    barrier = pltpu.get_barrier_semaphore()
    for shift in range(1, count):
        pl.semaphore_signal(barrier, inc=1, device_id={axis: (me + shift) % count},
                            device_id_type=pl.DeviceIdType.MESH)
    pl.semaphore_wait(barrier, count - 1)


def exchange_kernel(axis, count, summed, x_ref, out_ref, *rest):
    if summed:
        got, send_sem, recv_sem = rest
    else:
        got, (send_sem, recv_sem) = out_ref, rest
    me = lax.axis_index(axis)
    greet_all(axis, me, count)

    def copy(shift):
        target = (me + shift) % count
        return pltpu.make_async_remote_copy(
            src_ref=x_ref.at[target] if summed else x_ref,
            dst_ref=got.at[me],
            send_sem=send_sem.at[shift],
            recv_sem=recv_sem.at[me],
            device_id={axis: target},
            device_id_type=pl.DeviceIdType.MESH,
        )

    def arrival(shift):
        origin = (me + count - shift) % count
        return pltpu.make_async_remote_copy(
            src_ref=x_ref.at[origin] if summed else x_ref,
            dst_ref=got.at[origin],
            send_sem=send_sem.at[shift],
            recv_sem=recv_sem.at[origin],
            device_id={axis: origin},
            device_id_type=pl.DeviceIdType.MESH,
        )

    for shift in range(1, count):
        copy(shift).start()
    if summed:
        total = x_ref[me]
        for shift in range(1, count):
            arrival(shift).wait_recv()
            total = total + got[(me + count - shift) % count]
        out_ref[...] = total
    else:
        out_ref[me] = x_ref[...]
        for shift in range(1, count):
            arrival(shift).wait_recv()
    for shift in range(1, count):
        copy(shift).wait_send()


def exchange(x, axis, collective_id, summed):
    count = lax.axis_size(axis)
    if summed:
        out_shape = x.shape[1:]
        scratch = [pltpu.VMEM(x.shape, x.dtype)]
    else:
        out_shape = (count,) + x.shape
        scratch = []
    return pl.pallas_call(
        functools.partial(exchange_kernel, axis, count, summed),
        out_shape=jax.ShapeDtypeStruct(out_shape, x.dtype),
        in_specs=[pl.BlockSpec(memory_space=pltpu.VMEM)],
        out_specs=pl.BlockSpec(memory_space=pltpu.VMEM),
        scratch_shapes=scratch + [
            pltpu.SemaphoreType.DMA((count,)),
            pltpu.SemaphoreType.DMA((count,)),
        ],
        compiler_params=pltpu.CompilerParams(
            collective_id=collective_id, has_side_effects=True
        ),
    )(x)


def factor_gather_kernel(count, x_ref, out_ref, half_ref, send_sem, recv_sem):
    me = lax.axis_index("gene")
    greet_all("gene", me, count)

    def copy(shift, index, peer):
        return pltpu.make_async_remote_copy(
            src_ref=x_ref,
            dst_ref=out_ref.at[index],
            send_sem=send_sem.at[shift],
            recv_sem=recv_sem.at[index],
            device_id={"gene": peer},
            device_id_type=pl.DeviceIdType.MESH,
        )

    for shift in range(1, count):
        copy(shift, me, (me + shift) % count).start()
    out_ref[me] = x_ref[...]
    for shift in range(1, count):
        origin = (me + count - shift) % count
        copy(shift, origin, origin).wait_recv()
    half_ref[...] = out_ref[...].astype(half_ref.dtype)
    for shift in range(1, count):
        copy(shift, me, (me + shift) % count).wait_send()


def factor_gather(x, collective_id):
    count = lax.axis_size("gene")
    vmem = pl.BlockSpec(memory_space=pltpu.VMEM)
    shape = (count,) + x.shape
    return pl.pallas_call(
        functools.partial(factor_gather_kernel, count),
        out_shape=(
            jax.ShapeDtypeStruct(shape, x.dtype),
            jax.ShapeDtypeStruct(shape, jnp.bfloat16),
        ),
        in_specs=[vmem],
        out_specs=(vmem, vmem),
        scratch_shapes=[pltpu.SemaphoreType.DMA((count,))] * 2,
        compiler_params=pltpu.CompilerParams(
            collective_id=collective_id, has_side_effects=True
        ),
    )(x)


def loadings_kernel(count, cross_ref, gram_ref, load_ref, out_ref, got, got_gram, sem_a, sem_b, sem_c, sem_d):
    me = lax.axis_index("bin")
    greet_all("bin", me, count)

    def remote(src, dst, send, recv, shift, index, peer):
        return pltpu.make_async_remote_copy(
            src_ref=src.at[index],
            dst_ref=dst.at[index],
            send_sem=send.at[shift],
            recv_sem=recv.at[index],
            device_id={"bin": peer},
            device_id_type=pl.DeviceIdType.MESH,
        )

    def partial_copies(shift):
        target = (me + shift) % count
        return (
            pltpu.make_async_remote_copy(
                src_ref=cross_ref.at[target], dst_ref=got.at[me], send_sem=sem_a.at[0, shift],
                recv_sem=sem_b.at[0, me], device_id={"bin": target},
                device_id_type=pl.DeviceIdType.MESH,
            ),
            pltpu.make_async_remote_copy(
                src_ref=gram_ref.at[target], dst_ref=got_gram.at[me], send_sem=sem_a.at[1, shift],
                recv_sem=sem_b.at[1, me], device_id={"bin": target},
                device_id_type=pl.DeviceIdType.MESH,
            ),
        )

    def partial_arrivals(shift):
        origin = (me + count - shift) % count
        return (
            pltpu.make_async_remote_copy(
                src_ref=cross_ref.at[origin], dst_ref=got.at[origin], send_sem=sem_a.at[0, shift],
                recv_sem=sem_b.at[0, origin], device_id={"bin": origin},
                device_id_type=pl.DeviceIdType.MESH,
            ),
            pltpu.make_async_remote_copy(
                src_ref=gram_ref.at[origin], dst_ref=got_gram.at[origin], send_sem=sem_a.at[1, shift],
                recv_sem=sem_b.at[1, origin], device_id={"bin": origin},
                device_id_type=pl.DeviceIdType.MESH,
            ),
        )

    def result_copy(shift):
        target = (me + shift) % count
        return remote(out_ref, out_ref, sem_c, sem_d, shift, me, target)

    def result_arrival(shift):
        origin = (me + count - shift) % count
        return remote(out_ref, out_ref, sem_c, sem_d, shift, origin, origin)

    for shift in range(1, count):
        for copy in partial_copies(shift):
            copy.start()
    cross = cross_ref[me]
    fac_gram = gram_ref[me]
    for shift in range(1, count):
        origin = (me + count - shift) % count
        for copy in partial_arrivals(shift):
            copy.wait_recv()
        cross = cross + got[origin]
        fac_gram = fac_gram + got_gram[origin]
    rows = cross.shape[0]
    own = load_ref[pl.ds(pl.multiple_of(me * rows, rows), rows), :]
    denom = jnp.dot(
        fac_gram, load_ref[...], precision=lax.Precision.HIGHEST,
        preferred_element_type=jnp.float32,
    )
    out_ref[me] = own * cross / denom
    for shift in range(1, count):
        result_copy(shift).start()
    for shift in range(1, count):
        for copy in partial_copies(shift):
            copy.wait_send()
    for shift in range(1, count):
        result_arrival(shift).wait_recv()
    for shift in range(1, count):
        result_copy(shift).wait_send()


def loadings_update(cross_parts, gram_parts, loadings, collective_id):
    count, rows, genes = cross_parts.shape
    vmem = pl.BlockSpec(memory_space=pltpu.VMEM)
    return pl.pallas_call(
        functools.partial(loadings_kernel, count),
        out_shape=jax.ShapeDtypeStruct((count, rows, genes), loadings.dtype),
        in_specs=[vmem, vmem, vmem],
        out_specs=vmem,
        scratch_shapes=[
            pltpu.VMEM(cross_parts.shape, cross_parts.dtype),
            pltpu.VMEM(gram_parts.shape, gram_parts.dtype),
            pltpu.SemaphoreType.DMA((2, count)),
            pltpu.SemaphoreType.DMA((2, count)),
            pltpu.SemaphoreType.DMA((count,)),
            pltpu.SemaphoreType.DMA((count,)),
        ],
        compiler_params=pltpu.CompilerParams(
            collective_id=collective_id, has_side_effects=True
        ),
    )(cross_parts, gram_parts, loadings)


def split_three(values):
    high = lax.reduce_precision(values, exponent_bits=8, mantissa_bits=7)
    rest = values - high
    mid = lax.reduce_precision(rest, exponent_bits=8, mantissa_bits=7)
    low = rest - mid
    return jnp.concatenate([high, mid, low], 1).astype(jnp.bfloat16)


def join_three(parts, width):
    return (parts[:, :width] + parts[:, width : 2 * width]) + parts[:, 2 * width :]


def stencil_term(own, position, edge_codes):
    bin_count = lax.axis_size("bin")
    row_count, width = own.shape
    group_size = row_count // bin_count
    grid_rows, grid_cols = edge_codes.shape
    payload = jnp.concatenate([own, position.astype(jnp.float32)[:, None]], 1)
    got = lax.all_to_all(
        payload.reshape(bin_count, group_size, width + 1), "bin", 0, 0, tiled=True
    ).reshape(row_count, width + 1)
    tile_slot = got[:, width].astype(jnp.int32) - lax.axis_index("bin") * row_count
    cells = lax.broadcasted_iota(jnp.int32, (row_count, row_count), 1)
    onehot = (tile_slot[:, None] == cells).astype(jnp.bfloat16)
    placed = lax.dot_general(
        onehot, split_three(got[:, :width]), (((0,), (0,)), ((), ())),
        preferred_element_type=jnp.float32,
    )
    tile_rows = join_three(placed, width)
    cell_scale = edge_codes.astype(jnp.float32) / 8.0
    weighted = cell_scale[:, :, None] * tile_rows.reshape(grid_rows, grid_cols, width)
    rim_last, rim_first = (weighted[-1], weighted[0])
    upper_rows, upper_scale = passed_along((rim_last, cell_scale[-1]), "bin", 1)
    lower_rows, lower_scale = passed_along((rim_first, cell_scale[0]), "bin", -1)
    degree_grid = (
        cell_scale * neighbour_first(cell_scale[None], upper_scale[None], lower_scale[None])[0]
    )
    smooth_grid = cell_scale[:, :, None] * neighbour_sum(weighted, upper_rows, lower_rows)
    back = jnp.concatenate(
        [smooth_grid.reshape(row_count, width), degree_grid.reshape(row_count, 1)], 1
    )
    back_rows = join_three(
        jnp.dot(onehot, split_three(back), preferred_element_type=jnp.float32), width + 1
    )
    ret = lax.all_to_all(
        back_rows.reshape(bin_count, group_size, width + 1), "bin", 0, 0, tiled=True
    ).reshape(row_count, width + 1)
    return (ret[:, :width], ret[:, width])


def on_device(counts, factors, loadings, position, edge_codes):
    bin_count = lax.axis_size("bin")
    gene_count = lax.axis_size("gene")
    row_count, width_all = factors.shape
    width = width_all // gene_count
    k_rows = width_all // bin_count
    gene_at = lax.axis_index("gene")
    bin_at = lax.axis_index("bin")
    load_bf = loadings.astype(jnp.bfloat16)
    right_dims = (((1,), (1,)), ((), ()))
    numer_part = lax.dot_general(load_bf, counts, right_dims, preferred_element_type=jnp.float32)
    gram_part = lax.dot_general(load_bf, load_bf, right_dims, preferred_element_type=jnp.float32)
    both = jnp.concatenate([numer_part, gram_part], 1)
    both = lax.psum_scatter(
        both.reshape(gene_count, width, -1), "gene", scatter_dimension=0, tiled=True
    ).reshape(width, -1)
    numer_t, gram_rows = both[:, :row_count], both[:, row_count:]
    own = lax.dynamic_slice_in_dim(factors, gene_at * width, width, 1)
    smooth, degree = stencil_term(own, position, edge_codes)
    penalty = float(G * K) / 64.0
    own_t = own.T
    denom_t = (
        lax.dot_general(gram_rows, factors, right_dims, precision=lax.Precision.HIGHEST)
        + penalty * degree[None, :] * own_t
    )
    new_t = own_t * (numer_t + penalty * smooth.T) / denom_t
    factors_t, fac_bf_t = factor_gather(new_t, 0)
    factors_new = factors_t.reshape(width_all, row_count).T
    fac_bf_t = fac_bf_t.reshape(width_all, row_count)
    cross_part = jnp.dot(fac_bf_t, counts, preferred_element_type=jnp.float32)
    fgram_part = lax.dot_general(fac_bf_t, fac_bf_t, right_dims, preferred_element_type=jnp.float32)
    loadings_new = loadings_update(
        cross_part.reshape(bin_count, k_rows, -1),
        fgram_part.reshape(bin_count, k_rows, -1),
        loadings,
        2,
    ).reshape(width_all, -1)
    return (factors_new, loadings_new)


def solution(mesh):
    placed = (P("bin", "gene"), P("bin", None), P(None, "gene"), P("bin"), P("bin", None))
    return jax.shard_map(
        on_device,
        mesh=mesh,
        in_specs=placed,
        out_specs=(P("bin", None), P(None, "gene")),
        check_vma=False,
    )
```
